32 devices in a mesh: dp: 8 (over z, x), tensor: 4 (over y, core).
Axes of the slice: x: 2, y: 2, z: 4, core: 2. Of those that a mesh axis runs over, the one named last changes fastest.
Arguments:
- block_input: bfloat16 [20480, 1536], P(('dp', 'tensor')), may hold values from -6 to 6
- seq_lengths: int32 [8, 5], P('dp'), may hold values from 1 to 1024, 2560 in all within a row
- w_qkv: float32 [768, 3, 768], P('dp', None, 'tensor'), may hold values from -0.21875 to 0.21875
- w_out: float32 [768, 768], P('dp', 'tensor'), may hold values from -0.875 to 0.875
- w_gate_up: float32 [768, 2, 3072], P('dp', None, 'tensor'), may hold values from -0.21875 to 0.21875
- w_down: float32 [768, 3072], P('dp', 'tensor'), may hold values from -0.109375 to 0.109375
- gain_attn: float32 [768], replicated, may hold values from 0.5 to 1.5
- gain_ffn: float32 [768], replicated, may hold values from 0.5 to 1.5
- mix_matrix: float32 [2, 2], replicated, may hold values from 0.3 to 1
- correct_gain: float32 [2], replicated, may hold values from 0.5 to 1.5
- cotangent: bfloat16 [20480, 1536], P(('dp', 'tensor')), may hold values from -6 to 6
Outputs:
- block_output: bfloat16 [20480, 1536], P(('dp', 'tensor'))
- grad_input: float32 [20480, 1536], P(('dp', 'tensor'))
- grad_w_qkv: float32 [768, 3, 768], P('dp', None, 'tensor')
- grad_w_out: float32 [768, 768], P('dp', 'tensor')
- grad_w_gate_up: float32 [768, 2, 3072], P('dp', None, 'tensor')
- grad_w_down: float32 [768, 3072], P('dp', 'tensor')
- grad_gain_attn: float32 [768], replicated
- grad_gain_ffn: float32 [768], replicated
- grad_mix_matrix: float32 [2, 2], replicated
- grad_correct_gain: float32 [2], replicated
The draws below stay inside these ranges and needn't reach their ends.
Inputs may be any that keep to these rules, and one draw needn't show every extreme that they name: Each row of seq_lengths sums to 2560, and its largest entry is 1024.
All inputs are finite; a program needn't handle non-finite values.
Results may differ from the reference program's by a relative error of at most 0.014.
Values may be sent and summed in bfloat16 or wider, within the bound.
A program may use at most 192 MiB of HBM per device.

```python
import math
import jax
import jax.numpy as jnp
import numpy as np
from jax import lax

D = 768
FF = 3072
HEADS = 12
HEAD_DIM = 64
GROUP_ROWS = 2560
TOKENS = 20480
NSEQ = 5
SEQ_MAX = 1024
N_DP = 8


def levels(stream_key, dims, split, smallest, high):
    level, own = 1.0, jax.random.fold_in(stream_key, 6)
    for dim, parts in split:
        heights = jnp.exp(jax.random.uniform(jax.random.fold_in(own, dim), (parts,), jnp.float32, smallest / len(split), high / len(split)))
        level = level * jnp.repeat(heights, dims[dim] // parts).reshape([-1 if axis == dim else 1 for axis in range(len(dims))])
    return level


def split_up(amount, total, most, lean):
    loads = [(1 << 20) // math.isqrt(standing ** lean) + 1 for standing in range(2, amount + 1)]
    rest, holding = total - most - (amount - 1), [1] * (amount - 1)
    while rest > 0:
        movable = [i for i in range(amount - 1) if holding[i] < most]
        whole, remaining = sum([loads[i] for i in movable]), rest
        for i in movable:
            more = min(most - holding[i], max(1, remaining * loads[i] // whole), rest)
            holding[i] = holding[i] + more
            rest = rest - more
    return np.array([most] + holding)


def ragged(rng, number_of, total, bound, slope):
    if number_of == 2:
        one = jax.random.randint(rng, (), max(1, total - bound), min(bound, total - 1) + 1)
        return jnp.stack([one, total - one])
    lengths = jnp.asarray(split_up(number_of, total, bound, slope), jnp.int32)
    pairs = (number_of - 1) // 2
    donor, receiver = lengths[1:1 + 2 * pairs:2], lengths[2:2 + 2 * pairs:2]
    margin = jnp.minimum(donor - 1, bound - receiver)
    passed = jax.random.randint(jax.random.fold_in(rng, 1), (pairs,), 0, 1 << 20) % (margin + 1)
    lengths = lengths.at[1:1 + 2 * pairs:2].set(donor - passed).at[2:2 + 2 * pairs:2].set(receiver + passed)
    return lengths[jax.random.permutation(jax.random.fold_in(rng, 2), number_of)]


def noise(key, shape, scale, limit, pieces=(), kind=jnp.bfloat16):
    entries = scale * jax.random.normal(key, shape, jnp.float32)
    if pieces:
        entries = entries * levels(key, shape, pieces, -0.22, 0.18)
    return jnp.clip(entries, -limit, limit).astype(kind)


def setup_inputs(seed: int = 0) -> dict:
    seeds = jax.random.split(jax.random.key(seed), 12)
    return {
        "block_input": noise(seeds[0], (TOKENS, 2 * D), 1.0, 6.0, ((0, 32),)),
        "seq_lengths": jax.vmap(lambda own: ragged(own, NSEQ, GROUP_ROWS, SEQ_MAX, 2))(jax.random.split(seeds[1], N_DP)).reshape((N_DP, NSEQ)).astype(jnp.int32),
        "w_qkv": noise(seeds[2], (D, 3, D), D ** -0.5, 0.21875, ((0, 8), (2, 4)), jnp.float32),
        "w_out": noise(seeds[3], (D, D), (D // 16) ** -0.5, 0.875, ((0, 8), (1, 4)), jnp.float32),
        "w_gate_up": noise(seeds[4], (D, 2, FF), D ** -0.5, 0.21875, ((0, 8), (2, 4)), jnp.float32),
        "w_down": noise(seeds[5], (D, FF), FF ** -0.5, 0.109375, ((0, 8), (1, 4)), jnp.float32),
        "gain_attn": jnp.clip(1.0 + 0.1 * jax.random.normal(seeds[6], (D,), jnp.float32), 0.5, 1.5),
        "gain_ffn": jnp.clip(1.0 + 0.1 * jax.random.normal(seeds[7], (D,), jnp.float32), 0.5, 1.5),
        "mix_matrix": jnp.clip(jax.random.uniform(seeds[8], (2, 2), jnp.float32, 0.3, 1.0), 0.3, 1.0),
        "correct_gain": jnp.clip(jax.random.uniform(seeds[9], (2,), jnp.float32, 0.5, 1.5), 0.5, 1.5),
        "cotangent": noise(seeds[10], (TOKENS, 2 * D), 1.0, 6.0, ((0, 32),)),
    }


EPS = 1e-06
BIG = 1e+30
HIGH = lax.Precision.HIGHEST

@jax.custom_vjp
def low(v):
    return lax.optimization_barrier(v.astype(jnp.bfloat16)).astype(jnp.float32)

@jax.custom_vjp
def low_back(v):
    return v

def low_keep(v):
    return (low(v), None)

def low_pass(kept, grad):
    return (grad,)

def back_keep(v):
    return (v, None)

def back_low(kept, grad):
    return (low(grad),)
low.defvjp(low_keep, low_pass)
low_back.defvjp(back_keep, back_low)

def rms_norm(features, norm_gain):
    return features * lax.rsqrt(lax.optimization_barrier(jnp.mean(features * features, axis=-1, keepdims=True)) + EPS) * norm_gain

def segment_of(lengths_row, total_rows):
    boundary = jnp.cumsum(lengths_row).astype(jnp.int32)
    position = jnp.arange(total_rows, dtype=jnp.int32)
    return lax.optimization_barrier(jnp.sum((position[:, None] >= boundary[None, :]).astype(jnp.int32), axis=1))

def head_attention(operands, allowed):
    head_query, head_key, head_value = operands
    scores = jnp.dot(head_query, head_key.T, precision=HIGH) * 0.125
    scores = low_back(scores)
    scores = jnp.where(allowed, scores, -BIG)
    row_max = lax.optimization_barrier(jnp.max(scores, axis=-1, keepdims=True))
    weights_raw = jnp.exp(scores - row_max)
    attn_probs = weights_raw / lax.optimization_barrier(jnp.sum(weights_raw, axis=-1, keepdims=True))
    return jnp.dot(low(attn_probs), head_value, precision=HIGH)

def group_forward(weights, group_item):
    group_rows, lengths_row = group_item
    w_qkv, w_out, w_gate_up, w_down, gain_attn, gain_ffn, mix_matrix, correct_gain = weights
    stream_one = group_rows[:, :D]
    stream_two = group_rows[:, D:]
    predicted_main = mix_matrix[0, 0] * stream_one + mix_matrix[0, 1] * stream_two
    predicted_side = mix_matrix[1, 0] * stream_one + mix_matrix[1, 1] * stream_two
    normed_attn = low(rms_norm(predicted_main, gain_attn))
    projected = jnp.einsum('td,dkh->tkh', normed_attn, low(w_qkv), precision=HIGH)
    projected = low(low_back(projected))
    segment = segment_of(lengths_row, GROUP_ROWS)
    position = jnp.arange(GROUP_ROWS, dtype=jnp.int32)
    allowed = (segment[:, None] == segment[None, :]) & (position[None, :] <= position[:, None])
    queries = projected[:, 0].reshape(GROUP_ROWS, HEADS, HEAD_DIM).transpose(1, 0, 2)
    all_keys = projected[:, 1].reshape(GROUP_ROWS, HEADS, HEAD_DIM).transpose(1, 0, 2)
    values = projected[:, 2].reshape(GROUP_ROWS, HEADS, HEAD_DIM).transpose(1, 0, 2)
    head_fn = jax.checkpoint(lambda operands: head_attention(operands, allowed))
    attended = lax.map(head_fn, (queries, all_keys, values))
    attn_heads = attended.transpose(1, 0, 2).reshape(GROUP_ROWS, D)
    attn_heads = low(low_back(attn_heads))
    attn_branch = low_back(jnp.dot(attn_heads, low(w_out).T, precision=HIGH))
    middle = predicted_main + attn_branch
    normed_ffn = low(rms_norm(middle, gain_ffn))
    gate_up = jnp.einsum('td,dkf->tkf', normed_ffn, low(w_gate_up), precision=HIGH)
    gate_pre = low_back(gate_up[:, 0])
    up_proj = low_back(gate_up[:, 1])
    hidden = low(jax.nn.gelu(gate_pre) * up_proj)
    ffn_branch = low_back(jnp.dot(hidden, low(w_down).T, precision=HIGH))
    layer_top = middle + ffn_branch
    correction = layer_top - predicted_main
    return jnp.concatenate([predicted_main + correct_gain[0] * correction, predicted_side + correct_gain[1] * correction], axis=1)

def reference(block_input, seq_lengths, w_qkv, w_out, w_gate_up, w_down, gain_attn, gain_ffn, mix_matrix, correct_gain, cotangent):
    inputs = block_input.astype(jnp.float32)

    def forward(inputs, w_qkv, w_out, w_gate_up, w_down, gain_attn, gain_ffn, mix_matrix, correct_gain):
        weights = (w_qkv, w_out, w_gate_up, w_down, gain_attn, gain_ffn, mix_matrix, correct_gain)
        grouped = inputs.reshape(N_DP, GROUP_ROWS, 2 * D)
        group_fn = jax.checkpoint(lambda group_item: group_forward(weights, group_item))
        outputs = lax.map(group_fn, (grouped, seq_lengths))
        return outputs.reshape(TOKENS, 2 * D)
    block_output, pull_back = jax.vjp(forward, inputs, w_qkv, w_out, w_gate_up, w_down, gain_attn, gain_ffn, mix_matrix, correct_gain)
    grads = pull_back(cotangent.astype(jnp.float32))
    return (block_output.astype(jnp.bfloat16), grads[0], grads[1], grads[2], grads[3], grads[4], grads[5], grads[6], grads[7], grads[8])
```

```python
import functools
import math

import jax
import jax.numpy as jnp
from jax import lax
from jax.experimental import pallas as pl
from jax.experimental.pallas import tpu as pltpu
from jax.sharding import PartitionSpec as P

HEAD_DIM = 64
EPS = 1e-06
BIG = 1e30
BLK = 256
SUB = 128
MESH = pl.DeviceIdType.MESH


def dot(a, b):
    return jnp.dot(a, b, preferred_element_type=jnp.float32)


def dot_nt(a, b):
    return lax.dot_general(a, b, (((1,), (1,)), ((), ())), preferred_element_type=jnp.float32)


def dot_tn(a, b):
    return lax.dot_general(a, b, (((0,), (0,)), ((), ())), preferred_element_type=jnp.float32)


def turned(a):
    return a.astype(jnp.float32).T


def seg_vector(len_ref, pos):
    begin = jnp.zeros_like(pos)
    edge = jnp.int32(0)
    for k in range(len_ref.shape[1] - 1):
        edge = edge + len_ref[0, k]
        begin = jnp.where(pos >= edge, edge, begin)
    return begin


def seg_scalar(len_ref, row):
    begin = jnp.int32(0)
    end = jnp.int32(0)
    edge = jnp.int32(0)
    for k in range(len_ref.shape[1]):
        after = edge + len_ref[0, k]
        inside = (row >= edge) & (row < after)
        begin = jnp.where(inside, edge, begin)
        end = jnp.where(inside, after, end)
        edge = after
    return begin, end


def place(me, chunk, per):
    return (chunk // per) ^ me, pl.multiple_of((chunk % per) * SUB, SUB)


def fwd_kernel(heads, parts, len_ref, me_ref, *refs):
    proj = refs[:parts]
    o_ref, ot_ref, lse_ref, qt, kh, vt, acc, mx, tot = refs[parts:]
    i = pl.program_id(0)
    part_rows = proj[0].shape[0]
    per = part_rows // SUB
    blk, hd = BLK, HEAD_DIM
    feats = heads * hd
    me = me_ref[0]

    @pl.when(i == 0)
    def _():
        for c in range(parts):
            base = (me ^ c) * part_rows
            def turn(s, carry, c=c, base=base):
                src = pl.ds(pl.multiple_of(s * SUB, SUB), SUB)
                at = pl.ds(pl.multiple_of(base + s * SUB, SUB), SUB)
                rows = proj[c][src, :]
                qt[:, at] = (turned(rows[:, :feats]) * 0.125).astype(jnp.bfloat16)
                vt[:, at] = turned(rows[:, 2 * feats :]).astype(jnp.bfloat16)
                for h in range(heads):
                    kh[h, at, :] = rows[:, feats + h * hd : feats + (h + 1) * hd]
                return carry
            lax.fori_loop(0, per, turn, 0)

    first = pl.multiple_of(i * blk, blk)
    cols = pl.ds(first, blk)
    pos = first + lax.broadcasted_iota(jnp.int32, (1, blk), 1)
    begin = seg_vector(len_ref, pos)
    b_first, _ = seg_scalar(len_ref, first)
    b_last, _ = seg_scalar(len_ref, first + blk - 1)
    j_lo = b_first // blk
    j_full = jnp.minimum((b_last + blk - 1) // blk, i)
    mx[...] = jnp.full_like(mx, -BIG)
    tot[...] = jnp.zeros_like(tot)
    acc[...] = jnp.zeros_like(acc)

    def step(j, masked, first_pass):
        at = pl.ds(pl.multiple_of(j * blk, blk), blk)
        if masked:
            key = j * blk + lax.broadcasted_iota(jnp.int32, (blk, blk), 0)
            ok = (key >= begin) & (key <= pos)
        scores = []
        for h in range(heads):
            s = dot(kh[h, at, :], qt[h * hd : (h + 1) * hd, cols])
            scores.append(jnp.where(ok, s, -BIG) if masked else s)
        if first_pass:
            for h in range(heads):
                old = mx[h : h + 1]
                new = jnp.maximum(old, jnp.max(scores[h], axis=0, keepdims=True))
                total = jnp.sum(jnp.exp(scores[h] - new), axis=0, keepdims=True)
                mx[h : h + 1] = new
                tot[h : h + 1] = jnp.exp(old - new) * tot[h : h + 1] + total
        else:
            for h in range(heads):
                hs = slice(h * hd, (h + 1) * hd)
                p = jnp.exp(scores[h] - mx[h : h + 1])
                acc[hs] += dot(vt[hs, at], p.astype(jnp.bfloat16))

    def loop(lo, hi, masked, first_pass):
        def body(j, carry):
            step(j, masked, first_pass)
            return carry
        lax.fori_loop(lo, hi, body, 0)

    for first_pass in (True, False):
        loop(j_lo, j_full, True, first_pass)
        loop(jnp.maximum(j_full, j_lo), i, False, first_pass)
        step(i, True, first_pass)
        if first_pass:
            mx[...] = mx[...] + jnp.log(tot[...])
            lse_ref[...] = mx[...]
    ot_ref[...] = acc[...]
    out = acc[...].T.astype(jnp.bfloat16)
    for s in range(blk // SUB):
        c, row = place(me, i * (blk // SUB) + s, per)
        o_ref[c, pl.ds(row, SUB), :] = out[s * SUB : (s + 1) * SUB]


def attn_fwd(lengths, me, proj):
    parts = len(proj)
    part_rows, width = proj[0].shape
    feats = width // 3
    rows = parts * part_rows
    heads = feats // HEAD_DIM
    return pl.pallas_call(
        functools.partial(fwd_kernel, heads, parts),
        out_shape=(
            jax.ShapeDtypeStruct((parts, part_rows, feats), jnp.bfloat16),
            jax.ShapeDtypeStruct((feats, rows), jnp.float32),
            jax.ShapeDtypeStruct((8, rows), jnp.float32),
        ),
        grid_spec=pltpu.PrefetchScalarGridSpec(
            num_scalar_prefetch=2,
            grid=(rows // BLK,),
            in_specs=[pl.BlockSpec((part_rows, width), lambda i, s, m: (0, 0))] * parts,
            out_specs=(
                pl.BlockSpec((parts, part_rows, feats), lambda i, s, m: (0, 0, 0)),
                pl.BlockSpec((feats, BLK), lambda i, s, m: (0, i)),
                pl.BlockSpec((8, BLK), lambda i, s, m: (0, i)),
            ),
            scratch_shapes=[
                pltpu.VMEM((feats, rows), jnp.bfloat16),
                pltpu.VMEM((heads, rows, HEAD_DIM), jnp.bfloat16),
                pltpu.VMEM((feats, rows), jnp.bfloat16),
                pltpu.VMEM((feats, BLK), jnp.float32),
                pltpu.VMEM((8, BLK), jnp.float32),
                pltpu.VMEM((8, BLK), jnp.float32),
            ],
        ),
        cost_estimate=pl.CostEstimate(
            flops=rows * feats * 4096, bytes_accessed=12 * rows * feats, transcendentals=rows * 512 * heads
        ),
        name="attn_fwd",
    )(lengths, me, *proj)


def bwd_kernel(heads, parts, len_ref, me_ref, *refs):
    proj = refs[:parts]
    grads = refs[parts : 2 * parts]
    ot_ref, lse_ref, d_ref, qt, qp, gt, gp, kh, vh, kt, dqt, delta, dkv = refs[2 * parts :]
    j = pl.program_id(0)
    n = pl.num_programs(0)
    part_rows = proj[0].shape[0]
    per = part_rows // SUB
    blk, hd = BLK, HEAD_DIM
    feats = heads * hd
    me = me_ref[0]

    @pl.when(j == 0)
    def _():
        zero = jnp.zeros((SUB, hd), jnp.bfloat16)
        for c in range(parts):
            base = (me ^ c) * part_rows
            def turn(s, carry, c=c, base=base):
                src = pl.ds(pl.multiple_of(s * SUB, SUB), SUB)
                at = pl.ds(pl.multiple_of(base + s * SUB, SUB), SUB)
                rows = proj[c][src, :]
                g = grads[c][src, :]
                g_turned = turned(g)
                qt[:, at] = (turned(rows[:, :feats]) * 0.125).astype(jnp.bfloat16)
                kt[:, at] = turned(rows[:, feats : 2 * feats]).astype(jnp.bfloat16)
                gt[:, at] = g_turned.astype(jnp.bfloat16)
                prod = g_turned * ot_ref[:, at]
                dqt[:, at] = jnp.zeros((feats, SUB), jnp.float32)
                for h in range(heads):
                    hs = slice(h * hd, (h + 1) * hd)
                    delta[h : h + 1, at] = jnp.sum(prod[hs], axis=0, keepdims=True)
                    qp[h, at, :] = jnp.concatenate([rows[:, hs], zero], axis=1)
                    gp[h, at, :] = jnp.concatenate([zero, g[:, hs]], axis=1)
                    kh[h, at, :] = rows[:, feats + h * hd : feats + (h + 1) * hd]
                    vh[h, at, :] = rows[:, 2 * feats + h * hd : 2 * feats + (h + 1) * hd]
                return carry
            lax.fori_loop(0, per, turn, 0)

    first = pl.multiple_of(j * blk, blk)
    keys = pl.ds(first, blk)
    _, e_first = seg_scalar(len_ref, first)
    _, e_last = seg_scalar(len_ref, first + blk - 1)
    i_hi = (e_last - 1) // blk + 1
    i_full = jnp.clip(e_first // blk, j + 1, i_hi)
    key = first + lax.broadcasted_iota(jnp.int32, (blk, blk), 0)

    def step(i, masked, start):
        at = pl.ds(pl.multiple_of(i * blk, blk), blk)
        if masked:
            pos = i * blk + lax.broadcasted_iota(jnp.int32, (1, blk), 1)
            begin = seg_vector(len_ref, pos)
            ok = (key >= begin) & (key <= pos)
        scores, dprobs = [], []
        for h in range(heads):
            hs = slice(h * hd, (h + 1) * hd)
            scores.append(dot(kh[h, keys, :], qt[hs, at]))
            dprobs.append(dot(vh[h, keys, :], gt[hs, at]))
        both = []
        for h in range(heads):
            e = scores[h] - lse_ref[h : h + 1, at]
            if masked:
                e = jnp.where(ok, e, -BIG)
            p = jnp.exp(e)
            ds = p * (dprobs[h] - delta[h : h + 1, at])
            both.append((p.astype(jnp.bfloat16), ds.astype(jnp.bfloat16)))
        for h in range(heads):
            hs = slice(h * hd, (h + 1) * hd)
            p, ds = both[h]
            add = dot(
                jnp.concatenate([ds, p], axis=1),
                jnp.concatenate([qp[h, at, :], gp[h, at, :]], axis=0),
            )
            if start:
                dkv[h] = add
            else:
                dkv[h] += add
            dqt[hs, at] += dot(kt[hs, keys], ds)

    def loop(lo, hi, masked):
        def body(i, carry):
            step(i, masked, False)
            return carry
        lax.fori_loop(lo, hi, body, 0)

    step(j, True, True)
    loop(j + 1, i_full, False)
    loop(i_full, i_hi, True)
    pair = jnp.concatenate(
        [dkv[h][:, :hd] * 0.125 for h in range(heads)] + [dkv[h][:, hd:] for h in range(heads)], axis=1
    ).astype(jnp.bfloat16)
    for s in range(blk // SUB):
        c, row = place(me, j * (blk // SUB) + s, per)
        d_ref[c, pl.ds(row, SUB), feats:] = pair[s * SUB : (s + 1) * SUB]

    @pl.when(j == n - 1)
    def _():
        for c in range(parts):
            base = (me ^ c) * part_rows
            def turn(s, carry, c=c, base=base):
                at = pl.ds(pl.multiple_of(base + s * SUB, SUB), SUB)
                dst = pl.ds(pl.multiple_of(s * SUB, SUB), SUB)
                d_ref[c, dst, :feats] = (dqt[:, at] * 0.125).T.astype(jnp.bfloat16)
                return carry
            lax.fori_loop(0, per, turn, 0)


def attn_bwd(lengths, me, proj, grads, heads_turned, log_total):
    parts = len(proj)
    part_rows, width = proj[0].shape
    feats = width // 3
    rows = parts * part_rows
    heads = feats // HEAD_DIM
    return pl.pallas_call(
        functools.partial(bwd_kernel, heads, parts),
        out_shape=jax.ShapeDtypeStruct((parts, part_rows, width), jnp.bfloat16),
        grid_spec=pltpu.PrefetchScalarGridSpec(
            num_scalar_prefetch=2,
            grid=(rows // BLK,),
            in_specs=[pl.BlockSpec((part_rows, width), lambda i, s, m: (0, 0))] * parts
            + [pl.BlockSpec((part_rows, feats), lambda i, s, m: (0, 0))] * parts
            + [
                pl.BlockSpec((feats, rows), lambda i, s, m: (0, 0)),
                pl.BlockSpec((8, rows), lambda i, s, m: (0, 0)),
            ],
            out_specs=pl.BlockSpec((parts, part_rows, width), lambda i, s, m: (0, 0, 0)),
            scratch_shapes=[
                pltpu.VMEM((feats, rows), jnp.bfloat16),
                pltpu.VMEM((heads, rows, 2 * HEAD_DIM), jnp.bfloat16),
                pltpu.VMEM((feats, rows), jnp.bfloat16),
                pltpu.VMEM((heads, rows, 2 * HEAD_DIM), jnp.bfloat16),
                pltpu.VMEM((heads, rows, HEAD_DIM), jnp.bfloat16),
                pltpu.VMEM((heads, rows, HEAD_DIM), jnp.bfloat16),
                pltpu.VMEM((feats, rows), jnp.bfloat16),
                pltpu.VMEM((feats, rows), jnp.float32),
                pltpu.VMEM((8, rows), jnp.float32),
                pltpu.VMEM((heads, BLK, 2 * HEAD_DIM), jnp.float32),
            ],
        ),
        cost_estimate=pl.CostEstimate(
            flops=rows * feats * 10240, bytes_accessed=20 * rows * feats, transcendentals=rows * 512 * heads
        ),
        name="attn_bwd",
    )(lengths, me, *proj, *grads, heads_turned, log_total)


def gelu_parts(v):
    c = math.sqrt(2 / math.pi)
    square = v * v
    t = jnp.tanh(c * v * (1.0 + 0.044715 * square))
    half = 0.5 * (1.0 + t)
    slope = half + (0.5 * v) * (1.0 - t * t) * (c * (1.0 + 3 * 0.044715 * square))
    return v * half, slope


def ffn_kernel(tile, x_ref, g_ref, wg_ref, wu_ref, wd_ref, h_ref, dg_ref, du_ref, branch_ref, dx_ref, branch, dx):
    u = pl.program_id(0)
    x = x_ref[...]
    gate = dot(x, wg_ref[...])
    up = dot(x, wu_ref[...])
    grad_hidden = dot(g_ref[...], wd_ref[...])
    act, slope = gelu_parts(gate)
    hidden = (act * up).astype(jnp.bfloat16)
    dgate = (slope * (grad_hidden * up)).astype(jnp.bfloat16)
    dup = (grad_hidden * act).astype(jnp.bfloat16)
    h_ref[...] = hidden
    dg_ref[...] = dgate
    du_ref[...] = dup
    b_add = dot_nt(hidden, wd_ref[...])
    d_add = dot_nt(dgate, wg_ref[...]) + dot_nt(dup, wu_ref[...])

    @pl.when(u == 0)
    def _():
        branch[...] = b_add
        dx[...] = d_add

    @pl.when(u > 0)
    def _():
        branch[...] += b_add
        dx[...] += d_add

    @pl.when(u == pl.num_programs(0) - 1)
    def _():
        branch_ref[...] = branch[...]
        dx_ref[...] = dx[...].astype(jnp.bfloat16)


def ffn_rows(x, g, weights, tile=256):
    rows, d = x.shape
    units = weights.shape[1] // 3
    n = units // tile
    full = pl.BlockSpec((rows, d), lambda u: (0, 0))
    cols = pl.BlockSpec((rows, tile), lambda u: (0, u))
    wide = jax.ShapeDtypeStruct((rows, units), jnp.bfloat16)
    narrow = jax.ShapeDtypeStruct((rows, d), jnp.bfloat16)
    return pl.pallas_call(
        functools.partial(ffn_kernel, tile),
        out_shape=(wide, wide, wide, jax.ShapeDtypeStruct((rows, d), jnp.float32), narrow),
        grid=(n,),
        in_specs=[
            full,
            full,
            pl.BlockSpec((d, tile), lambda u: (0, u)),
            pl.BlockSpec((d, tile), lambda u: (0, u + n)),
            pl.BlockSpec((d, tile), lambda u: (0, u + 2 * n)),
        ],
        out_specs=(cols, cols, cols, full, full),
        scratch_shapes=[pltpu.VMEM((rows, d), jnp.float32), pltpu.VMEM((rows, d), jnp.float32)],
        cost_estimate=pl.CostEstimate(
            flops=12 * rows * d * units,
            bytes_accessed=2 * (4 * rows * d + 3 * rows * units + 3 * d * units),
            transcendentals=rows * units,
        ),
        name="ffn_rows",
    )(x, g, weights, weights, weights)


def wgrad_kernel(parts, n, *refs):
    xs, gs, gates, ups, hiddens = [refs[parts * m : parts * (m + 1)] for m in range(5)]
    out, left_t = refs[-2:]
    i = pl.program_id(0)
    rows = xs[0].shape[0]

    def turn_all(lefts):
        for c in range(parts):
            def turn(s, carry, c=c):
                src = pl.ds(pl.multiple_of(s * SUB, SUB), SUB)
                at = pl.ds(pl.multiple_of(c * rows + s * SUB, SUB), SUB)
                left_t[:, at] = turned(lefts[c][src, :]).astype(jnp.bfloat16)
                return carry
            lax.fori_loop(0, rows // SUB, turn, 0)

    def product(rights):
        total = dot(left_t[:, :rows], rights[0][...])
        for c in range(1, parts):
            total += dot(left_t[:, c * rows : (c + 1) * rows], rights[c][...])
        out[...] = total.astype(jnp.bfloat16)

    @pl.when(i == 0)
    def _():
        turn_all(xs)

    @pl.when(i == 2 * n)
    def _():
        turn_all(gs)

    @pl.when(i < n)
    def _():
        product(gates)

    @pl.when((i >= n) & (i < 2 * n))
    def _():
        product(ups)

    @pl.when(i >= 2 * n)
    def _():
        product(hiddens)


def wgrad(xs, gs, gates, ups, hiddens, tile=256):
    parts = len(xs)
    rows, d = xs[0].shape
    units = gates[0].shape[1]
    n = units // tile

    def tiles(m):
        return [pl.BlockSpec((rows, tile), lambda i: (0, jnp.clip(i - m * n, 0, n - 1)))] * parts

    return pl.pallas_call(
        functools.partial(wgrad_kernel, parts, n),
        out_shape=jax.ShapeDtypeStruct((d, 3 * units), jnp.bfloat16),
        grid=(3 * n,),
        in_specs=[pl.BlockSpec((rows, d), lambda i: (0, 0))] * (2 * parts) + tiles(0) + tiles(1) + tiles(2),
        out_specs=pl.BlockSpec((d, tile), lambda i: (0, i)),
        scratch_shapes=[pltpu.VMEM((d, parts * rows), jnp.bfloat16)],
        cost_estimate=pl.CostEstimate(
            flops=6 * parts * rows * d * units,
            bytes_accessed=2 * parts * rows * (2 * d + 3 * units) + 6 * d * units,
            transcendentals=0,
        ),
        name="wgrad",
    )(*xs, *gs, *gates, *ups, *hiddens)


def rms_norm(features, norm_gain):
    return features * lax.rsqrt(jnp.mean(features * features, axis=-1, keepdims=True) + EPS) * norm_gain


def norm_pull(features, norm_gain, incoming):
    rate = lax.rsqrt(jnp.mean(features * features, axis=-1, keepdims=True) + EPS)
    scaled = norm_gain * incoming
    dot_mean = jnp.mean(scaled * features, axis=-1, keepdims=True)
    grad = rate * scaled - features * (rate * rate * rate * dot_mean)
    return grad, jnp.sum(incoming * features * rate, axis=0)


def swap(array, bit):
    count = lax.axis_size("tensor")
    return lax.ppermute(array, "tensor", [(i, i ^ bit) for i in range(count)])


def after(value, *others):
    return lax.optimization_barrier((value, *others))[0]


def flipped(index, bits):
    bit = 1
    while bit <= bits:
        if bits & bit:
            index = index + bit - 2 * bit * lax.rem(lax.div(index, bit), 2)
        bit *= 2
    return index


def start_kernel(
    count, chunks, x, qkv, wo, sib, far, diag, qkv_all, wo_all,
    local_sem, sib_sem, far_send, far_recv, diag_send, diag_recv, wo_send, wo_recv, qkv_dp, wo_dp,
):
    t = lax.axis_index("tensor")
    g = lax.axis_index("dp")
    order = []
    bit = 2
    while bit < count:
        order.append(bit)
        bit *= 2
    order.append(1)

    def last(e):
        return max(k for k, b in enumerate(order) if e & b)

    barrier = pltpu.get_barrier_semaphore()
    for c in (1, 2, 3):
        pl.semaphore_signal(barrier, inc=1, device_id={"tensor": flipped(t, c)}, device_id_type=MESH)
    for b in order:
        pl.semaphore_signal(barrier, inc=1, device_id={"dp": flipped(g, b)}, device_id_type=MESH)
    pl.semaphore_wait(barrier, 3 + len(order))

    size = x.shape[0] // chunks

    def far_copy(k):
        rows = pl.ds(k * size, size)
        return pltpu.make_async_remote_copy(
            x.at[rows], far.at[rows], far_send.at[k], far_recv.at[k], {"tensor": flipped(t, 2)}, MESH
        )

    def diag_copy(k):
        rows = pl.ds(k * size, size)
        return pltpu.make_async_remote_copy(
            far.at[rows], diag.at[rows], diag_send.at[k], diag_recv.at[k], {"tensor": flipped(t, 1)}, MESH
        )

    def wo_copy(c):
        return pltpu.make_async_remote_copy(
            wo, wo_all.at[c, g], wo_send.at[c - 1], wo_recv.at[c - 1], {"tensor": flipped(t, c)}, MESH
        )

    def dp_copy(which, e):
        b = order[last(e)]
        block = flipped(g, e ^ b)
        if which == 0:
            src = qkv if e == b else qkv_all.at[block]
            dst, sems = qkv_all.at[block], qkv_dp
        else:
            src = dst = wo_all.at[:, block]
            sems = wo_dp
        return pltpu.make_async_remote_copy(
            src, dst, sems.at[0, e - 1], sems.at[1, e - 1], {"dp": flipped(g, b)}, MESH
        )

    def dp_arrival(which, e):
        block = flipped(g, e)
        dst, sems = (qkv_all.at[block], qkv_dp) if which == 0 else (wo_all.at[:, block], wo_dp)
        return pltpu.make_async_remote_copy(
            dst, dst, sems.at[0, e - 1], sems.at[1, e - 1], {"dp": flipped(g, order[last(e)])}, MESH
        )

    sends = []

    def go(copy):
        copy.start()
        sends.append(copy)

    wos = [wo_copy(c) for c in (1, 2, 3)]
    for copy in wos:
        go(copy)
    for b in order:
        go(dp_copy(0, b))
    fars = [far_copy(k) for k in range(chunks)]
    for copy in fars:
        go(copy)
    near = pltpu.make_async_remote_copy(
        x, sib, sib_sem.at[0], sib_sem.at[1], {"tensor": flipped(t, 1)}, MESH
    )
    go(near)
    kept = [
        pltpu.make_async_copy(qkv, qkv_all.at[g], local_sem.at[0]),
        pltpu.make_async_copy(wo, wo_all.at[0, g], local_sem.at[1]),
    ]
    for copy in kept:
        copy.start()
    for copy in kept:
        copy.wait()
    for copy in wos:
        copy.wait_recv()
    for b in order:
        go(dp_copy(1, b))
    diags = []

    def pass_on(k):
        fars[k].wait_recv()
        diags.append(diag_copy(k))
        go(diags[-1])

    done = 0
    for e in sorted(range(1, count), key=lambda e: (last(e), e)):
        for which in (0, 1):
            dp_arrival(which, e).wait_recv()
            for b in order[last(e) + 1 :]:
                go(dp_copy(which, e ^ b))
        if done < chunks and e & 1 == 0:
            pass_on(done)
            done += 1
    while done < chunks:
        pass_on(done)
        done += 1
    for copy in diags:
        copy.wait_recv()
    near.wait_recv()
    for copy in sends:
        copy.wait_send()


def start(x, qkv, wo, chunks=4):
    count = lax.axis_size("dp")
    rows = jax.ShapeDtypeStruct(x.shape, x.dtype)
    dma = pltpu.SemaphoreType.DMA
    sib, far, diag, qkv_all, wo_all = pl.pallas_call(
        functools.partial(start_kernel, count, chunks),
        out_shape=(
            rows,
            rows,
            rows,
            jax.ShapeDtypeStruct((count, *qkv.shape), qkv.dtype),
            jax.ShapeDtypeStruct((4, count, *wo.shape), wo.dtype),
        ),
        in_specs=[pl.BlockSpec(memory_space=pl.ANY)] * 3,
        out_specs=(pl.BlockSpec(memory_space=pl.ANY),) * 5,
        scratch_shapes=[
            dma((2,)),
            dma((2,)),
            dma((chunks,)),
            dma((chunks,)),
            dma((chunks,)),
            dma((chunks,)),
            dma((3,)),
            dma((3,)),
            dma((2, count - 1)),
            dma((2, count - 1)),
        ],
        compiler_params=pltpu.CompilerParams(collective_id=0, has_side_effects=True),
        cost_estimate=pl.CostEstimate(flops=0, bytes_accessed=100_000_000, transcendentals=0),
        name="start",
    )(x, qkv, wo)
    whole = count * qkv.shape[0]
    return [x, sib, far, diag], qkv_all.reshape(whole, -1), [wo_all[c].reshape(whole, -1) for c in range(4)]


def spread(rows):
    far = swap(rows, 2)
    return [rows, swap(rows, 1), far, swap(far, 1)]


def exchange(blocks):
    return [blocks[0]] + [swap(blocks[c], c) for c in range(1, len(blocks))]


def summed(shares, before=None, beside=None):
    f32 = jnp.float32
    far = (shares[2].astype(f32) + swap(shares[3], 1).astype(f32)).astype(jnp.bfloat16)
    if before is not None:
        far = after(far, before)
    got = swap(far, 2)
    near = shares[0].astype(f32) + swap(shares[1], 1).astype(f32)
    if beside is not None:
        got, beside = lax.optimization_barrier((got, beside(far)))
    return near + got.astype(f32), beside


def sum_everywhere(array):
    for axis in ("tensor", "dp"):
        count = lax.axis_size(axis)
        bit = 1
        while bit < count:
            array = array + lax.ppermute(array, axis, [(i, i ^ bit) for i in range(count)])
            bit *= 2
    return array


def local(
    block_input, seq_lengths, w_qkv, w_out, w_gate_up, w_down, gain_attn, gain_ffn, mix_matrix, correct_gain, cotangent
):
    f32, bf16 = jnp.float32, jnp.bfloat16
    width = gain_attn.shape[0]
    me = lax.axis_index("tensor").astype(jnp.int32)[None]
    shard = w_qkv.shape[0]
    feats = w_out.shape[1]
    inputs = block_input.astype(f32)
    stream_one = inputs[:, :width]
    stream_two = inputs[:, width:]
    predicted_main = mix_matrix[0, 0] * stream_one + mix_matrix[0, 1] * stream_two
    predicted_side = mix_matrix[1, 0] * stream_one + mix_matrix[1, 1] * stream_two
    units = w_down.shape[1]

    normed_attn, qkv_all, out_parts = start(
        rms_norm(predicted_main, gain_attn).astype(bf16),
        w_qkv.reshape(shard, 3 * feats).astype(bf16),
        w_out.astype(bf16),
    )
    ffn_mine = jnp.concatenate([w_gate_up.reshape(shard, -1), w_down], axis=1).astype(bf16)
    ffn_all = lax.all_gather(after(ffn_mine, normed_attn[1]), "dp", axis=0, tiled=True)
    proj = [dot(x, qkv_all).astype(bf16) for x in normed_attn]
    attended, heads_turned, log_total = attn_fwd(seq_lengths, me, proj)

    incoming = cotangent.astype(f32)
    cot_one = incoming[:, :width]
    cot_two = incoming[:, width:]
    grad_top = correct_gain[0] * cot_one + correct_gain[1] * cot_two
    grad_ffn = spread(after(grad_top.astype(bf16), normed_attn[1]))

    attended = after(attended, grad_ffn[2])
    head_parts = exchange([attended[c] for c in range(len(proj))])
    attn_branch = sum(dot_nt(a, w) for a, w in zip(head_parts, out_parts))
    middle = predicted_main + attn_branch

    normed_mine = rms_norm(middle, gain_ffn).astype(bf16)
    normed_ffn = [normed_mine, swap(normed_mine, 1), swap(normed_mine, 2)]
    pieces = [ffn_rows(x, g, ffn_all) for x, g in zip(normed_ffn, grad_ffn[:2])]
    normed_ffn[2] = after(normed_ffn[2], pieces[0][0], pieces[1][0])
    normed_ffn.append(swap(normed_ffn[2], 1))
    pieces += [ffn_rows(x, g, ffn_all) for x, g in zip(normed_ffn[2:], grad_ffn[2:])]
    hidden, dgate, dup, branch, dnormed = zip(*pieces)
    grad_normed_ffn, weight_ffn = summed(
        dnormed, beside=lambda far: wgrad([after(normed_ffn[0], far)] + normed_ffn[1:], grad_ffn, dgate, dup, hidden)
    )
    weight_ffn = lax.psum_scatter(weight_ffn, "dp", scatter_dimension=0, tiled=True)
    grad_middle_norm, grad_gain_ffn = norm_pull(middle, gain_ffn, grad_normed_ffn)
    grad_middle = grad_top + grad_middle_norm
    grad_attn = grad_middle.astype(bf16)
    grad_heads = exchange([dot(grad_attn, w).astype(bf16) for w in out_parts])
    grad_proj = attn_bwd(seq_lengths, me, proj, grad_heads, heads_turned, log_total)
    *late, later_attn = lax.optimization_barrier((*head_parts, grad_heads[2], grad_heads[3], grad_attn))
    out_shares = exchange([dot_tn(later_attn, a).astype(bf16) for a in late[:4]])
    weight_out = sum(s.astype(f32) for s in out_shares)
    ffn_branch, (grad_proj, weight_out) = summed(branch, before=late[4], beside=lambda far: (grad_proj, weight_out))
    grad_proj = [grad_proj[c] for c in range(len(proj))]

    correction = (middle + ffn_branch) - predicted_main
    block_output = jnp.concatenate(
        [predicted_main + correct_gain[0] * correction, predicted_side + correct_gain[1] * correction], axis=1
    ).astype(bf16)
    grad_correct = jnp.stack([jnp.sum(cot_one * correction), jnp.sum(cot_two * correction)])

    far = [dot_nt(g, qkv_all).astype(bf16) for g in grad_proj[2:]]
    far = (far[0].astype(f32) + swap(far[1], 1).astype(f32)).astype(bf16)
    half = far.shape[0] // 2
    got = [swap(far[:half], 2), swap(far[half:], 2)]
    *late, far = lax.optimization_barrier((*grad_proj, *normed_attn, weight_out, far))
    near = [dot_nt(g, qkv_all).astype(bf16) for g in late[:2]]
    weight_qkv = sum(dot_tn(x, g) for x, g in zip(late[4:8], late[:4]))
    last = jnp.concatenate([weight_qkv, late[8]], axis=1).astype(bf16)
    last = last.reshape(lax.axis_size("dp"), shard, -1)
    last, weight_ffn, got[0] = lax.optimization_barrier((last, weight_ffn, got[0]))
    last = lax.all_to_all(last, "dp", split_axis=0, concat_axis=0, tiled=True)
    near = near[0].astype(f32) + swap(near[1], 1).astype(f32)
    got[1], last, near, grad_correct, block_output = lax.optimization_barrier(
        (got[1], last, near, grad_correct, block_output)
    )
    grad_normed_attn = near + jnp.concatenate(got, axis=0).astype(f32)
    weight_ffn = weight_ffn.astype(f32)
    sum_gate_up = weight_ffn[:, : 2 * units].reshape(shard, 2, units)
    sum_down = weight_ffn[:, 2 * units :]
    last = last.astype(f32).sum(axis=0)
    sum_qkv = last[:, : 3 * feats].reshape(shard, 3, feats)
    sum_out = last[:, 3 * feats :]

    grad_main_norm, grad_gain_attn = norm_pull(predicted_main, gain_attn, grad_normed_attn)
    grad_main = cot_one + grad_middle + grad_main_norm - grad_top
    grad_input = jnp.concatenate(
        [
            mix_matrix[0, 0] * grad_main + mix_matrix[1, 0] * cot_two,
            mix_matrix[0, 1] * grad_main + mix_matrix[1, 1] * cot_two,
        ],
        axis=1,
    )
    small = jnp.stack(
        [
            jnp.sum(grad_main * stream_one),
            jnp.sum(grad_main * stream_two),
            jnp.sum(cot_two * stream_one),
            jnp.sum(cot_two * stream_two),
            grad_correct[0],
            grad_correct[1],
        ]
    )
    small = jnp.stack([grad_gain_attn, grad_gain_ffn, jnp.pad(small, (0, width - small.shape[0]))])
    small = sum_everywhere(small)
    return (
        block_output,
        grad_input,
        sum_qkv,
        sum_out,
        sum_gate_up,
        sum_down,
        small[0],
        small[1],
        small[2, :4].reshape(2, 2),
        small[2, 4:6],
    )


def solution(mesh):
    placed = (
        P(("dp", "tensor"), None),
        P("dp", None),
        P("dp", None, "tensor"),
        P("dp", "tensor"),
        P("dp", None, "tensor"),
        P("dp", "tensor"),
        P(),
        P(),
        P(),
        P(),
        P(("dp", "tensor"), None),
    )
    return jax.shard_map(
        local,
        mesh=mesh,
        in_specs=placed,
        out_specs=(
            P(("dp", "tensor"), None),
            P(("dp", "tensor"), None),
            P("dp", None, "tensor"),
            P("dp", "tensor"),
            P("dp", None, "tensor"),
            P("dp", "tensor"),
            P(),
            P(),
            P(),
            P(),
        ),
        check_vma=False,
    )
```

```python
import functools
import math

import jax
import jax.numpy as jnp
from jax import lax
from jax.experimental import pallas as pl
from jax.experimental.pallas import tpu as pltpu
from jax.sharding import PartitionSpec as P

HEAD_DIM = 64
EPS = 1e-06
BIG = 1e30
BLK = 256
SUB = 128
MESH = pl.DeviceIdType.MESH


def dot(a, b):
    return jnp.dot(a, b, preferred_element_type=jnp.float32)


def dot_nt(a, b):
    return lax.dot_general(a, b, (((1,), (1,)), ((), ())), preferred_element_type=jnp.float32)


def dot_tn(a, b):
    return lax.dot_general(a, b, (((0,), (0,)), ((), ())), preferred_element_type=jnp.float32)


def turned(a):
    return a.astype(jnp.float32).T


def seg_vector(len_ref, pos):
    begin = jnp.zeros_like(pos)
    edge = jnp.int32(0)
    for k in range(len_ref.shape[1] - 1):
        edge = edge + len_ref[0, k]
        begin = jnp.where(pos >= edge, edge, begin)
    return begin


def seg_scalar(len_ref, row):
    begin = jnp.int32(0)
    end = jnp.int32(0)
    edge = jnp.int32(0)
    for k in range(len_ref.shape[1]):
        after = edge + len_ref[0, k]
        inside = (row >= edge) & (row < after)
        begin = jnp.where(inside, edge, begin)
        end = jnp.where(inside, after, end)
        edge = after
    return begin, end


def place(me, chunk, per):
    return (chunk // per) ^ me, pl.multiple_of((chunk % per) * SUB, SUB)


def fwd_kernel(heads, parts, len_ref, me_ref, *refs):
    proj = refs[:parts]
    o_ref, ot_ref, lse_ref, qt, kh, vt, acc, mx, tot = refs[parts:]
    i = pl.program_id(0)
    part_rows = proj[0].shape[0]
    per = part_rows // SUB
    blk, hd = BLK, HEAD_DIM
    feats = heads * hd
    me = me_ref[0]

    @pl.when(i == 0)
    def _():
        for c in range(parts):
            base = (me ^ c) * part_rows
            def turn(s, carry, c=c, base=base):
                src = pl.ds(pl.multiple_of(s * SUB, SUB), SUB)
                at = pl.ds(pl.multiple_of(base + s * SUB, SUB), SUB)
                rows = proj[c][src, :]
                qt[:, at] = (turned(rows[:, :feats]) * 0.125).astype(jnp.bfloat16)
                vt[:, at] = turned(rows[:, 2 * feats :]).astype(jnp.bfloat16)
                for h in range(heads):
                    kh[h, at, :] = rows[:, feats + h * hd : feats + (h + 1) * hd]
                return carry
            lax.fori_loop(0, per, turn, 0)

    first = pl.multiple_of(i * blk, blk)
    cols = pl.ds(first, blk)
    pos = first + lax.broadcasted_iota(jnp.int32, (1, blk), 1)
    begin = seg_vector(len_ref, pos)
    b_first, _ = seg_scalar(len_ref, first)
    b_last, _ = seg_scalar(len_ref, first + blk - 1)
    j_lo = b_first // blk
    j_full = jnp.minimum((b_last + blk - 1) // blk, i)
    mx[...] = jnp.full_like(mx, -BIG)
    tot[...] = jnp.zeros_like(tot)
    acc[...] = jnp.zeros_like(acc)

    def step(j, masked, first_pass):
        at = pl.ds(pl.multiple_of(j * blk, blk), blk)
        if masked:
            key = j * blk + lax.broadcasted_iota(jnp.int32, (blk, blk), 0)
            ok = (key >= begin) & (key <= pos)
        scores = []
        for h in range(heads):
            s = dot(kh[h, at, :], qt[h * hd : (h + 1) * hd, cols])
            scores.append(jnp.where(ok, s, -BIG) if masked else s)
        if first_pass:
            for h in range(heads):
                old = mx[h : h + 1]
                new = jnp.maximum(old, jnp.max(scores[h], axis=0, keepdims=True))
                total = jnp.sum(jnp.exp(scores[h] - new), axis=0, keepdims=True)
                mx[h : h + 1] = new
                tot[h : h + 1] = jnp.exp(old - new) * tot[h : h + 1] + total
        else:
            for h in range(heads):
                hs = slice(h * hd, (h + 1) * hd)
                p = jnp.exp(scores[h] - mx[h : h + 1])
                acc[hs] += dot(vt[hs, at], p.astype(jnp.bfloat16))

    def loop(lo, hi, masked, first_pass):
        def body(j, carry):
            step(j, masked, first_pass)
            return carry
        lax.fori_loop(lo, hi, body, 0)

    for first_pass in (True, False):
        loop(j_lo, j_full, True, first_pass)
        loop(jnp.maximum(j_full, j_lo), i, False, first_pass)
        step(i, True, first_pass)
        if first_pass:
            mx[...] = mx[...] + jnp.log(tot[...])
            lse_ref[...] = mx[...]
    ot_ref[...] = acc[...]
    out = acc[...].T.astype(jnp.bfloat16)
    for s in range(blk // SUB):
        c, row = place(me, i * (blk // SUB) + s, per)
        o_ref[c, pl.ds(row, SUB), :] = out[s * SUB : (s + 1) * SUB]


def attn_fwd(lengths, me, proj):
    parts = len(proj)
    part_rows, width = proj[0].shape
    feats = width // 3
    rows = parts * part_rows
    heads = feats // HEAD_DIM
    return pl.pallas_call(
        functools.partial(fwd_kernel, heads, parts),
        out_shape=(
            jax.ShapeDtypeStruct((parts, part_rows, feats), jnp.bfloat16),
            jax.ShapeDtypeStruct((feats, rows), jnp.float32),
            jax.ShapeDtypeStruct((8, rows), jnp.float32),
        ),
        grid_spec=pltpu.PrefetchScalarGridSpec(
            num_scalar_prefetch=2,
            grid=(rows // BLK,),
            in_specs=[pl.BlockSpec((part_rows, width), lambda i, s, m: (0, 0))] * parts,
            out_specs=(
                pl.BlockSpec((parts, part_rows, feats), lambda i, s, m: (0, 0, 0)),
                pl.BlockSpec((feats, BLK), lambda i, s, m: (0, i)),
                pl.BlockSpec((8, BLK), lambda i, s, m: (0, i)),
            ),
            scratch_shapes=[
                pltpu.VMEM((feats, rows), jnp.bfloat16),
                pltpu.VMEM((heads, rows, HEAD_DIM), jnp.bfloat16),
                pltpu.VMEM((feats, rows), jnp.bfloat16),
                pltpu.VMEM((feats, BLK), jnp.float32),
                pltpu.VMEM((8, BLK), jnp.float32),
                pltpu.VMEM((8, BLK), jnp.float32),
            ],
        ),
        cost_estimate=pl.CostEstimate(
            flops=rows * feats * 4096, bytes_accessed=12 * rows * feats, transcendentals=rows * 512 * heads
        ),
        name="attn_fwd",
    )(lengths, me, *proj)


def bwd_kernel(heads, parts, len_ref, me_ref, *refs):
    proj = refs[:parts]
    grads = refs[parts : 2 * parts]
    ot_ref, lse_ref, d_ref, qt, qp, gt, gp, kh, vh, kt, dqt, delta, dkv = refs[2 * parts :]
    j = pl.program_id(0)
    n = pl.num_programs(0)
    part_rows = proj[0].shape[0]
    per = part_rows // SUB
    blk, hd = BLK, HEAD_DIM
    feats = heads * hd
    me = me_ref[0]

    @pl.when(j == 0)
    def _():
        zero = jnp.zeros((SUB, hd), jnp.bfloat16)
        for c in range(parts):
            base = (me ^ c) * part_rows
            def turn(s, carry, c=c, base=base):
                src = pl.ds(pl.multiple_of(s * SUB, SUB), SUB)
                at = pl.ds(pl.multiple_of(base + s * SUB, SUB), SUB)
                rows = proj[c][src, :]
                g = grads[c][src, :]
                g_turned = turned(g)
                qt[:, at] = (turned(rows[:, :feats]) * 0.125).astype(jnp.bfloat16)
                kt[:, at] = turned(rows[:, feats : 2 * feats]).astype(jnp.bfloat16)
                gt[:, at] = g_turned.astype(jnp.bfloat16)
                prod = g_turned * ot_ref[:, at]
                dqt[:, at] = jnp.zeros((feats, SUB), jnp.float32)
                for h in range(heads):
                    hs = slice(h * hd, (h + 1) * hd)
                    delta[h : h + 1, at] = jnp.sum(prod[hs], axis=0, keepdims=True)
                    qp[h, at, :] = jnp.concatenate([rows[:, hs], zero], axis=1)
                    gp[h, at, :] = jnp.concatenate([zero, g[:, hs]], axis=1)
                    kh[h, at, :] = rows[:, feats + h * hd : feats + (h + 1) * hd]
                    vh[h, at, :] = rows[:, 2 * feats + h * hd : 2 * feats + (h + 1) * hd]
                return carry
            lax.fori_loop(0, per, turn, 0)

    first = pl.multiple_of(j * blk, blk)
    keys = pl.ds(first, blk)
    _, e_first = seg_scalar(len_ref, first)
    _, e_last = seg_scalar(len_ref, first + blk - 1)
    i_hi = (e_last - 1) // blk + 1
    i_full = jnp.clip(e_first // blk, j + 1, i_hi)
    key = first + lax.broadcasted_iota(jnp.int32, (blk, blk), 0)

    def step(i, masked, start):
        at = pl.ds(pl.multiple_of(i * blk, blk), blk)
        if masked:
            pos = i * blk + lax.broadcasted_iota(jnp.int32, (1, blk), 1)
            begin = seg_vector(len_ref, pos)
            ok = (key >= begin) & (key <= pos)
        scores, dprobs = [], []
        for h in range(heads):
            hs = slice(h * hd, (h + 1) * hd)
            scores.append(dot(kh[h, keys, :], qt[hs, at]))
            dprobs.append(dot(vh[h, keys, :], gt[hs, at]))
        both = []
        for h in range(heads):
            e = scores[h] - lse_ref[h : h + 1, at]
            if masked:
                e = jnp.where(ok, e, -BIG)
            p = jnp.exp(e)
            ds = p * (dprobs[h] - delta[h : h + 1, at])
            both.append((p.astype(jnp.bfloat16), ds.astype(jnp.bfloat16)))
        for h in range(heads):
            hs = slice(h * hd, (h + 1) * hd)
            p, ds = both[h]
            add = dot(
                jnp.concatenate([ds, p], axis=1),
                jnp.concatenate([qp[h, at, :], gp[h, at, :]], axis=0),
            )
            if start:
                dkv[h] = add
            else:
                dkv[h] += add
            dqt[hs, at] += dot(kt[hs, keys], ds)

    def loop(lo, hi, masked):
        def body(i, carry):
            step(i, masked, False)
            return carry
        lax.fori_loop(lo, hi, body, 0)

    step(j, True, True)
    loop(j + 1, i_full, False)
    loop(i_full, i_hi, True)
    pair = jnp.concatenate(
        [dkv[h][:, :hd] * 0.125 for h in range(heads)] + [dkv[h][:, hd:] for h in range(heads)], axis=1
    ).astype(jnp.bfloat16)
    for s in range(blk // SUB):
        c, row = place(me, j * (blk // SUB) + s, per)
        d_ref[c, pl.ds(row, SUB), feats:] = pair[s * SUB : (s + 1) * SUB]

    @pl.when(j == n - 1)
    def _():
        for c in range(parts):
            base = (me ^ c) * part_rows
            def turn(s, carry, c=c, base=base):
                at = pl.ds(pl.multiple_of(base + s * SUB, SUB), SUB)
                dst = pl.ds(pl.multiple_of(s * SUB, SUB), SUB)
                d_ref[c, dst, :feats] = (dqt[:, at] * 0.125).T.astype(jnp.bfloat16)
                return carry
            lax.fori_loop(0, per, turn, 0)


def attn_bwd(lengths, me, proj, grads, heads_turned, log_total):
    parts = len(proj)
    part_rows, width = proj[0].shape
    feats = width // 3
    rows = parts * part_rows
    heads = feats // HEAD_DIM
    return pl.pallas_call(
        functools.partial(bwd_kernel, heads, parts),
        out_shape=jax.ShapeDtypeStruct((parts, part_rows, width), jnp.bfloat16),
        grid_spec=pltpu.PrefetchScalarGridSpec(
            num_scalar_prefetch=2,
            grid=(rows // BLK,),
            in_specs=[pl.BlockSpec((part_rows, width), lambda i, s, m: (0, 0))] * parts
            + [pl.BlockSpec((part_rows, feats), lambda i, s, m: (0, 0))] * parts
            + [
                pl.BlockSpec((feats, rows), lambda i, s, m: (0, 0)),
                pl.BlockSpec((8, rows), lambda i, s, m: (0, 0)),
            ],
            out_specs=pl.BlockSpec((parts, part_rows, width), lambda i, s, m: (0, 0, 0)),
            scratch_shapes=[
                pltpu.VMEM((feats, rows), jnp.bfloat16),
                pltpu.VMEM((heads, rows, 2 * HEAD_DIM), jnp.bfloat16),
                pltpu.VMEM((feats, rows), jnp.bfloat16),
                pltpu.VMEM((heads, rows, 2 * HEAD_DIM), jnp.bfloat16),
                pltpu.VMEM((heads, rows, HEAD_DIM), jnp.bfloat16),
                pltpu.VMEM((heads, rows, HEAD_DIM), jnp.bfloat16),
                pltpu.VMEM((feats, rows), jnp.bfloat16),
                pltpu.VMEM((feats, rows), jnp.float32),
                pltpu.VMEM((8, rows), jnp.float32),
                pltpu.VMEM((heads, BLK, 2 * HEAD_DIM), jnp.float32),
            ],
        ),
        cost_estimate=pl.CostEstimate(
            flops=rows * feats * 10240, bytes_accessed=20 * rows * feats, transcendentals=rows * 512 * heads
        ),
        name="attn_bwd",
    )(lengths, me, *proj, *grads, heads_turned, log_total)


def gelu_parts(v):
    c = math.sqrt(2 / math.pi)
    square = v * v
    t = jnp.tanh(c * v * (1.0 + 0.044715 * square))
    half = 0.5 * (1.0 + t)
    slope = half + (0.5 * v) * (1.0 - t * t) * (c * (1.0 + 3 * 0.044715 * square))
    return v * half, slope


def ffn_kernel(tile, x_ref, g_ref, wg_ref, wu_ref, wd_ref, h_ref, dg_ref, du_ref, branch_ref, dx_ref, branch, dx):
    u = pl.program_id(0)
    x = x_ref[...]
    gate = dot(x, wg_ref[...])
    up = dot(x, wu_ref[...])
    grad_hidden = dot(g_ref[...], wd_ref[...])
    act, slope = gelu_parts(gate)
    hidden = (act * up).astype(jnp.bfloat16)
    dgate = (slope * (grad_hidden * up)).astype(jnp.bfloat16)
    dup = (grad_hidden * act).astype(jnp.bfloat16)
    h_ref[...] = hidden
    dg_ref[...] = dgate
    du_ref[...] = dup
    b_add = dot_nt(hidden, wd_ref[...])
    d_add = dot_nt(dgate, wg_ref[...]) + dot_nt(dup, wu_ref[...])

    @pl.when(u == 0)
    def _():
        branch[...] = b_add
        dx[...] = d_add

    @pl.when(u > 0)
    def _():
        branch[...] += b_add
        dx[...] += d_add

    @pl.when(u == pl.num_programs(0) - 1)
    def _():
        branch_ref[...] = branch[...]
        dx_ref[...] = dx[...].astype(jnp.bfloat16)


def ffn_rows(x, g, weights, tile=256):
    rows, d = x.shape
    units = weights.shape[1] // 3
    n = units // tile
    full = pl.BlockSpec((rows, d), lambda u: (0, 0))
    cols = pl.BlockSpec((rows, tile), lambda u: (0, u))
    wide = jax.ShapeDtypeStruct((rows, units), jnp.bfloat16)
    narrow = jax.ShapeDtypeStruct((rows, d), jnp.bfloat16)
    return pl.pallas_call(
        functools.partial(ffn_kernel, tile),
        out_shape=(wide, wide, wide, jax.ShapeDtypeStruct((rows, d), jnp.float32), narrow),
        grid=(n,),
        in_specs=[
            full,
            full,
            pl.BlockSpec((d, tile), lambda u: (0, u)),
            pl.BlockSpec((d, tile), lambda u: (0, u + n)),
            pl.BlockSpec((d, tile), lambda u: (0, u + 2 * n)),
        ],
        out_specs=(cols, cols, cols, full, full),
        scratch_shapes=[pltpu.VMEM((rows, d), jnp.float32), pltpu.VMEM((rows, d), jnp.float32)],
        cost_estimate=pl.CostEstimate(
            flops=12 * rows * d * units,
            bytes_accessed=2 * (4 * rows * d + 3 * rows * units + 3 * d * units),
            transcendentals=rows * units,
        ),
        name="ffn_rows",
    )(x, g, weights, weights, weights)


def wgrad_kernel(parts, n, *refs):
    xs, gs, gates, ups, hiddens = [refs[parts * m : parts * (m + 1)] for m in range(5)]
    out, left_t = refs[-2:]
    i = pl.program_id(0)
    rows = xs[0].shape[0]

    def turn_all(lefts):
        for c in range(parts):
            def turn(s, carry, c=c):
                src = pl.ds(pl.multiple_of(s * SUB, SUB), SUB)
                at = pl.ds(pl.multiple_of(c * rows + s * SUB, SUB), SUB)
                left_t[:, at] = turned(lefts[c][src, :]).astype(jnp.bfloat16)
                return carry
            lax.fori_loop(0, rows // SUB, turn, 0)

    def product(rights):
        total = dot(left_t[:, :rows], rights[0][...])
        for c in range(1, parts):
            total += dot(left_t[:, c * rows : (c + 1) * rows], rights[c][...])
        out[...] = total.astype(jnp.bfloat16)

    @pl.when(i == 0)
    def _():
        turn_all(xs)

    @pl.when(i == 2 * n)
    def _():
        turn_all(gs)

    @pl.when(i < n)
    def _():
        product(gates)

    @pl.when((i >= n) & (i < 2 * n))
    def _():
        product(ups)

    @pl.when(i >= 2 * n)
    def _():
        product(hiddens)


def wgrad(xs, gs, gates, ups, hiddens, tile=256):
    parts = len(xs)
    rows, d = xs[0].shape
    units = gates[0].shape[1]
    n = units // tile

    def tiles(m):
        return [pl.BlockSpec((rows, tile), lambda i: (0, jnp.clip(i - m * n, 0, n - 1)))] * parts

    return pl.pallas_call(
        functools.partial(wgrad_kernel, parts, n),
        out_shape=jax.ShapeDtypeStruct((d, 3 * units), jnp.bfloat16),
        grid=(3 * n,),
        in_specs=[pl.BlockSpec((rows, d), lambda i: (0, 0))] * (2 * parts) + tiles(0) + tiles(1) + tiles(2),
        out_specs=pl.BlockSpec((d, tile), lambda i: (0, i)),
        scratch_shapes=[pltpu.VMEM((d, parts * rows), jnp.bfloat16)],
        cost_estimate=pl.CostEstimate(
            flops=6 * parts * rows * d * units,
            bytes_accessed=2 * parts * rows * (2 * d + 3 * units) + 6 * d * units,
            transcendentals=0,
        ),
        name="wgrad",
    )(*xs, *gs, *gates, *ups, *hiddens)


def rms_norm(features, norm_gain):
    return features * lax.rsqrt(jnp.mean(features * features, axis=-1, keepdims=True) + EPS) * norm_gain


def norm_back(v, gain, e):
    rate = lax.rsqrt(jnp.mean(v * v, axis=-1, keepdims=True) + EPS)
    scaled = gain * e
    dot_mean = jnp.mean(scaled * v, axis=-1, keepdims=True)
    return rate * scaled - v * (rate * rate * rate * dot_mean), jnp.sum(e * v * rate, axis=0, keepdims=True)


def middle_kernel(parts, share, came, got, middle, top, gain, *refs):
    weights = refs[:parts]
    grad_ref, low_ref = refs[parts : parts + 2]
    heads = refs[parts + 2 : 2 * parts + 2]
    gain_ref = refs[-1]
    f32 = jnp.float32
    e = share[...].astype(f32) + came[...].astype(f32) + got[...].astype(f32)
    grad, part = norm_back(middle[...], gain[...], e)
    grad = top[...] + grad
    grad_ref[...] = grad
    low = grad.astype(jnp.bfloat16)
    low_ref[...] = low
    for c in range(parts):
        heads[c][...] = dot(low, weights[c][...]).astype(jnp.bfloat16)

    @pl.when(pl.program_id(0) == 0)
    def _():
        gain_ref[...] = part

    @pl.when(pl.program_id(0) > 0)
    def _():
        gain_ref[...] += part


def middle_back(share, came, got, middle, top, gain, weights, block=160):
    rows, d = middle.shape
    feats = weights[0].shape[1]
    parts = len(weights)
    row = pl.BlockSpec((block, d), lambda i: (i, 0))
    one = pl.BlockSpec((1, d), lambda i: (0, 0))
    outs = pl.pallas_call(
        functools.partial(middle_kernel, parts),
        out_shape=(
            jax.ShapeDtypeStruct((rows, d), jnp.float32),
            jax.ShapeDtypeStruct((rows, d), jnp.bfloat16),
            *[jax.ShapeDtypeStruct((rows, feats), jnp.bfloat16)] * parts,
            jax.ShapeDtypeStruct((1, d), jnp.float32),
        ),
        grid=(rows // block,),
        in_specs=[row] * 5 + [one] + [pl.BlockSpec((d, feats), lambda i: (0, 0))] * parts,
        out_specs=(row, row, *[pl.BlockSpec((block, feats), lambda i: (i, 0))] * parts, one),
        cost_estimate=pl.CostEstimate(
            flops=2 * rows * d * feats * parts, bytes_accessed=22 * rows * d, transcendentals=rows
        ),
        name="middle_back",
    )(share, came, got, middle, top, gain[None], *weights)
    return outs[0], outs[1], list(outs[2 : 2 + parts]), outs[-1]


def input_kernel(share, came, got_a, got_b, inputs, cot, grad_middle, early, gain, mix, correct, out, sums):
    i = pl.program_id(0)
    f32 = jnp.float32
    d = gain.shape[1]
    got = jnp.where(i < pl.num_programs(0) // 2, got_a[...].astype(f32), got_b[...].astype(f32))
    e = share[...].astype(f32) + came[...].astype(f32) + got
    one, two = inputs[:, :d].astype(f32), inputs[:, d:].astype(f32)
    cot_one, cot_two = cot[:, :d].astype(f32), cot[:, d:].astype(f32)
    grad, part = norm_back(mix[0, 0] * one + mix[0, 1] * two, gain[...], e)
    main = cot_one + grad_middle[...] + grad - (correct[0] * cot_one + correct[1] * cot_two)
    out[:, :d] = mix[0, 0] * main + mix[1, 0] * cot_two
    out[:, d:] = mix[0, 1] * main + mix[1, 1] * cot_two

    @pl.when(i == 0)
    def _():
        sums[...] = early[...]

    sums[0:1] += part
    for r, value in enumerate((main * one, main * two, cot_two * one, cot_two * two)):
        sums[r + 1 : r + 2] += jnp.sum(value, axis=0, keepdims=True)


def input_back(share, came, got, inputs, cot, grad_middle, early, gain, mix, correct, block=160):
    rows, d = grad_middle.shape
    half = rows // block // 2
    row = pl.BlockSpec((block, d), lambda i: (i, 0))
    wide = pl.BlockSpec((block, 2 * d), lambda i: (i, 0))
    sums = pl.BlockSpec((8, d), lambda i: (0, 0))
    small = pl.BlockSpec(memory_space=pltpu.SMEM)
    return pl.pallas_call(
        input_kernel,
        out_shape=(jax.ShapeDtypeStruct((rows, 2 * d), jnp.float32), jax.ShapeDtypeStruct((8, d), jnp.float32)),
        grid=(2 * half,),
        in_specs=[
            row,
            row,
            pl.BlockSpec((block, d), lambda i: (jnp.minimum(i, half - 1), 0)),
            pl.BlockSpec((block, d), lambda i: (jnp.maximum(i - half, 0), 0)),
            wide,
            wide,
            row,
            sums,
            pl.BlockSpec((1, d), lambda i: (0, 0)),
            small,
            small,
        ],
        out_specs=(wide, sums),
        cost_estimate=pl.CostEstimate(flops=60 * rows * d, bytes_accessed=30 * rows * d, transcendentals=rows),
        name="input_back",
    )(share, came, *got, inputs, cot, grad_middle, early, gain[None], mix, correct)


def swap(array, bit):
    count = lax.axis_size("tensor")
    return lax.ppermute(array, "tensor", [(i, i ^ bit) for i in range(count)])


def after(value, *others):
    return lax.optimization_barrier((value, *others))[0]


def flipped(index, bits):
    bit = 1
    while bit <= bits:
        if bits & bit:
            index = index + bit - 2 * bit * lax.rem(lax.div(index, bit), 2)
        bit *= 2
    return index


def start_kernel(
    count, chunks, x, qkv, wo, sib, far, diag, qkv_all, wo_all,
    local_sem, sib_sem, far_send, far_recv, diag_send, diag_recv, qkv_dp, wo_dp,
):
    t = lax.axis_index("tensor")
    g = lax.axis_index("dp")
    order = []
    bit = 2
    while bit < count:
        order.append(bit)
        bit *= 2
    order.append(1)

    def last(e):
        return max(k for k, b in enumerate(order) if e & b)

    barrier = pltpu.get_barrier_semaphore()
    for c in (1, 2):
        pl.semaphore_signal(barrier, inc=1, device_id={"tensor": flipped(t, c)}, device_id_type=MESH)
    for b in order:
        pl.semaphore_signal(barrier, inc=1, device_id={"dp": flipped(g, b)}, device_id_type=MESH)
    pl.semaphore_wait(barrier, 2 + len(order))

    size = x.shape[0] // chunks

    def far_copy(k):
        rows = pl.ds(k * size, size)
        return pltpu.make_async_remote_copy(
            x.at[rows], far.at[rows], far_send.at[k], far_recv.at[k], {"tensor": flipped(t, 2)}, MESH
        )

    def diag_copy(k):
        rows = pl.ds(k * size, size)
        return pltpu.make_async_remote_copy(
            far.at[rows], diag.at[rows], diag_send.at[k], diag_recv.at[k], {"tensor": flipped(t, 1)}, MESH
        )

    def dp_copy(which, e):
        own, whole, sems = ((qkv, qkv_all, qkv_dp), (wo, wo_all, wo_dp))[which]
        b = order[last(e)]
        block = flipped(g, e ^ b)
        return pltpu.make_async_remote_copy(
            own if e == b else whole.at[block],
            whole.at[block],
            sems.at[0, e - 1],
            sems.at[1, e - 1],
            {"dp": flipped(g, b)},
            MESH,
        )

    def dp_arrival(which, e):
        whole, sems = ((qkv_all, qkv_dp), (wo_all, wo_dp))[which]
        dst = whole.at[flipped(g, e)]
        return pltpu.make_async_remote_copy(
            dst, dst, sems.at[0, e - 1], sems.at[1, e - 1], {"dp": flipped(g, order[last(e)])}, MESH
        )

    sends = []

    def go(copy):
        copy.start()
        sends.append(copy)

    for b in order:
        go(dp_copy(0, b))
    fars = [far_copy(k) for k in range(chunks)]
    for copy in fars:
        go(copy)
    near = pltpu.make_async_remote_copy(
        x, sib, sib_sem.at[0], sib_sem.at[1], {"tensor": flipped(t, 1)}, MESH
    )
    go(near)
    kept = [
        pltpu.make_async_copy(qkv, qkv_all.at[g], local_sem.at[0]),
        pltpu.make_async_copy(wo, wo_all.at[g], local_sem.at[1]),
    ]
    for copy in kept:
        copy.start()
    for b in order:
        go(dp_copy(1, b))
    diags = []

    def pass_on(k):
        fars[k].wait_recv()
        diags.append(diag_copy(k))
        go(diags[-1])

    done = 0
    for e in sorted(range(1, count), key=lambda e: (last(e), e)):
        for which in (0, 1):
            dp_arrival(which, e).wait_recv()
            for b in order[last(e) + 1 :]:
                go(dp_copy(which, e ^ b))
        if done < chunks and e & 1 == 0:
            pass_on(done)
            done += 1
    while done < chunks:
        pass_on(done)
        done += 1
    for copy in diags:
        copy.wait_recv()
    near.wait_recv()
    for copy in sends:
        copy.wait_send()
    for copy in kept:
        copy.wait()


def start(x, qkv, wo, chunks=4):
    count = lax.axis_size("dp")
    rows = jax.ShapeDtypeStruct(x.shape, x.dtype)
    dma = pltpu.SemaphoreType.DMA
    sib, far, diag, qkv_all, wo_all = pl.pallas_call(
        functools.partial(start_kernel, count, chunks),
        out_shape=(
            rows,
            rows,
            rows,
            jax.ShapeDtypeStruct((count, *qkv.shape), qkv.dtype),
            jax.ShapeDtypeStruct((count, *wo.shape), wo.dtype),
        ),
        in_specs=[pl.BlockSpec(memory_space=pl.ANY)] * 3,
        out_specs=(pl.BlockSpec(memory_space=pl.ANY),) * 5,
        scratch_shapes=[
            dma((2,)),
            dma((2,)),
            dma((chunks,)),
            dma((chunks,)),
            dma((chunks,)),
            dma((chunks,)),
            dma((2, count - 1)),
            dma((2, count - 1)),
        ],
        compiler_params=pltpu.CompilerParams(collective_id=0, has_side_effects=True),
        cost_estimate=pl.CostEstimate(flops=0, bytes_accessed=100_000_000, transcendentals=0),
        name="start",
    )(x, qkv, wo)
    whole = count * qkv.shape[0]
    return [x, sib, far, diag], qkv_all.reshape(whole, -1), wo_all.reshape(whole, -1)


def spread(rows):
    far = swap(rows, 2)
    return [rows, swap(rows, 1), far, swap(far, 1)]


def exchange(blocks):
    return [blocks[0]] + [swap(blocks[c], c) for c in range(1, len(blocks))]


def summed(shares, before=None, beside=None):
    f32 = jnp.float32
    far = (shares[2].astype(f32) + swap(shares[3], 1).astype(f32)).astype(jnp.bfloat16)
    if before is not None:
        far = after(far, before)
    got = swap(far, 2)
    near = shares[0].astype(f32) + swap(shares[1], 1).astype(f32)
    if beside is not None:
        got, beside = lax.optimization_barrier((got, beside(far)))
    return near + got.astype(f32), beside


def sum_everywhere(array):
    for axis in ("tensor", "dp"):
        count = lax.axis_size(axis)
        bit = 1
        while bit < count:
            array = array + lax.ppermute(array, axis, [(i, i ^ bit) for i in range(count)])
            bit *= 2
    return array


def local(
    block_input, seq_lengths, w_qkv, w_out, w_gate_up, w_down, gain_attn, gain_ffn, mix_matrix, correct_gain, cotangent
):
    f32, bf16 = jnp.float32, jnp.bfloat16
    width = gain_attn.shape[0]
    me = lax.axis_index("tensor").astype(jnp.int32)[None]
    shard = w_qkv.shape[0]
    feats = w_out.shape[1]
    inputs = block_input.astype(f32)
    stream_one = inputs[:, :width]
    stream_two = inputs[:, width:]
    predicted_main = mix_matrix[0, 0] * stream_one + mix_matrix[0, 1] * stream_two
    predicted_side = mix_matrix[1, 0] * stream_one + mix_matrix[1, 1] * stream_two
    units = w_down.shape[1]

    normed_attn, qkv_all, out_mine = start(
        rms_norm(predicted_main, gain_attn).astype(bf16),
        w_qkv.reshape(shard, 3 * feats).astype(bf16),
        w_out.astype(bf16),
    )
    ffn_mine = jnp.concatenate([w_gate_up.reshape(shard, -1), w_down], axis=1).astype(bf16)
    ffn_all = lax.all_gather(after(ffn_mine, normed_attn[1]), "dp", axis=0, tiled=True)
    proj = [dot(x, qkv_all).astype(bf16) for x in normed_attn]
    attended, heads_turned, log_total = attn_fwd(seq_lengths, me, proj)

    incoming = cotangent.astype(f32)
    cot_one = incoming[:, :width]
    cot_two = incoming[:, width:]
    grad_top = correct_gain[0] * cot_one + correct_gain[1] * cot_two
    grad_ffn = spread(after(grad_top.astype(bf16), normed_attn[1]))

    out_parts = [out_mine] + [swap(out_mine, c) for c in (1, 2, 3)]
    attended = after(attended, grad_ffn[2], out_parts[2], out_parts[3])
    head_parts = exchange([attended[c] for c in range(len(proj))])
    attn_branch = sum(dot_nt(a, w) for a, w in zip(head_parts, out_parts))
    middle = predicted_main + attn_branch

    normed_mine = rms_norm(middle, gain_ffn).astype(bf16)
    normed_ffn = [normed_mine, swap(normed_mine, 1), swap(normed_mine, 2)]
    pieces = [ffn_rows(x, g, ffn_all) for x, g in zip(normed_ffn, grad_ffn[:2])]
    normed_ffn[2] = after(normed_ffn[2], pieces[0][0], pieces[1][0])
    normed_ffn.append(swap(normed_ffn[2], 1))
    pieces += [ffn_rows(x, g, ffn_all) for x, g in zip(normed_ffn[2:], grad_ffn[2:])]
    hidden, dgate, dup, branch, dnormed = zip(*pieces)
    far = (dnormed[2].astype(f32) + swap(dnormed[3], 1).astype(f32)).astype(bf16)
    got = swap(far, 2)
    came = swap(dnormed[1], 1)
    weight_ffn = wgrad([after(normed_ffn[0], far)] + normed_ffn[1:], grad_ffn, dgate, dup, hidden)
    got, came, weight_ffn = lax.optimization_barrier((got, came, weight_ffn))
    weight_ffn = lax.psum_scatter(weight_ffn, "dp", scatter_dimension=0, tiled=True)
    grad_middle, grad_attn, grad_heads, grad_gain_ffn = middle_back(
        dnormed[0], came, got, middle, grad_top, gain_ffn, out_parts
    )
    grad_heads = exchange(grad_heads)
    grad_proj = attn_bwd(seq_lengths, me, proj, grad_heads, heads_turned, log_total)
    *late, later_attn = lax.optimization_barrier((*head_parts, grad_heads[2], grad_heads[3], grad_attn))
    out_shares = exchange([dot_tn(later_attn, a).astype(bf16) for a in late[:4]])
    weight_out = sum(s.astype(f32) for s in out_shares)
    ffn_branch, (grad_proj, weight_out) = summed(branch, before=late[4], beside=lambda far: (grad_proj, weight_out))
    grad_proj = [grad_proj[c] for c in range(len(proj))]

    correction = (middle + ffn_branch) - predicted_main
    block_output = jnp.concatenate(
        [predicted_main + correct_gain[0] * correction, predicted_side + correct_gain[1] * correction], axis=1
    ).astype(bf16)
    early = jnp.concatenate(
        [
            jnp.zeros((5, width), f32),
            grad_gain_ffn,
            jnp.sum(cot_one * correction, axis=0, keepdims=True),
            jnp.sum(cot_two * correction, axis=0, keepdims=True),
        ],
        axis=0,
    )

    far = [dot_nt(g, qkv_all).astype(bf16) for g in grad_proj[2:]]
    far = (far[0].astype(f32) + swap(far[1], 1).astype(f32)).astype(bf16)
    half = far.shape[0] // 2
    got = [swap(far[:half], 2), swap(far[half:], 2)]
    *late, far = lax.optimization_barrier((*grad_proj, *normed_attn, weight_out, far))
    near = [dot_nt(g, qkv_all).astype(bf16) for g in late[:2]]
    weight_qkv = sum(dot_tn(x, g) for x, g in zip(late[4:8], late[:4]))
    last = jnp.concatenate([weight_qkv, late[8]], axis=1).astype(bf16)
    last = last.reshape(lax.axis_size("dp"), shard, -1)
    last, weight_ffn, got[0] = lax.optimization_barrier((last, weight_ffn, got[0]))
    last = lax.all_to_all(last, "dp", split_axis=0, concat_axis=0, tiled=True)
    came = swap(near[1], 1)
    got[1], last, came, early, block_output = lax.optimization_barrier((got[1], last, came, early, block_output))
    grad_input, small = input_back(
        near[0], came, got, block_input, cotangent, grad_middle, early, gain_attn, mix_matrix, correct_gain
    )
    weight_ffn = weight_ffn.astype(f32)
    sum_gate_up = weight_ffn[:, : 2 * units].reshape(shard, 2, units)
    sum_down = weight_ffn[:, 2 * units :]
    last = last.astype(f32).sum(axis=0)
    sum_qkv = last[:, : 3 * feats].reshape(shard, 3, feats)
    sum_out = last[:, 3 * feats :]

    small = sum_everywhere(small)
    return (
        block_output,
        grad_input,
        sum_qkv,
        sum_out,
        sum_gate_up,
        sum_down,
        small[0],
        small[5],
        small[1:5].sum(axis=1).reshape(2, 2),
        small[6:].sum(axis=1),
    )


def solution(mesh):
    placed = (
        P(("dp", "tensor"), None),
        P("dp", None),
        P("dp", None, "tensor"),
        P("dp", "tensor"),
        P("dp", None, "tensor"),
        P("dp", "tensor"),
        P(),
        P(),
        P(),
        P(),
        P(("dp", "tensor"), None),
    )
    return jax.shard_map(
        local,
        mesh=mesh,
        in_specs=placed,
        out_specs=(
            P(("dp", "tensor"), None),
            P(("dp", "tensor"), None),
            P("dp", None, "tensor"),
            P("dp", "tensor"),
            P("dp", None, "tensor"),
            P("dp", "tensor"),
            P(),
            P(),
            P(),
            P(),
        ),
        check_vma=False,
    )
```

```python
import functools
import math

import jax
import jax.numpy as jnp
from jax import lax
from jax.experimental import pallas as pl
from jax.experimental.pallas import tpu as pltpu
from jax.sharding import PartitionSpec as P

HEAD_DIM = 64
EPS = 1e-06
BIG = 1e30
BLK = 256
SUB = 128
MESH = pl.DeviceIdType.MESH


def dot(a, b):
    return jnp.dot(a, b, preferred_element_type=jnp.float32)


def dot_nt(a, b):
    return lax.dot_general(a, b, (((1,), (1,)), ((), ())), preferred_element_type=jnp.float32)


def dot_tn(a, b):
    return lax.dot_general(a, b, (((0,), (0,)), ((), ())), preferred_element_type=jnp.float32)


def turned(a):
    return a.astype(jnp.float32).T


def seg_vector(len_ref, pos):
    begin = jnp.zeros_like(pos)
    edge = jnp.int32(0)
    for k in range(len_ref.shape[1] - 1):
        edge = edge + len_ref[0, k]
        begin = jnp.where(pos >= edge, edge, begin)
    return begin


def seg_scalar(len_ref, row):
    begin = jnp.int32(0)
    end = jnp.int32(0)
    edge = jnp.int32(0)
    for k in range(len_ref.shape[1]):
        after = edge + len_ref[0, k]
        inside = (row >= edge) & (row < after)
        begin = jnp.where(inside, edge, begin)
        end = jnp.where(inside, after, end)
        edge = after
    return begin, end


def place(me, chunk, per):
    return (chunk // per) ^ me, pl.multiple_of((chunk % per) * SUB, SUB)


def fwd_kernel(heads, parts, len_ref, me_ref, *refs):
    proj = refs[:parts]
    o_ref, ot_ref, lse_ref, qt, kh, vt, acc, mx, tot = refs[parts:]
    i = pl.program_id(0)
    part_rows = proj[0].shape[0]
    per = part_rows // SUB
    blk, hd = BLK, HEAD_DIM
    feats = heads * hd
    me = me_ref[0]

    @pl.when(i == 0)
    def _():
        for c in range(parts):
            base = (me ^ c) * part_rows
            def turn(s, carry, c=c, base=base):
                src = pl.ds(pl.multiple_of(s * SUB, SUB), SUB)
                at = pl.ds(pl.multiple_of(base + s * SUB, SUB), SUB)
                rows = proj[c][src, :]
                qt[:, at] = (turned(rows[:, :feats]) * 0.125).astype(jnp.bfloat16)
                vt[:, at] = turned(rows[:, 2 * feats :]).astype(jnp.bfloat16)
                for h in range(heads):
                    kh[h, at, :] = rows[:, feats + h * hd : feats + (h + 1) * hd]
                return carry
            lax.fori_loop(0, per, turn, 0)

    first = pl.multiple_of(i * blk, blk)
    cols = pl.ds(first, blk)
    pos = first + lax.broadcasted_iota(jnp.int32, (1, blk), 1)
    begin = seg_vector(len_ref, pos)
    b_first, _ = seg_scalar(len_ref, first)
    b_last, _ = seg_scalar(len_ref, first + blk - 1)
    j_lo = b_first // blk
    j_full = jnp.minimum((b_last + blk - 1) // blk, i)
    mx[...] = jnp.full_like(mx, -BIG)
    tot[...] = jnp.zeros_like(tot)
    acc[...] = jnp.zeros_like(acc)

    def step(j, masked, first_pass):
        at = pl.ds(pl.multiple_of(j * blk, blk), blk)
        if masked:
            key = j * blk + lax.broadcasted_iota(jnp.int32, (blk, blk), 0)
            ok = (key >= begin) & (key <= pos)
        scores = []
        for h in range(heads):
            s = dot(kh[h, at, :], qt[h * hd : (h + 1) * hd, cols])
            scores.append(jnp.where(ok, s, -BIG) if masked else s)
        if first_pass:
            for h in range(heads):
                old = mx[h : h + 1]
                new = jnp.maximum(old, jnp.max(scores[h], axis=0, keepdims=True))
                total = jnp.sum(jnp.exp(scores[h] - new), axis=0, keepdims=True)
                mx[h : h + 1] = new
                tot[h : h + 1] = jnp.exp(old - new) * tot[h : h + 1] + total
        else:
            for h in range(heads):
                hs = slice(h * hd, (h + 1) * hd)
                p = jnp.exp(scores[h] - mx[h : h + 1])
                acc[hs] += dot(vt[hs, at], p.astype(jnp.bfloat16))

    def loop(lo, hi, masked, first_pass):
        def body(j, carry):
            step(j, masked, first_pass)
            return carry
        lax.fori_loop(lo, hi, body, 0)

    for first_pass in (True, False):
        loop(j_lo, j_full, True, first_pass)
        loop(jnp.maximum(j_full, j_lo), i, False, first_pass)
        step(i, True, first_pass)
        if first_pass:
            mx[...] = mx[...] + jnp.log(tot[...])
            lse_ref[...] = mx[...]
    ot_ref[...] = acc[...]
    out = acc[...].T.astype(jnp.bfloat16)
    for s in range(blk // SUB):
        c, row = place(me, i * (blk // SUB) + s, per)
        o_ref[c, pl.ds(row, SUB), :] = out[s * SUB : (s + 1) * SUB]


def attn_fwd(lengths, me, proj):
    parts = len(proj)
    part_rows, width = proj[0].shape
    feats = width // 3
    rows = parts * part_rows
    heads = feats // HEAD_DIM
    return pl.pallas_call(
        functools.partial(fwd_kernel, heads, parts),
        out_shape=(
            jax.ShapeDtypeStruct((parts, part_rows, feats), jnp.bfloat16),
            jax.ShapeDtypeStruct((feats, rows), jnp.float32),
            jax.ShapeDtypeStruct((8, rows), jnp.float32),
        ),
        grid_spec=pltpu.PrefetchScalarGridSpec(
            num_scalar_prefetch=2,
            grid=(rows // BLK,),
            in_specs=[pl.BlockSpec((part_rows, width), lambda i, s, m: (0, 0))] * parts,
            out_specs=(
                pl.BlockSpec((parts, part_rows, feats), lambda i, s, m: (0, 0, 0)),
                pl.BlockSpec((feats, BLK), lambda i, s, m: (0, i)),
                pl.BlockSpec((8, BLK), lambda i, s, m: (0, i)),
            ),
            scratch_shapes=[
                pltpu.VMEM((feats, rows), jnp.bfloat16),
                pltpu.VMEM((heads, rows, HEAD_DIM), jnp.bfloat16),
                pltpu.VMEM((feats, rows), jnp.bfloat16),
                pltpu.VMEM((feats, BLK), jnp.float32),
                pltpu.VMEM((8, BLK), jnp.float32),
                pltpu.VMEM((8, BLK), jnp.float32),
            ],
        ),
        cost_estimate=pl.CostEstimate(
            flops=rows * feats * 4096, bytes_accessed=12 * rows * feats, transcendentals=rows * 512 * heads
        ),
        name="attn_fwd",
    )(lengths, me, *proj)


def bwd_kernel(heads, parts, len_ref, me_ref, *refs):
    proj = refs[:parts]
    grads = refs[parts : 2 * parts]
    ot_ref, lse_ref, d_ref, qt, qp, gt, gp, kh, vh, kt, dqt, delta, dkv = refs[2 * parts :]
    j = pl.program_id(0)
    n = pl.num_programs(0)
    part_rows = proj[0].shape[0]
    per = part_rows // SUB
    blk, hd = BLK, HEAD_DIM
    feats = heads * hd
    me = me_ref[0]

    @pl.when(j == 0)
    def _():
        zero = jnp.zeros((SUB, hd), jnp.bfloat16)
        for c in range(parts):
            base = (me ^ c) * part_rows
            def turn(s, carry, c=c, base=base):
                src = pl.ds(pl.multiple_of(s * SUB, SUB), SUB)
                at = pl.ds(pl.multiple_of(base + s * SUB, SUB), SUB)
                rows = proj[c][src, :]
                g = grads[c][src, :]
                g_turned = turned(g)
                qt[:, at] = (turned(rows[:, :feats]) * 0.125).astype(jnp.bfloat16)
                kt[:, at] = turned(rows[:, feats : 2 * feats]).astype(jnp.bfloat16)
                gt[:, at] = g_turned.astype(jnp.bfloat16)
                prod = g_turned * ot_ref[:, at]
                dqt[:, at] = jnp.zeros((feats, SUB), jnp.float32)
                for h in range(heads):
                    hs = slice(h * hd, (h + 1) * hd)
                    delta[h : h + 1, at] = jnp.sum(prod[hs], axis=0, keepdims=True)
                    qp[h, at, :] = jnp.concatenate([rows[:, hs], zero], axis=1)
                    gp[h, at, :] = jnp.concatenate([zero, g[:, hs]], axis=1)
                    kh[h, at, :] = rows[:, feats + h * hd : feats + (h + 1) * hd]
                    vh[h, at, :] = rows[:, 2 * feats + h * hd : 2 * feats + (h + 1) * hd]
                return carry
            lax.fori_loop(0, per, turn, 0)

    first = pl.multiple_of(j * blk, blk)
    keys = pl.ds(first, blk)
    _, e_first = seg_scalar(len_ref, first)
    _, e_last = seg_scalar(len_ref, first + blk - 1)
    i_hi = (e_last - 1) // blk + 1
    i_full = jnp.clip(e_first // blk, j + 1, i_hi)
    key = first + lax.broadcasted_iota(jnp.int32, (blk, blk), 0)

    def step(i, masked, start):
        at = pl.ds(pl.multiple_of(i * blk, blk), blk)
        if masked:
            pos = i * blk + lax.broadcasted_iota(jnp.int32, (1, blk), 1)
            begin = seg_vector(len_ref, pos)
            ok = (key >= begin) & (key <= pos)
        scores, dprobs = [], []
        for h in range(heads):
            hs = slice(h * hd, (h + 1) * hd)
            scores.append(dot(kh[h, keys, :], qt[hs, at]))
            dprobs.append(dot(vh[h, keys, :], gt[hs, at]))
        both = []
        for h in range(heads):
            e = scores[h] - lse_ref[h : h + 1, at]
            if masked:
                e = jnp.where(ok, e, -BIG)
            p = jnp.exp(e)
            ds = p * (dprobs[h] - delta[h : h + 1, at])
            both.append((p.astype(jnp.bfloat16), ds.astype(jnp.bfloat16)))
        for h in range(heads):
            hs = slice(h * hd, (h + 1) * hd)
            p, ds = both[h]
            add = dot(
                jnp.concatenate([ds, p], axis=1),
                jnp.concatenate([qp[h, at, :], gp[h, at, :]], axis=0),
            )
            if start:
                dkv[h] = add
            else:
                dkv[h] += add
            dqt[hs, at] += dot(kt[hs, keys], ds)

    def loop(lo, hi, masked):
        def body(i, carry):
            step(i, masked, False)
            return carry
        lax.fori_loop(lo, hi, body, 0)

    step(j, True, True)
    loop(j + 1, i_full, False)
    loop(i_full, i_hi, True)
    pair = jnp.concatenate(
        [dkv[h][:, :hd] * 0.125 for h in range(heads)] + [dkv[h][:, hd:] for h in range(heads)], axis=1
    ).astype(jnp.bfloat16)
    for s in range(blk // SUB):
        c, row = place(me, j * (blk // SUB) + s, per)
        d_ref[c, pl.ds(row, SUB), feats:] = pair[s * SUB : (s + 1) * SUB]

    @pl.when(j == n - 1)
    def _():
        for c in range(parts):
            base = (me ^ c) * part_rows
            def turn(s, carry, c=c, base=base):
                at = pl.ds(pl.multiple_of(base + s * SUB, SUB), SUB)
                dst = pl.ds(pl.multiple_of(s * SUB, SUB), SUB)
                d_ref[c, dst, :feats] = (dqt[:, at] * 0.125).T.astype(jnp.bfloat16)
                return carry
            lax.fori_loop(0, per, turn, 0)


def attn_bwd(lengths, me, proj, grads, heads_turned, log_total):
    parts = len(proj)
    part_rows, width = proj[0].shape
    feats = width // 3
    rows = parts * part_rows
    heads = feats // HEAD_DIM
    return pl.pallas_call(
        functools.partial(bwd_kernel, heads, parts),
        out_shape=jax.ShapeDtypeStruct((parts, part_rows, width), jnp.bfloat16),
        grid_spec=pltpu.PrefetchScalarGridSpec(
            num_scalar_prefetch=2,
            grid=(rows // BLK,),
            in_specs=[pl.BlockSpec((part_rows, width), lambda i, s, m: (0, 0))] * parts
            + [pl.BlockSpec((part_rows, feats), lambda i, s, m: (0, 0))] * parts
            + [
                pl.BlockSpec((feats, rows), lambda i, s, m: (0, 0)),
                pl.BlockSpec((8, rows), lambda i, s, m: (0, 0)),
            ],
            out_specs=pl.BlockSpec((parts, part_rows, width), lambda i, s, m: (0, 0, 0)),
            scratch_shapes=[
                pltpu.VMEM((feats, rows), jnp.bfloat16),
                pltpu.VMEM((heads, rows, 2 * HEAD_DIM), jnp.bfloat16),
                pltpu.VMEM((feats, rows), jnp.bfloat16),
                pltpu.VMEM((heads, rows, 2 * HEAD_DIM), jnp.bfloat16),
                pltpu.VMEM((heads, rows, HEAD_DIM), jnp.bfloat16),
                pltpu.VMEM((heads, rows, HEAD_DIM), jnp.bfloat16),
                pltpu.VMEM((feats, rows), jnp.bfloat16),
                pltpu.VMEM((feats, rows), jnp.float32),
                pltpu.VMEM((8, rows), jnp.float32),
                pltpu.VMEM((heads, BLK, 2 * HEAD_DIM), jnp.float32),
            ],
        ),
        cost_estimate=pl.CostEstimate(
            flops=rows * feats * 10240, bytes_accessed=20 * rows * feats, transcendentals=rows * 512 * heads
        ),
        name="attn_bwd",
    )(lengths, me, *proj, *grads, heads_turned, log_total)


def gelu_parts(v):
    c = math.sqrt(2 / math.pi)
    square = v * v
    t = jnp.tanh(c * v * (1.0 + 0.044715 * square))
    half = 0.5 * (1.0 + t)
    slope = half + (0.5 * v) * (1.0 - t * t) * (c * (1.0 + 3 * 0.044715 * square))
    return v * half, slope


def ffn_kernel(tile, x_ref, g_ref, wg_ref, wu_ref, wd_ref, h_ref, dg_ref, du_ref, branch_ref, dx_ref, branch, dx):
    u = pl.program_id(0)
    x = x_ref[...]
    gate = dot(x, wg_ref[...])
    up = dot(x, wu_ref[...])
    grad_hidden = dot(g_ref[...], wd_ref[...])
    act, slope = gelu_parts(gate)
    hidden = (act * up).astype(jnp.bfloat16)
    dgate = (slope * (grad_hidden * up)).astype(jnp.bfloat16)
    dup = (grad_hidden * act).astype(jnp.bfloat16)
    h_ref[...] = hidden
    dg_ref[...] = dgate
    du_ref[...] = dup
    b_add = dot_nt(hidden, wd_ref[...])
    d_add = dot_nt(dgate, wg_ref[...]) + dot_nt(dup, wu_ref[...])

    @pl.when(u == 0)
    def _():
        branch[...] = b_add
        dx[...] = d_add

    @pl.when(u > 0)
    def _():
        branch[...] += b_add
        dx[...] += d_add

    @pl.when(u == pl.num_programs(0) - 1)
    def _():
        branch_ref[...] = branch[...]
        dx_ref[...] = dx[...].astype(jnp.bfloat16)


def ffn_rows(x, g, weights, tile=256):
    rows, d = x.shape
    units = weights.shape[1] // 3
    n = units // tile
    full = pl.BlockSpec((rows, d), lambda u: (0, 0))
    cols = pl.BlockSpec((rows, tile), lambda u: (0, u))
    wide = jax.ShapeDtypeStruct((rows, units), jnp.bfloat16)
    narrow = jax.ShapeDtypeStruct((rows, d), jnp.bfloat16)
    return pl.pallas_call(
        functools.partial(ffn_kernel, tile),
        out_shape=(wide, wide, wide, jax.ShapeDtypeStruct((rows, d), jnp.float32), narrow),
        grid=(n,),
        in_specs=[
            full,
            full,
            pl.BlockSpec((d, tile), lambda u: (0, u)),
            pl.BlockSpec((d, tile), lambda u: (0, u + n)),
            pl.BlockSpec((d, tile), lambda u: (0, u + 2 * n)),
        ],
        out_specs=(cols, cols, cols, full, full),
        scratch_shapes=[pltpu.VMEM((rows, d), jnp.float32), pltpu.VMEM((rows, d), jnp.float32)],
        cost_estimate=pl.CostEstimate(
            flops=12 * rows * d * units,
            bytes_accessed=2 * (4 * rows * d + 3 * rows * units + 3 * d * units),
            transcendentals=rows * units,
        ),
        name="ffn_rows",
    )(x, g, weights, weights, weights)


def wgrad_kernel(parts, n, *refs):
    xs, gs, gates, ups, hiddens = [refs[parts * m : parts * (m + 1)] for m in range(5)]
    out, left_t = refs[-2:]
    i = pl.program_id(0)
    rows = xs[0].shape[0]

    def turn_all(lefts):
        for c in range(parts):
            def turn(s, carry, c=c):
                src = pl.ds(pl.multiple_of(s * SUB, SUB), SUB)
                at = pl.ds(pl.multiple_of(c * rows + s * SUB, SUB), SUB)
                left_t[:, at] = turned(lefts[c][src, :]).astype(jnp.bfloat16)
                return carry
            lax.fori_loop(0, rows // SUB, turn, 0)

    def product(rights):
        total = dot(left_t[:, :rows], rights[0][...])
        for c in range(1, parts):
            total += dot(left_t[:, c * rows : (c + 1) * rows], rights[c][...])
        out[...] = total.astype(jnp.bfloat16)

    @pl.when(i == 0)
    def _():
        turn_all(xs)

    @pl.when(i == 2 * n)
    def _():
        turn_all(gs)

    @pl.when(i < n)
    def _():
        product(gates)

    @pl.when((i >= n) & (i < 2 * n))
    def _():
        product(ups)

    @pl.when(i >= 2 * n)
    def _():
        product(hiddens)


def wgrad(xs, gs, gates, ups, hiddens, tile=256):
    parts = len(xs)
    rows, d = xs[0].shape
    units = gates[0].shape[1]
    n = units // tile

    def tiles(m):
        return [pl.BlockSpec((rows, tile), lambda i: (0, jnp.clip(i - m * n, 0, n - 1)))] * parts

    return pl.pallas_call(
        functools.partial(wgrad_kernel, parts, n),
        out_shape=jax.ShapeDtypeStruct((d, 3 * units), jnp.bfloat16),
        grid=(3 * n,),
        in_specs=[pl.BlockSpec((rows, d), lambda i: (0, 0))] * (2 * parts) + tiles(0) + tiles(1) + tiles(2),
        out_specs=pl.BlockSpec((d, tile), lambda i: (0, i)),
        scratch_shapes=[pltpu.VMEM((d, parts * rows), jnp.bfloat16)],
        cost_estimate=pl.CostEstimate(
            flops=6 * parts * rows * d * units,
            bytes_accessed=2 * parts * rows * (2 * d + 3 * units) + 6 * d * units,
            transcendentals=0,
        ),
        name="wgrad",
    )(*xs, *gs, *gates, *ups, *hiddens)


def rms_norm(features, norm_gain):
    return features * lax.rsqrt(jnp.mean(features * features, axis=-1, keepdims=True) + EPS) * norm_gain


def norm_back(v, gain, e):
    rate = lax.rsqrt(jnp.mean(v * v, axis=-1, keepdims=True) + EPS)
    scaled = gain * e
    dot_mean = jnp.mean(scaled * v, axis=-1, keepdims=True)
    return rate * scaled - v * (rate * rate * rate * dot_mean), jnp.sum(e * v * rate, axis=0, keepdims=True)


def middle_kernel(parts, share, came, got, middle, top, gain, *refs):
    weights = refs[:parts]
    grad_ref, low_ref = refs[parts : parts + 2]
    heads = refs[parts + 2 : 2 * parts + 2]
    gain_ref = refs[-1]
    f32 = jnp.float32
    e = share[...].astype(f32) + came[...].astype(f32) + got[...].astype(f32)
    grad, part = norm_back(middle[...], gain[...], e)
    grad = top[...] + grad
    grad_ref[...] = grad
    low = grad.astype(jnp.bfloat16)
    low_ref[...] = low
    for c in range(parts):
        heads[c][...] = dot(low, weights[c][...]).astype(jnp.bfloat16)

    @pl.when(pl.program_id(0) == 0)
    def _():
        gain_ref[...] = part

    @pl.when(pl.program_id(0) > 0)
    def _():
        gain_ref[...] += part


def middle_back(share, came, got, middle, top, gain, weights, block=160):
    rows, d = middle.shape
    feats = weights[0].shape[1]
    parts = len(weights)
    row = pl.BlockSpec((block, d), lambda i: (i, 0))
    one = pl.BlockSpec((1, d), lambda i: (0, 0))
    outs = pl.pallas_call(
        functools.partial(middle_kernel, parts),
        out_shape=(
            jax.ShapeDtypeStruct((rows, d), jnp.float32),
            jax.ShapeDtypeStruct((rows, d), jnp.bfloat16),
            *[jax.ShapeDtypeStruct((rows, feats), jnp.bfloat16)] * parts,
            jax.ShapeDtypeStruct((1, d), jnp.float32),
        ),
        grid=(rows // block,),
        in_specs=[row] * 5 + [one] + [pl.BlockSpec((d, feats), lambda i: (0, 0))] * parts,
        out_specs=(row, row, *[pl.BlockSpec((block, feats), lambda i: (i, 0))] * parts, one),
        cost_estimate=pl.CostEstimate(
            flops=2 * rows * d * feats * parts, bytes_accessed=22 * rows * d, transcendentals=rows
        ),
        name="middle_back",
    )(share, came, got, middle, top, gain[None], *weights)
    return outs[0], outs[1], list(outs[2 : 2 + parts]), outs[-1]


def input_kernel(share, came, got_a, got_b, inputs, cot, grad_middle, early, gain, mix, correct, out, sums):
    i = pl.program_id(0)
    f32 = jnp.float32
    d = gain.shape[1]
    got = jnp.where(i < pl.num_programs(0) // 2, got_a[...].astype(f32), got_b[...].astype(f32))
    e = share[...].astype(f32) + came[...].astype(f32) + got
    one, two = inputs[:, :d].astype(f32), inputs[:, d:].astype(f32)
    cot_one, cot_two = cot[:, :d].astype(f32), cot[:, d:].astype(f32)
    grad, part = norm_back(mix[0, 0] * one + mix[0, 1] * two, gain[...], e)
    main = cot_one + grad_middle[...] + grad - (correct[0] * cot_one + correct[1] * cot_two)
    out[:, :d] = mix[0, 0] * main + mix[1, 0] * cot_two
    out[:, d:] = mix[0, 1] * main + mix[1, 1] * cot_two

    @pl.when(i == 0)
    def _():
        sums[...] = early[...]

    sums[0:1] += part
    for r, value in enumerate((main * one, main * two, cot_two * one, cot_two * two)):
        sums[r + 1 : r + 2] += jnp.sum(value, axis=0, keepdims=True)


def input_back(share, came, got, inputs, cot, grad_middle, early, gain, mix, correct, block=160):
    rows, d = grad_middle.shape
    half = rows // block // 2
    row = pl.BlockSpec((block, d), lambda i: (i, 0))
    wide = pl.BlockSpec((block, 2 * d), lambda i: (i, 0))
    sums = pl.BlockSpec((8, d), lambda i: (0, 0))
    small = pl.BlockSpec(memory_space=pltpu.SMEM)
    return pl.pallas_call(
        input_kernel,
        out_shape=(jax.ShapeDtypeStruct((rows, 2 * d), jnp.float32), jax.ShapeDtypeStruct((8, d), jnp.float32)),
        grid=(2 * half,),
        in_specs=[
            row,
            row,
            pl.BlockSpec((block, d), lambda i: (jnp.minimum(i, half - 1), 0)),
            pl.BlockSpec((block, d), lambda i: (jnp.maximum(i - half, 0), 0)),
            wide,
            wide,
            row,
            sums,
            pl.BlockSpec((1, d), lambda i: (0, 0)),
            small,
            small,
        ],
        out_specs=(wide, sums),
        cost_estimate=pl.CostEstimate(flops=60 * rows * d, bytes_accessed=30 * rows * d, transcendentals=rows),
        name="input_back",
    )(share, came, *got, inputs, cot, grad_middle, early, gain[None], mix, correct)


def swap(array, bit):
    count = lax.axis_size("tensor")
    return lax.ppermute(array, "tensor", [(i, i ^ bit) for i in range(count)])


def after(value, *others):
    return lax.optimization_barrier((value, *others))[0]


def flipped(index, bits):
    bit = 1
    while bit <= bits:
        if bits & bit:
            index = index + bit - 2 * bit * lax.rem(lax.div(index, bit), 2)
        bit *= 2
    return index


def start_kernel(
    count, chunks, x, qkv, wo, sib, far, diag, qkv_all, wo_all,
    local_sem, sib_sem, far_send, far_recv, diag_send, diag_recv, qkv_dp, wo_dp,
):
    t = lax.axis_index("tensor")
    g = lax.axis_index("dp")
    order = []
    bit = 2
    while bit < count:
        order.append(bit)
        bit *= 2
    order.append(1)

    def last(e):
        return max(k for k, b in enumerate(order) if e & b)

    barrier = pltpu.get_barrier_semaphore()
    for c in (1, 2):
        pl.semaphore_signal(barrier, inc=1, device_id={"tensor": flipped(t, c)}, device_id_type=MESH)
    for b in order:
        pl.semaphore_signal(barrier, inc=1, device_id={"dp": flipped(g, b)}, device_id_type=MESH)
    pl.semaphore_wait(barrier, 2 + len(order))

    size = x.shape[0] // chunks

    def far_copy(k):
        rows = pl.ds(k * size, size)
        return pltpu.make_async_remote_copy(
            x.at[rows], far.at[rows], far_send.at[k], far_recv.at[k], {"tensor": flipped(t, 2)}, MESH
        )

    def diag_copy(k):
        rows = pl.ds(k * size, size)
        return pltpu.make_async_remote_copy(
            far.at[rows], diag.at[rows], diag_send.at[k], diag_recv.at[k], {"tensor": flipped(t, 1)}, MESH
        )

    def dp_copy(which, e):
        own, whole, sems = ((qkv, qkv_all, qkv_dp), (wo, wo_all, wo_dp))[which]
        b = order[last(e)]
        block = flipped(g, e ^ b)
        return pltpu.make_async_remote_copy(
            own if e == b else whole.at[block],
            whole.at[block],
            sems.at[0, e - 1],
            sems.at[1, e - 1],
            {"dp": flipped(g, b)},
            MESH,
        )

    def dp_arrival(which, e):
        whole, sems = ((qkv_all, qkv_dp), (wo_all, wo_dp))[which]
        dst = whole.at[flipped(g, e)]
        return pltpu.make_async_remote_copy(
            dst, dst, sems.at[0, e - 1], sems.at[1, e - 1], {"dp": flipped(g, order[last(e)])}, MESH
        )

    sends = []

    def go(copy):
        copy.start()
        sends.append(copy)

    for b in order:
        go(dp_copy(0, b))
    fars = [far_copy(k) for k in range(chunks)]
    for copy in fars:
        go(copy)
    near = pltpu.make_async_remote_copy(
        x, sib, sib_sem.at[0], sib_sem.at[1], {"tensor": flipped(t, 1)}, MESH
    )
    go(near)
    kept = [
        pltpu.make_async_copy(qkv, qkv_all.at[g], local_sem.at[0]),
        pltpu.make_async_copy(wo, wo_all.at[g], local_sem.at[1]),
    ]
    for copy in kept:
        copy.start()
    for b in order:
        go(dp_copy(1, b))
    diags = []

    def pass_on(k):
        fars[k].wait_recv()
        diags.append(diag_copy(k))
        go(diags[-1])

    done = 0
    for e in sorted(range(1, count), key=lambda e: (last(e), e)):
        for which in (0, 1):
            dp_arrival(which, e).wait_recv()
            for b in order[last(e) + 1 :]:
                go(dp_copy(which, e ^ b))
        if done < chunks and e & 1 == 0:
            pass_on(done)
            done += 1
    while done < chunks:
        pass_on(done)
        done += 1
    for copy in diags:
        copy.wait_recv()
    near.wait_recv()
    for copy in sends:
        copy.wait_send()
    for copy in kept:
        copy.wait()


def start(x, qkv, wo, chunks=4):
    count = lax.axis_size("dp")
    rows = jax.ShapeDtypeStruct(x.shape, x.dtype)
    dma = pltpu.SemaphoreType.DMA
    sib, far, diag, qkv_all, wo_all = pl.pallas_call(
        functools.partial(start_kernel, count, chunks),
        out_shape=(
            rows,
            rows,
            rows,
            jax.ShapeDtypeStruct((count, *qkv.shape), qkv.dtype),
            jax.ShapeDtypeStruct((count, *wo.shape), wo.dtype),
        ),
        in_specs=[pl.BlockSpec(memory_space=pl.ANY)] * 3,
        out_specs=(pl.BlockSpec(memory_space=pl.ANY),) * 5,
        scratch_shapes=[
            dma((2,)),
            dma((2,)),
            dma((chunks,)),
            dma((chunks,)),
            dma((chunks,)),
            dma((chunks,)),
            dma((2, count - 1)),
            dma((2, count - 1)),
        ],
        compiler_params=pltpu.CompilerParams(collective_id=0, has_side_effects=True),
        cost_estimate=pl.CostEstimate(flops=0, bytes_accessed=100_000_000, transcendentals=0),
        name="start",
    )(x, qkv, wo)
    whole = count * qkv.shape[0]
    return [x, sib, far, diag], qkv_all.reshape(whole, -1), wo_all.reshape(whole, -1)


def spread(rows):
    far = swap(rows, 2)
    return [rows, swap(rows, 1), far, swap(far, 1)]


def exchange(blocks):
    return [blocks[0]] + [swap(blocks[c], c) for c in range(1, len(blocks))]


def summed(shares, before=None, beside=None):
    f32 = jnp.float32
    far = (shares[2].astype(f32) + swap(shares[3], 1).astype(f32)).astype(jnp.bfloat16)
    if before is not None:
        far = after(far, before)
    got = swap(far, 2)
    near = shares[0].astype(f32) + swap(shares[1], 1).astype(f32)
    if beside is not None:
        got, beside = lax.optimization_barrier((got, beside(far)))
    return near + got.astype(f32), beside


def end_kernel(count, blocks, mine, out, total, own, inbox, near, mid, far, own_sem, in_sem, near_sem, far_sem):
    t = lax.axis_index("tensor")
    g = lax.axis_index("dp")
    f32 = jnp.float32
    barrier = pltpu.get_barrier_semaphore()
    for c in (1, 2, 3):
        pl.semaphore_signal(barrier, inc=1, device_id={"tensor": flipped(t, c)}, device_id_type=MESH)
    for e in range(1, count):
        pl.semaphore_signal(barrier, inc=1, device_id={"dp": flipped(g, e)}, device_id_type=MESH)
    pl.semaphore_wait(barrier, 2 + count)

    nears = [
        pltpu.make_async_remote_copy(
            mine, near.at[c - 1], near_sem.at[0, c - 1], near_sem.at[1, c - 1], {"tensor": flipped(t, c)}, MESH
        )
        for c in (1, 2, 3)
    ]
    ins = [
        pltpu.make_async_remote_copy(
            blocks.at[flipped(g, e)],
            inbox.at[e - 1],
            in_sem.at[0, e - 1],
            in_sem.at[1, e - 1],
            {"dp": flipped(g, e)},
            MESH,
        )
        for e in range(1, count)
    ]
    fars = [
        pltpu.make_async_remote_copy(
            mid, far.at[e - 1], far_sem.at[0, e - 1], far_sem.at[1, e - 1], {"dp": flipped(g, e)}, MESH
        )
        for e in range(1, count)
    ]
    kept = pltpu.make_async_copy(blocks.at[g], own, own_sem.at[0])
    for copy in nears:
        copy.start()
    for copy in nears:
        copy.wait_recv()
    mid[...] = (mine[...] + near[0]) + (near[1] + near[2])
    for copy in fars:
        copy.start()
    for copy in ins:
        copy.start()
    kept.start()
    for copy in fars:
        copy.wait_recv()
    level = [mid[...]] + [far[e] for e in range(count - 1)]
    while len(level) > 1:
        level = [level[k] + level[k + 1] for k in range(0, len(level), 2)]
    total[...] = level[0]
    kept.wait()
    out[...] = own[...].astype(f32)
    for e, copy in enumerate(ins):
        copy.wait_recv()
        out[...] += inbox[e].astype(f32)
    for copy in nears + fars + ins:
        copy.wait_send()


def end(blocks, mine):
    count, rows, cols = blocks.shape
    dma = pltpu.SemaphoreType.DMA
    vmem = pl.BlockSpec(memory_space=pltpu.VMEM)
    return pl.pallas_call(
        functools.partial(end_kernel, count),
        out_shape=(
            jax.ShapeDtypeStruct((rows, cols), jnp.float32),
            jax.ShapeDtypeStruct(mine.shape, jnp.float32),
        ),
        in_specs=[pl.BlockSpec(memory_space=pl.ANY), vmem],
        out_specs=(vmem, vmem),
        scratch_shapes=[
            pltpu.VMEM((rows, cols), blocks.dtype),
            pltpu.VMEM((count - 1, rows, cols), blocks.dtype),
            pltpu.VMEM((3, *mine.shape), jnp.float32),
            pltpu.VMEM(mine.shape, jnp.float32),
            pltpu.VMEM((count - 1, *mine.shape), jnp.float32),
            dma((1,)),
            dma((2, count - 1)),
            dma((2, 3)),
            dma((2, count - 1)),
        ],
        compiler_params=pltpu.CompilerParams(collective_id=1, has_side_effects=True),
        cost_estimate=pl.CostEstimate(flops=0, bytes_accessed=50_000_000, transcendentals=0),
        name="end",
    )(blocks, mine)


def local(
    block_input, seq_lengths, w_qkv, w_out, w_gate_up, w_down, gain_attn, gain_ffn, mix_matrix, correct_gain, cotangent
):
    f32, bf16 = jnp.float32, jnp.bfloat16
    width = gain_attn.shape[0]
    me = lax.axis_index("tensor").astype(jnp.int32)[None]
    shard = w_qkv.shape[0]
    feats = w_out.shape[1]
    inputs = block_input.astype(f32)
    stream_one = inputs[:, :width]
    stream_two = inputs[:, width:]
    predicted_main = mix_matrix[0, 0] * stream_one + mix_matrix[0, 1] * stream_two
    predicted_side = mix_matrix[1, 0] * stream_one + mix_matrix[1, 1] * stream_two
    units = w_down.shape[1]

    normed_attn, qkv_all, out_mine = start(
        rms_norm(predicted_main, gain_attn).astype(bf16),
        w_qkv.reshape(shard, 3 * feats).astype(bf16),
        w_out.astype(bf16),
    )
    ffn_mine = jnp.concatenate([w_gate_up.reshape(shard, -1), w_down], axis=1).astype(bf16)
    ffn_all = lax.all_gather(after(ffn_mine, normed_attn[1]), "dp", axis=0, tiled=True)
    proj = [dot(x, qkv_all).astype(bf16) for x in normed_attn]
    attended, heads_turned, log_total = attn_fwd(seq_lengths, me, proj)

    incoming = cotangent.astype(f32)
    cot_one = incoming[:, :width]
    cot_two = incoming[:, width:]
    grad_top = correct_gain[0] * cot_one + correct_gain[1] * cot_two
    grad_ffn = spread(after(grad_top.astype(bf16), normed_attn[1]))

    out_parts = [out_mine] + [swap(out_mine, c) for c in (1, 2, 3)]
    attended = after(attended, grad_ffn[2], out_parts[2], out_parts[3])
    head_parts = exchange([attended[c] for c in range(len(proj))])
    attn_branch = sum(dot_nt(a, w) for a, w in zip(head_parts, out_parts))
    middle = predicted_main + attn_branch

    normed_mine = rms_norm(middle, gain_ffn).astype(bf16)
    normed_ffn = [normed_mine, swap(normed_mine, 1), swap(normed_mine, 2)]
    pieces = [ffn_rows(x, g, ffn_all) for x, g in zip(normed_ffn, grad_ffn[:2])]
    normed_ffn[2] = after(normed_ffn[2], pieces[0][0], pieces[1][0])
    normed_ffn.append(swap(normed_ffn[2], 1))
    pieces += [ffn_rows(x, g, ffn_all) for x, g in zip(normed_ffn[2:], grad_ffn[2:])]
    hidden, dgate, dup, branch, dnormed = zip(*pieces)
    far = (dnormed[2].astype(f32) + swap(dnormed[3], 1).astype(f32)).astype(bf16)
    got = swap(far, 2)
    came = swap(dnormed[1], 1)
    weight_ffn = wgrad([after(normed_ffn[0], far)] + normed_ffn[1:], grad_ffn, dgate, dup, hidden)
    got, came, weight_ffn = lax.optimization_barrier((got, came, weight_ffn))
    weight_ffn = lax.psum_scatter(weight_ffn, "dp", scatter_dimension=0, tiled=True)
    grad_middle, grad_attn, grad_heads, grad_gain_ffn = middle_back(
        dnormed[0], came, got, middle, grad_top, gain_ffn, out_parts
    )
    grad_heads = exchange(grad_heads)
    grad_proj = attn_bwd(seq_lengths, me, proj, grad_heads, heads_turned, log_total)
    *late, later_attn = lax.optimization_barrier((*head_parts, grad_heads[2], grad_heads[3], grad_attn))
    out_shares = exchange([dot_tn(later_attn, a).astype(bf16) for a in late[:4]])
    weight_out = sum(s.astype(f32) for s in out_shares)
    ffn_branch, (grad_proj, weight_out) = summed(branch, before=late[4], beside=lambda far: (grad_proj, weight_out))
    grad_proj = [grad_proj[c] for c in range(len(proj))]

    correction = (middle + ffn_branch) - predicted_main
    block_output = jnp.concatenate(
        [predicted_main + correct_gain[0] * correction, predicted_side + correct_gain[1] * correction], axis=1
    ).astype(bf16)
    early = jnp.concatenate(
        [
            jnp.zeros((5, width), f32),
            grad_gain_ffn,
            jnp.sum(cot_one * correction, axis=0, keepdims=True),
            jnp.sum(cot_two * correction, axis=0, keepdims=True),
        ],
        axis=0,
    )

    far = [dot_nt(g, qkv_all).astype(bf16) for g in grad_proj[2:]]
    far = (far[0].astype(f32) + swap(far[1], 1).astype(f32)).astype(bf16)
    half = far.shape[0] // 2
    got = [swap(far[:half], 2), swap(far[half:], 2)]
    *late, far = lax.optimization_barrier((*grad_proj, *normed_attn, weight_out, far))
    near = [dot_nt(g, qkv_all).astype(bf16) for g in late[:2]]
    weight_qkv = sum(dot_tn(x, g) for x, g in zip(late[4:8], late[:4]))
    last = jnp.concatenate([weight_qkv, late[8]], axis=1).astype(bf16)
    last = last.reshape(lax.axis_size("dp"), shard, -1)
    last, weight_ffn, got[0] = lax.optimization_barrier((last, weight_ffn, got[0]))
    came = swap(near[1], 1)
    got[1], last, came, early, block_output = lax.optimization_barrier((got[1], last, came, early, block_output))
    grad_input, small = input_back(
        near[0], came, got, block_input, cotangent, grad_middle, early, gain_attn, mix_matrix, correct_gain
    )
    weight_ffn = weight_ffn.astype(f32)
    sum_gate_up = weight_ffn[:, : 2 * units].reshape(shard, 2, units)
    sum_down = weight_ffn[:, 2 * units :]
    last, small = end(last, small)
    sum_qkv = last[:, : 3 * feats].reshape(shard, 3, feats)
    sum_out = last[:, 3 * feats :]
    return (
        block_output,
        grad_input,
        sum_qkv,
        sum_out,
        sum_gate_up,
        sum_down,
        small[0],
        small[5],
        small[1:5].sum(axis=1).reshape(2, 2),
        small[6:].sum(axis=1),
    )


def solution(mesh):
    placed = (
        P(("dp", "tensor"), None),
        P("dp", None),
        P("dp", None, "tensor"),
        P("dp", "tensor"),
        P("dp", None, "tensor"),
        P("dp", "tensor"),
        P(),
        P(),
        P(),
        P(),
        P(("dp", "tensor"), None),
    )
    return jax.shard_map(
        local,
        mesh=mesh,
        in_specs=placed,
        out_specs=(
            P(("dp", "tensor"), None),
            P(("dp", "tensor"), None),
            P("dp", None, "tensor"),
            P("dp", "tensor"),
            P("dp", None, "tensor"),
            P("dp", "tensor"),
            P(),
            P(),
            P(),
            P(),
        ),
        check_vma=False,
    )
```

```python
import functools
import math

import jax
import jax.numpy as jnp
from jax import lax
from jax.experimental import pallas as pl
from jax.experimental.pallas import tpu as pltpu
from jax.sharding import PartitionSpec as P

HEAD_DIM = 64
EPS = 1e-06
BIG = 1e30
BLK = 256
SUB = 128
MESH = pl.DeviceIdType.MESH


def dot(a, b):
    return jnp.dot(a, b, preferred_element_type=jnp.float32)


def dot_nt(a, b):
    return lax.dot_general(a, b, (((1,), (1,)), ((), ())), preferred_element_type=jnp.float32)


def dot_tn(a, b):
    return lax.dot_general(a, b, (((0,), (0,)), ((), ())), preferred_element_type=jnp.float32)


def turned(a):
    return a.astype(jnp.float32).T


def seg_vector(len_ref, pos):
    begin = jnp.zeros_like(pos)
    edge = jnp.int32(0)
    for k in range(len_ref.shape[1] - 1):
        edge = edge + len_ref[0, k]
        begin = jnp.where(pos >= edge, edge, begin)
    return begin


def seg_scalar(len_ref, row):
    begin = jnp.int32(0)
    end = jnp.int32(0)
    edge = jnp.int32(0)
    for k in range(len_ref.shape[1]):
        after = edge + len_ref[0, k]
        inside = (row >= edge) & (row < after)
        begin = jnp.where(inside, edge, begin)
        end = jnp.where(inside, after, end)
        edge = after
    return begin, end


def place(me, chunk, per):
    return (chunk // per) ^ me, pl.multiple_of((chunk % per) * SUB, SUB)


def fwd_kernel(heads, parts, len_ref, me_ref, *refs):
    proj = refs[:parts]
    o_ref, ot_ref, lse_ref, qt, kh, vt, acc, mx, tot = refs[parts:]
    i = pl.program_id(0)
    part_rows = proj[0].shape[0]
    per = part_rows // SUB
    blk, hd = BLK, HEAD_DIM
    feats = heads * hd
    me = me_ref[0]

    @pl.when(i == 0)
    def _():
        for c in range(parts):
            base = (me ^ c) * part_rows
            def turn(s, carry, c=c, base=base):
                src = pl.ds(pl.multiple_of(s * SUB, SUB), SUB)
                at = pl.ds(pl.multiple_of(base + s * SUB, SUB), SUB)
                rows = proj[c][src, :]
                qt[:, at] = (turned(rows[:, :feats]) * 0.125).astype(jnp.bfloat16)
                vt[:, at] = turned(rows[:, 2 * feats :]).astype(jnp.bfloat16)
                for h in range(heads):
                    kh[h, at, :] = rows[:, feats + h * hd : feats + (h + 1) * hd]
                return carry
            lax.fori_loop(0, per, turn, 0)

    first = pl.multiple_of(i * blk, blk)
    cols = pl.ds(first, blk)
    pos = first + lax.broadcasted_iota(jnp.int32, (1, blk), 1)
    begin = seg_vector(len_ref, pos)
    b_first, _ = seg_scalar(len_ref, first)
    b_last, _ = seg_scalar(len_ref, first + blk - 1)
    j_lo = b_first // blk
    j_full = jnp.minimum((b_last + blk - 1) // blk, i)
    mx[...] = jnp.full_like(mx, -BIG)
    tot[...] = jnp.zeros_like(tot)
    acc[...] = jnp.zeros_like(acc)

    def step(j, masked, first_pass):
        at = pl.ds(pl.multiple_of(j * blk, blk), blk)
        if masked:
            key = j * blk + lax.broadcasted_iota(jnp.int32, (blk, blk), 0)
            ok = (key >= begin) & (key <= pos)
        scores = []
        for h in range(heads):
            s = dot(kh[h, at, :], qt[h * hd : (h + 1) * hd, cols])
            scores.append(jnp.where(ok, s, -BIG) if masked else s)
        if first_pass:
            for h in range(heads):
                old = mx[h : h + 1]
                new = jnp.maximum(old, jnp.max(scores[h], axis=0, keepdims=True))
                total = jnp.sum(jnp.exp(scores[h] - new), axis=0, keepdims=True)
                mx[h : h + 1] = new
                tot[h : h + 1] = jnp.exp(old - new) * tot[h : h + 1] + total
        else:
            for h in range(heads):
                hs = slice(h * hd, (h + 1) * hd)
                p = jnp.exp(scores[h] - mx[h : h + 1])
                acc[hs] += dot(vt[hs, at], p.astype(jnp.bfloat16))

    def loop(lo, hi, masked, first_pass):
        def body(j, carry):
            step(j, masked, first_pass)
            return carry
        lax.fori_loop(lo, hi, body, 0)

    for first_pass in (True, False):
        loop(j_lo, j_full, True, first_pass)
        loop(jnp.maximum(j_full, j_lo), i, False, first_pass)
        step(i, True, first_pass)
        if first_pass:
            mx[...] = mx[...] + jnp.log(tot[...])
            lse_ref[...] = mx[...]
    ot_ref[...] = acc[...]
    out = acc[...].T.astype(jnp.bfloat16)
    for s in range(blk // SUB):
        c, row = place(me, i * (blk // SUB) + s, per)
        o_ref[c, pl.ds(row, SUB), :] = out[s * SUB : (s + 1) * SUB]


def attn_fwd(lengths, me, proj):
    parts = len(proj)
    part_rows, width = proj[0].shape
    feats = width // 3
    rows = parts * part_rows
    heads = feats // HEAD_DIM
    return pl.pallas_call(
        functools.partial(fwd_kernel, heads, parts),
        out_shape=(
            jax.ShapeDtypeStruct((parts, part_rows, feats), jnp.bfloat16),
            jax.ShapeDtypeStruct((feats, rows), jnp.float32),
            jax.ShapeDtypeStruct((8, rows), jnp.float32),
        ),
        grid_spec=pltpu.PrefetchScalarGridSpec(
            num_scalar_prefetch=2,
            grid=(rows // BLK,),
            in_specs=[pl.BlockSpec((part_rows, width), lambda i, s, m: (0, 0))] * parts,
            out_specs=(
                pl.BlockSpec((parts, part_rows, feats), lambda i, s, m: (0, 0, 0)),
                pl.BlockSpec((feats, BLK), lambda i, s, m: (0, i)),
                pl.BlockSpec((8, BLK), lambda i, s, m: (0, i)),
            ),
            scratch_shapes=[
                pltpu.VMEM((feats, rows), jnp.bfloat16),
                pltpu.VMEM((heads, rows, HEAD_DIM), jnp.bfloat16),
                pltpu.VMEM((feats, rows), jnp.bfloat16),
                pltpu.VMEM((feats, BLK), jnp.float32),
                pltpu.VMEM((8, BLK), jnp.float32),
                pltpu.VMEM((8, BLK), jnp.float32),
            ],
        ),
        cost_estimate=pl.CostEstimate(
            flops=rows * feats * 4096, bytes_accessed=12 * rows * feats, transcendentals=rows * 512 * heads
        ),
        name="attn_fwd",
    )(lengths, me, *proj)


def bwd_kernel(heads, parts, len_ref, me_ref, *refs):
    proj = refs[:parts]
    grads = refs[parts : 2 * parts]
    ot_ref, lse_ref, d_ref, qt, qp, gt, gp, kh, vh, kt, dqt, delta, dkv = refs[2 * parts :]
    j = pl.program_id(0)
    n = pl.num_programs(0)
    part_rows = proj[0].shape[0]
    per = part_rows // SUB
    blk, hd = BLK, HEAD_DIM
    feats = heads * hd
    me = me_ref[0]

    @pl.when(j == 0)
    def _():
        zero = jnp.zeros((SUB, hd), jnp.bfloat16)
        for c in range(parts):
            base = (me ^ c) * part_rows
            def turn(s, carry, c=c, base=base):
                src = pl.ds(pl.multiple_of(s * SUB, SUB), SUB)
                at = pl.ds(pl.multiple_of(base + s * SUB, SUB), SUB)
                rows = proj[c][src, :]
                g = grads[c][src, :]
                g_turned = turned(g)
                qt[:, at] = (turned(rows[:, :feats]) * 0.125).astype(jnp.bfloat16)
                kt[:, at] = turned(rows[:, feats : 2 * feats]).astype(jnp.bfloat16)
                gt[:, at] = g_turned.astype(jnp.bfloat16)
                prod = g_turned * ot_ref[:, at]
                dqt[:, at] = jnp.zeros((feats, SUB), jnp.float32)
                for h in range(heads):
                    hs = slice(h * hd, (h + 1) * hd)
                    delta[h : h + 1, at] = jnp.sum(prod[hs], axis=0, keepdims=True)
                    qp[h, at, :] = jnp.concatenate([rows[:, hs], zero], axis=1)
                    gp[h, at, :] = jnp.concatenate([zero, g[:, hs]], axis=1)
                    kh[h, at, :] = rows[:, feats + h * hd : feats + (h + 1) * hd]
                    vh[h, at, :] = rows[:, 2 * feats + h * hd : 2 * feats + (h + 1) * hd]
                return carry
            lax.fori_loop(0, per, turn, 0)

    first = pl.multiple_of(j * blk, blk)
    keys = pl.ds(first, blk)
    _, e_first = seg_scalar(len_ref, first)
    _, e_last = seg_scalar(len_ref, first + blk - 1)
    i_hi = (e_last - 1) // blk + 1
    i_full = jnp.clip(e_first // blk, j + 1, i_hi)
    key = first + lax.broadcasted_iota(jnp.int32, (blk, blk), 0)

    def step(i, masked, start):
        at = pl.ds(pl.multiple_of(i * blk, blk), blk)
        if masked:
            pos = i * blk + lax.broadcasted_iota(jnp.int32, (1, blk), 1)
            begin = seg_vector(len_ref, pos)
            ok = (key >= begin) & (key <= pos)
        scores, dprobs = [], []
        for h in range(heads):
            hs = slice(h * hd, (h + 1) * hd)
            scores.append(dot(kh[h, keys, :], qt[hs, at]))
            dprobs.append(dot(vh[h, keys, :], gt[hs, at]))
        both = []
        for h in range(heads):
            e = scores[h] - lse_ref[h : h + 1, at]
            if masked:
                e = jnp.where(ok, e, -BIG)
            p = jnp.exp(e)
            ds = p * (dprobs[h] - delta[h : h + 1, at])
            both.append((p.astype(jnp.bfloat16), ds.astype(jnp.bfloat16)))
        for h in range(heads):
            hs = slice(h * hd, (h + 1) * hd)
            p, ds = both[h]
            add = dot(
                jnp.concatenate([ds, p], axis=1),
                jnp.concatenate([qp[h, at, :], gp[h, at, :]], axis=0),
            )
            if start:
                dkv[h] = add
            else:
                dkv[h] += add
            dqt[hs, at] += dot(kt[hs, keys], ds)

    def loop(lo, hi, masked):
        def body(i, carry):
            step(i, masked, False)
            return carry
        lax.fori_loop(lo, hi, body, 0)

    step(j, True, True)
    loop(j + 1, i_full, False)
    loop(i_full, i_hi, True)
    pair = jnp.concatenate(
        [dkv[h][:, :hd] * 0.125 for h in range(heads)] + [dkv[h][:, hd:] for h in range(heads)], axis=1
    ).astype(jnp.bfloat16)
    for s in range(blk // SUB):
        c, row = place(me, j * (blk // SUB) + s, per)
        d_ref[c, pl.ds(row, SUB), feats:] = pair[s * SUB : (s + 1) * SUB]

    @pl.when(j == n - 1)
    def _():
        for c in range(parts):
            base = (me ^ c) * part_rows
            def turn(s, carry, c=c, base=base):
                at = pl.ds(pl.multiple_of(base + s * SUB, SUB), SUB)
                dst = pl.ds(pl.multiple_of(s * SUB, SUB), SUB)
                d_ref[c, dst, :feats] = (dqt[:, at] * 0.125).T.astype(jnp.bfloat16)
                return carry
            lax.fori_loop(0, per, turn, 0)


def attn_bwd(lengths, me, proj, grads, heads_turned, log_total):
    parts = len(proj)
    part_rows, width = proj[0].shape
    feats = width // 3
    rows = parts * part_rows
    heads = feats // HEAD_DIM
    return pl.pallas_call(
        functools.partial(bwd_kernel, heads, parts),
        out_shape=jax.ShapeDtypeStruct((parts, part_rows, width), jnp.bfloat16),
        grid_spec=pltpu.PrefetchScalarGridSpec(
            num_scalar_prefetch=2,
            grid=(rows // BLK,),
            in_specs=[pl.BlockSpec((part_rows, width), lambda i, s, m: (0, 0))] * parts
            + [pl.BlockSpec((part_rows, feats), lambda i, s, m: (0, 0))] * parts
            + [
                pl.BlockSpec((feats, rows), lambda i, s, m: (0, 0)),
                pl.BlockSpec((8, rows), lambda i, s, m: (0, 0)),
            ],
            out_specs=pl.BlockSpec((parts, part_rows, width), lambda i, s, m: (0, 0, 0)),
            scratch_shapes=[
                pltpu.VMEM((feats, rows), jnp.bfloat16),
                pltpu.VMEM((heads, rows, 2 * HEAD_DIM), jnp.bfloat16),
                pltpu.VMEM((feats, rows), jnp.bfloat16),
                pltpu.VMEM((heads, rows, 2 * HEAD_DIM), jnp.bfloat16),
                pltpu.VMEM((heads, rows, HEAD_DIM), jnp.bfloat16),
                pltpu.VMEM((heads, rows, HEAD_DIM), jnp.bfloat16),
                pltpu.VMEM((feats, rows), jnp.bfloat16),
                pltpu.VMEM((feats, rows), jnp.float32),
                pltpu.VMEM((8, rows), jnp.float32),
                pltpu.VMEM((heads, BLK, 2 * HEAD_DIM), jnp.float32),
            ],
        ),
        cost_estimate=pl.CostEstimate(
            flops=rows * feats * 10240, bytes_accessed=20 * rows * feats, transcendentals=rows * 512 * heads
        ),
        name="attn_bwd",
    )(lengths, me, *proj, *grads, heads_turned, log_total)


def gelu_parts(v):
    c = math.sqrt(2 / math.pi)
    square = v * v
    t = jnp.tanh(c * v * (1.0 + 0.044715 * square))
    half = 0.5 * (1.0 + t)
    slope = half + (0.5 * v) * (1.0 - t * t) * (c * (1.0 + 3 * 0.044715 * square))
    return v * half, slope


def ffn_kernel(tile, x_ref, g_ref, wg_ref, wu_ref, wd_ref, h_ref, dg_ref, du_ref, branch_ref, dx_ref, branch, dx):
    u = pl.program_id(0)
    x = x_ref[...]
    gate = dot(x, wg_ref[...])
    up = dot(x, wu_ref[...])
    grad_hidden = dot(g_ref[...], wd_ref[...])
    act, slope = gelu_parts(gate)
    hidden = (act * up).astype(jnp.bfloat16)
    dgate = (slope * (grad_hidden * up)).astype(jnp.bfloat16)
    dup = (grad_hidden * act).astype(jnp.bfloat16)
    h_ref[...] = hidden
    dg_ref[...] = dgate
    du_ref[...] = dup
    b_add = dot_nt(hidden, wd_ref[...])
    d_add = dot_nt(dgate, wg_ref[...]) + dot_nt(dup, wu_ref[...])

    @pl.when(u == 0)
    def _():
        branch[...] = b_add
        dx[...] = d_add

    @pl.when(u > 0)
    def _():
        branch[...] += b_add
        dx[...] += d_add

    @pl.when(u == pl.num_programs(0) - 1)
    def _():
        branch_ref[...] = branch[...]
        dx_ref[...] = dx[...].astype(jnp.bfloat16)


def ffn_rows(x, g, weights, tile=256):
    rows, d = x.shape
    units = weights.shape[1] // 3
    n = units // tile
    full = pl.BlockSpec((rows, d), lambda u: (0, 0))
    cols = pl.BlockSpec((rows, tile), lambda u: (0, u))
    wide = jax.ShapeDtypeStruct((rows, units), jnp.bfloat16)
    narrow = jax.ShapeDtypeStruct((rows, d), jnp.bfloat16)
    return pl.pallas_call(
        functools.partial(ffn_kernel, tile),
        out_shape=(wide, wide, wide, jax.ShapeDtypeStruct((rows, d), jnp.float32), narrow),
        grid=(n,),
        in_specs=[
            full,
            full,
            pl.BlockSpec((d, tile), lambda u: (0, u)),
            pl.BlockSpec((d, tile), lambda u: (0, u + n)),
            pl.BlockSpec((d, tile), lambda u: (0, u + 2 * n)),
        ],
        out_specs=(cols, cols, cols, full, full),
        scratch_shapes=[pltpu.VMEM((rows, d), jnp.float32), pltpu.VMEM((rows, d), jnp.float32)],
        cost_estimate=pl.CostEstimate(
            flops=12 * rows * d * units,
            bytes_accessed=2 * (4 * rows * d + 3 * rows * units + 3 * d * units),
            transcendentals=rows * units,
        ),
        name="ffn_rows",
    )(x, g, weights, weights, weights)


def wgrad_kernel(parts, n, *refs):
    xs, gs, gates, ups, hiddens = [refs[parts * m : parts * (m + 1)] for m in range(5)]
    out, left_t = refs[-2:]
    i = pl.program_id(0)
    rows = xs[0].shape[0]

    def turn_all(lefts):
        for c in range(parts):
            def turn(s, carry, c=c):
                src = pl.ds(pl.multiple_of(s * SUB, SUB), SUB)
                at = pl.ds(pl.multiple_of(c * rows + s * SUB, SUB), SUB)
                left_t[:, at] = turned(lefts[c][src, :]).astype(jnp.bfloat16)
                return carry
            lax.fori_loop(0, rows // SUB, turn, 0)

    def product(rights):
        total = dot(left_t[:, :rows], rights[0][...])
        for c in range(1, parts):
            total += dot(left_t[:, c * rows : (c + 1) * rows], rights[c][...])
        out[...] = total.astype(jnp.bfloat16)

    @pl.when(i == 0)
    def _():
        turn_all(xs)

    @pl.when(i == 2 * n)
    def _():
        turn_all(gs)

    @pl.when(i < n)
    def _():
        product(gates)

    @pl.when((i >= n) & (i < 2 * n))
    def _():
        product(ups)

    @pl.when(i >= 2 * n)
    def _():
        product(hiddens)


def wgrad(xs, gs, gates, ups, hiddens, tile=256):
    parts = len(xs)
    rows, d = xs[0].shape
    units = gates[0].shape[1]
    n = units // tile

    def tiles(m):
        return [pl.BlockSpec((rows, tile), lambda i: (0, jnp.clip(i - m * n, 0, n - 1)))] * parts

    return pl.pallas_call(
        functools.partial(wgrad_kernel, parts, n),
        out_shape=jax.ShapeDtypeStruct((d, 3 * units), jnp.bfloat16),
        grid=(3 * n,),
        in_specs=[pl.BlockSpec((rows, d), lambda i: (0, 0))] * (2 * parts) + tiles(0) + tiles(1) + tiles(2),
        out_specs=pl.BlockSpec((d, tile), lambda i: (0, i)),
        scratch_shapes=[pltpu.VMEM((d, parts * rows), jnp.bfloat16)],
        cost_estimate=pl.CostEstimate(
            flops=6 * parts * rows * d * units,
            bytes_accessed=2 * parts * rows * (2 * d + 3 * units) + 6 * d * units,
            transcendentals=0,
        ),
        name="wgrad",
    )(*xs, *gs, *gates, *ups, *hiddens)


def rms_norm(features, norm_gain):
    return features * lax.rsqrt(jnp.mean(features * features, axis=-1, keepdims=True) + EPS) * norm_gain


def norm_back(v, gain, e):
    rate = lax.rsqrt(jnp.mean(v * v, axis=-1, keepdims=True) + EPS)
    scaled = gain * e
    dot_mean = jnp.mean(scaled * v, axis=-1, keepdims=True)
    return rate * scaled - v * (rate * rate * rate * dot_mean), jnp.sum(e * v * rate, axis=0, keepdims=True)


def middle_kernel(parts, share, came, got, middle, top, gain, *refs):
    weights = refs[:parts]
    grad_ref, low_ref = refs[parts : parts + 2]
    heads = refs[parts + 2 : 2 * parts + 2]
    gain_ref = refs[-1]
    f32 = jnp.float32
    e = share[...].astype(f32) + came[...].astype(f32) + got[...].astype(f32)
    grad, part = norm_back(middle[...], gain[...], e)
    grad = top[...] + grad
    grad_ref[...] = grad
    low = grad.astype(jnp.bfloat16)
    low_ref[...] = low
    for c in range(parts):
        heads[c][...] = dot(low, weights[c][...]).astype(jnp.bfloat16)

    @pl.when(pl.program_id(0) == 0)
    def _():
        gain_ref[...] = part

    @pl.when(pl.program_id(0) > 0)
    def _():
        gain_ref[...] += part


def middle_back(share, came, got, middle, top, gain, weights, block=160):
    rows, d = middle.shape
    feats = weights[0].shape[1]
    parts = len(weights)
    row = pl.BlockSpec((block, d), lambda i: (i, 0))
    one = pl.BlockSpec((1, d), lambda i: (0, 0))
    outs = pl.pallas_call(
        functools.partial(middle_kernel, parts),
        out_shape=(
            jax.ShapeDtypeStruct((rows, d), jnp.float32),
            jax.ShapeDtypeStruct((rows, d), jnp.bfloat16),
            *[jax.ShapeDtypeStruct((rows, feats), jnp.bfloat16)] * parts,
            jax.ShapeDtypeStruct((1, d), jnp.float32),
        ),
        grid=(rows // block,),
        in_specs=[row] * 5 + [one] + [pl.BlockSpec((d, feats), lambda i: (0, 0))] * parts,
        out_specs=(row, row, *[pl.BlockSpec((block, feats), lambda i: (i, 0))] * parts, one),
        cost_estimate=pl.CostEstimate(
            flops=2 * rows * d * feats * parts, bytes_accessed=22 * rows * d, transcendentals=rows
        ),
        name="middle_back",
    )(share, came, got, middle, top, gain[None], *weights)
    return outs[0], outs[1], list(outs[2 : 2 + parts]), outs[-1]


def input_kernel(share, came, got_a, got_b, inputs, cot, grad_middle, early, gain, mix, correct, out, sums):
    i = pl.program_id(0)
    f32 = jnp.float32
    d = gain.shape[1]
    got = jnp.where(i < pl.num_programs(0) // 2, got_a[...].astype(f32), got_b[...].astype(f32))
    e = share[...].astype(f32) + came[...].astype(f32) + got
    one, two = inputs[:, :d].astype(f32), inputs[:, d:].astype(f32)
    cot_one, cot_two = cot[:, :d].astype(f32), cot[:, d:].astype(f32)
    grad, part = norm_back(mix[0, 0] * one + mix[0, 1] * two, gain[...], e)
    main = cot_one + grad_middle[...] + grad - (correct[0] * cot_one + correct[1] * cot_two)
    out[:, :d] = mix[0, 0] * main + mix[1, 0] * cot_two
    out[:, d:] = mix[0, 1] * main + mix[1, 1] * cot_two

    @pl.when(i == 0)
    def _():
        sums[...] = early[...]

    sums[0:1] += part
    for r, value in enumerate((main * one, main * two, cot_two * one, cot_two * two)):
        sums[r + 1 : r + 2] += jnp.sum(value, axis=0, keepdims=True)


def input_back(share, came, got, inputs, cot, grad_middle, early, gain, mix, correct, block=160):
    rows, d = grad_middle.shape
    half = rows // block // 2
    row = pl.BlockSpec((block, d), lambda i: (i, 0))
    wide = pl.BlockSpec((block, 2 * d), lambda i: (i, 0))
    sums = pl.BlockSpec((8, d), lambda i: (0, 0))
    small = pl.BlockSpec(memory_space=pltpu.SMEM)
    return pl.pallas_call(
        input_kernel,
        out_shape=(jax.ShapeDtypeStruct((rows, 2 * d), jnp.float32), jax.ShapeDtypeStruct((8, d), jnp.float32)),
        grid=(2 * half,),
        in_specs=[
            row,
            row,
            pl.BlockSpec((block, d), lambda i: (jnp.minimum(i, half - 1), 0)),
            pl.BlockSpec((block, d), lambda i: (jnp.maximum(i - half, 0), 0)),
            wide,
            wide,
            row,
            sums,
            pl.BlockSpec((1, d), lambda i: (0, 0)),
            small,
            small,
        ],
        out_specs=(wide, sums),
        cost_estimate=pl.CostEstimate(flops=60 * rows * d, bytes_accessed=30 * rows * d, transcendentals=rows),
        name="input_back",
    )(share, came, *got, inputs, cot, grad_middle, early, gain[None], mix, correct)


def swap(array, bit):
    count = lax.axis_size("tensor")
    return lax.ppermute(array, "tensor", [(i, i ^ bit) for i in range(count)])


def after(value, *others):
    return lax.optimization_barrier((value, *others))[0]


def flipped(index, bits):
    bit = 1
    while bit <= bits:
        if bits & bit:
            index = index + bit - 2 * bit * lax.rem(lax.div(index, bit), 2)
        bit *= 2
    return index


def start_kernel(
    count, chunks, x, qkv, wo, sib, far, diag, qkv_all, wo_all,
    local_sem, sib_sem, far_send, far_recv, diag_send, diag_recv, qkv_dp, wo_dp,
):
    t = lax.axis_index("tensor")
    g = lax.axis_index("dp")
    order = []
    bit = 2
    while bit < count:
        order.append(bit)
        bit *= 2
    order.append(1)

    def last(e):
        return max(k for k, b in enumerate(order) if e & b)

    barrier = pltpu.get_barrier_semaphore()
    for c in (1, 2):
        pl.semaphore_signal(barrier, inc=1, device_id={"tensor": flipped(t, c)}, device_id_type=MESH)
    for b in order:
        pl.semaphore_signal(barrier, inc=1, device_id={"dp": flipped(g, b)}, device_id_type=MESH)
    pl.semaphore_wait(barrier, 2 + len(order))

    size = x.shape[0] // chunks

    def far_copy(k):
        rows = pl.ds(k * size, size)
        return pltpu.make_async_remote_copy(
            x.at[rows], far.at[rows], far_send.at[k], far_recv.at[k], {"tensor": flipped(t, 2)}, MESH
        )

    def diag_copy(k):
        rows = pl.ds(k * size, size)
        return pltpu.make_async_remote_copy(
            far.at[rows], diag.at[rows], diag_send.at[k], diag_recv.at[k], {"tensor": flipped(t, 1)}, MESH
        )

    def dp_copy(which, e):
        own, whole, sems = ((qkv, qkv_all, qkv_dp), (wo, wo_all, wo_dp))[which]
        b = order[last(e)]
        block = flipped(g, e ^ b)
        return pltpu.make_async_remote_copy(
            own if e == b else whole.at[block],
            whole.at[block],
            sems.at[0, e - 1],
            sems.at[1, e - 1],
            {"dp": flipped(g, b)},
            MESH,
        )

    def dp_arrival(which, e):
        whole, sems = ((qkv_all, qkv_dp), (wo_all, wo_dp))[which]
        dst = whole.at[flipped(g, e)]
        return pltpu.make_async_remote_copy(
            dst, dst, sems.at[0, e - 1], sems.at[1, e - 1], {"dp": flipped(g, order[last(e)])}, MESH
        )

    sends = []

    def go(copy):
        copy.start()
        sends.append(copy)

    for b in order:
        go(dp_copy(0, b))
    fars = [far_copy(k) for k in range(chunks)]
    for copy in fars:
        go(copy)
    near = pltpu.make_async_remote_copy(
        x, sib, sib_sem.at[0], sib_sem.at[1], {"tensor": flipped(t, 1)}, MESH
    )
    go(near)
    kept = [
        pltpu.make_async_copy(qkv, qkv_all.at[g], local_sem.at[0]),
        pltpu.make_async_copy(wo, wo_all.at[g], local_sem.at[1]),
    ]
    for copy in kept:
        copy.start()
    for b in order:
        go(dp_copy(1, b))
    diags = []

    def pass_on(k):
        fars[k].wait_recv()
        diags.append(diag_copy(k))
        go(diags[-1])

    done = 0
    for e in sorted(range(1, count), key=lambda e: (last(e), e)):
        for which in (0, 1):
            dp_arrival(which, e).wait_recv()
            for b in order[last(e) + 1 :]:
                go(dp_copy(which, e ^ b))
        if done < chunks and e & 1 == 0:
            pass_on(done)
            done += 1
    while done < chunks:
        pass_on(done)
        done += 1
    for copy in diags:
        copy.wait_recv()
    near.wait_recv()
    for copy in sends:
        copy.wait_send()
    for copy in kept:
        copy.wait()


def start(x, qkv, wo, chunks=4):
    count = lax.axis_size("dp")
    rows = jax.ShapeDtypeStruct(x.shape, x.dtype)
    dma = pltpu.SemaphoreType.DMA
    sib, far, diag, qkv_all, wo_all = pl.pallas_call(
        functools.partial(start_kernel, count, chunks),
        out_shape=(
            rows,
            rows,
            rows,
            jax.ShapeDtypeStruct((count, *qkv.shape), qkv.dtype),
            jax.ShapeDtypeStruct((count, *wo.shape), wo.dtype),
        ),
        in_specs=[pl.BlockSpec(memory_space=pl.ANY)] * 3,
        out_specs=(pl.BlockSpec(memory_space=pl.ANY),) * 5,
        scratch_shapes=[
            dma((2,)),
            dma((2,)),
            dma((chunks,)),
            dma((chunks,)),
            dma((chunks,)),
            dma((chunks,)),
            dma((2, count - 1)),
            dma((2, count - 1)),
        ],
        compiler_params=pltpu.CompilerParams(collective_id=0, has_side_effects=True),
        cost_estimate=pl.CostEstimate(flops=0, bytes_accessed=100_000_000, transcendentals=0),
        name="start",
    )(x, qkv, wo)
    whole = count * qkv.shape[0]
    return [x, sib, far, diag], qkv_all.reshape(whole, -1), wo_all.reshape(whole, -1)


def spread(rows):
    far = swap(rows, 2)
    return [rows, swap(rows, 1), far, swap(far, 1)]


def exchange(blocks):
    return [blocks[0]] + [swap(blocks[c], c) for c in range(1, len(blocks))]


def summed(shares, before=None, beside=None):
    f32 = jnp.float32
    far = (shares[2].astype(f32) + swap(shares[3], 1).astype(f32)).astype(jnp.bfloat16)
    if before is not None:
        far = after(far, before)
    got = swap(far, 2)
    near = shares[0].astype(f32) + swap(shares[1], 1).astype(f32)
    if beside is not None:
        got, beside = lax.optimization_barrier((got, beside(far)))
    return near + got.astype(f32), beside


def end_kernel(count, mine, total, near, mid, far, near_sem, far_sem):
    t = lax.axis_index("tensor")
    g = lax.axis_index("dp")
    barrier = pltpu.get_barrier_semaphore()
    for c in (1, 2, 3):
        pl.semaphore_signal(barrier, inc=1, device_id={"tensor": flipped(t, c)}, device_id_type=MESH)
    for e in range(1, count):
        pl.semaphore_signal(barrier, inc=1, device_id={"dp": flipped(g, e)}, device_id_type=MESH)
    pl.semaphore_wait(barrier, 2 + count)

    nears = [
        pltpu.make_async_remote_copy(
            mine, near.at[c - 1], near_sem.at[0, c - 1], near_sem.at[1, c - 1], {"tensor": flipped(t, c)}, MESH
        )
        for c in (1, 2, 3)
    ]
    fars = [
        pltpu.make_async_remote_copy(
            mid, far.at[e - 1], far_sem.at[0, e - 1], far_sem.at[1, e - 1], {"dp": flipped(g, e)}, MESH
        )
        for e in range(1, count)
    ]
    for copy in nears:
        copy.start()
    for copy in nears:
        copy.wait_recv()
    mid[...] = (mine[...] + near[0]) + (near[1] + near[2])
    for copy in fars:
        copy.start()
    for copy in fars:
        copy.wait_recv()
    level = [mid[...]] + [far[e] for e in range(count - 1)]
    while len(level) > 1:
        level = [level[k] + level[k + 1] for k in range(0, len(level), 2)]
    total[...] = level[0]
    for copy in nears + fars:
        copy.wait_send()


def end(mine):
    count = lax.axis_size("dp")
    dma = pltpu.SemaphoreType.DMA
    vmem = pl.BlockSpec(memory_space=pltpu.VMEM)
    return pl.pallas_call(
        functools.partial(end_kernel, count),
        out_shape=jax.ShapeDtypeStruct(mine.shape, jnp.float32),
        in_specs=[vmem],
        out_specs=vmem,
        scratch_shapes=[
            pltpu.VMEM((3, *mine.shape), jnp.float32),
            pltpu.VMEM(mine.shape, jnp.float32),
            pltpu.VMEM((count - 1, *mine.shape), jnp.float32),
            dma((2, 3)),
            dma((2, count - 1)),
        ],
        compiler_params=pltpu.CompilerParams(collective_id=1, has_side_effects=True),
        cost_estimate=pl.CostEstimate(flops=0, bytes_accessed=30_000_000, transcendentals=0),
        name="end",
    )(mine)


def local(
    block_input, seq_lengths, w_qkv, w_out, w_gate_up, w_down, gain_attn, gain_ffn, mix_matrix, correct_gain, cotangent
):
    f32, bf16 = jnp.float32, jnp.bfloat16
    width = gain_attn.shape[0]
    me = lax.axis_index("tensor").astype(jnp.int32)[None]
    shard = w_qkv.shape[0]
    feats = w_out.shape[1]
    inputs = block_input.astype(f32)
    stream_one = inputs[:, :width]
    stream_two = inputs[:, width:]
    predicted_main = mix_matrix[0, 0] * stream_one + mix_matrix[0, 1] * stream_two
    predicted_side = mix_matrix[1, 0] * stream_one + mix_matrix[1, 1] * stream_two
    units = w_down.shape[1]

    normed_attn, qkv_all, out_mine = start(
        rms_norm(predicted_main, gain_attn).astype(bf16),
        w_qkv.reshape(shard, 3 * feats).astype(bf16),
        w_out.astype(bf16),
    )
    ffn_mine = jnp.concatenate([w_gate_up.reshape(shard, -1), w_down], axis=1).astype(bf16)
    ffn_all = lax.all_gather(after(ffn_mine, normed_attn[1]), "dp", axis=0, tiled=True)
    proj = [dot(x, qkv_all).astype(bf16) for x in normed_attn]
    attended, heads_turned, log_total = attn_fwd(seq_lengths, me, proj)

    incoming = cotangent.astype(f32)
    cot_one = incoming[:, :width]
    cot_two = incoming[:, width:]
    grad_top = correct_gain[0] * cot_one + correct_gain[1] * cot_two
    grad_ffn = spread(after(grad_top.astype(bf16), normed_attn[1]))

    out_parts = [out_mine] + [swap(out_mine, c) for c in (1, 2, 3)]
    attended = after(attended, grad_ffn[2], out_parts[2], out_parts[3])
    head_parts = exchange([attended[c] for c in range(len(proj))])
    attn_branch = sum(dot_nt(a, w) for a, w in zip(head_parts, out_parts))
    middle = predicted_main + attn_branch

    normed_mine = rms_norm(middle, gain_ffn).astype(bf16)
    normed_ffn = [normed_mine, swap(normed_mine, 1), swap(normed_mine, 2)]
    pieces = [ffn_rows(x, g, ffn_all) for x, g in zip(normed_ffn, grad_ffn[:2])]
    normed_ffn[2] = after(normed_ffn[2], pieces[0][0], pieces[1][0])
    normed_ffn.append(swap(normed_ffn[2], 1))
    pieces += [ffn_rows(x, g, ffn_all) for x, g in zip(normed_ffn[2:], grad_ffn[2:])]
    hidden, dgate, dup, branch, dnormed = zip(*pieces)
    far = (dnormed[2].astype(f32) + swap(dnormed[3], 1).astype(f32)).astype(bf16)
    got = swap(far, 2)
    came = swap(dnormed[1], 1)
    weight_ffn = wgrad([after(normed_ffn[0], far)] + normed_ffn[1:], grad_ffn, dgate, dup, hidden)
    got, came, weight_ffn = lax.optimization_barrier((got, came, weight_ffn))
    weight_ffn = lax.psum_scatter(weight_ffn, "dp", scatter_dimension=0, tiled=True)
    grad_middle, grad_attn, grad_heads, grad_gain_ffn = middle_back(
        dnormed[0], came, got, middle, grad_top, gain_ffn, out_parts
    )
    grad_heads = exchange(grad_heads)
    grad_proj = attn_bwd(seq_lengths, me, proj, grad_heads, heads_turned, log_total)
    *late, later_attn = lax.optimization_barrier((*head_parts, grad_heads[2], grad_heads[3], grad_attn))
    out_shares = exchange([dot_tn(later_attn, a).astype(bf16) for a in late[:4]])
    weight_out = sum(s.astype(f32) for s in out_shares)
    ffn_branch, (grad_proj, weight_out) = summed(branch, before=late[4], beside=lambda far: (grad_proj, weight_out))
    grad_proj = [grad_proj[c] for c in range(len(proj))]

    correction = (middle + ffn_branch) - predicted_main
    block_output = jnp.concatenate(
        [predicted_main + correct_gain[0] * correction, predicted_side + correct_gain[1] * correction], axis=1
    ).astype(bf16)
    early = jnp.concatenate(
        [
            jnp.zeros((5, width), f32),
            grad_gain_ffn,
            jnp.sum(cot_one * correction, axis=0, keepdims=True),
            jnp.sum(cot_two * correction, axis=0, keepdims=True),
        ],
        axis=0,
    )

    far = [dot_nt(g, qkv_all).astype(bf16) for g in grad_proj[2:]]
    far = (far[0].astype(f32) + swap(far[1], 1).astype(f32)).astype(bf16)
    half = far.shape[0] // 2
    got = [swap(far[:half], 2), swap(far[half:], 2)]
    *late, far = lax.optimization_barrier((*grad_proj, *normed_attn, weight_out, far))
    near = [dot_nt(g, qkv_all).astype(bf16) for g in late[:2]]
    weight_qkv = sum(dot_tn(x, g) for x, g in zip(late[4:8], late[:4]))
    last = jnp.concatenate([weight_qkv, late[8]], axis=1).astype(bf16)
    last, weight_ffn, got[0] = lax.optimization_barrier((last, weight_ffn, got[0]))
    summed_last = lax.psum_scatter(last, "dp", scatter_dimension=0, tiled=True)
    came = swap(near[1], 1)
    got[1], last, came, early, block_output = lax.optimization_barrier((got[1], last, came, early, block_output))
    grad_input, small = input_back(
        near[0], came, got, block_input, cotangent, grad_middle, early, gain_attn, mix_matrix, correct_gain
    )
    weight_ffn = weight_ffn.astype(f32)
    sum_gate_up = weight_ffn[:, : 2 * units].reshape(shard, 2, units)
    sum_down = weight_ffn[:, 2 * units :]
    small = end(small)
    last = summed_last.astype(f32)
    sum_qkv = last[:, : 3 * feats].reshape(shard, 3, feats)
    sum_out = last[:, 3 * feats :]
    return (
        block_output,
        grad_input,
        sum_qkv,
        sum_out,
        sum_gate_up,
        sum_down,
        small[0],
        small[5],
        small[1:5].sum(axis=1).reshape(2, 2),
        small[6:].sum(axis=1),
    )


def solution(mesh):
    placed = (
        P(("dp", "tensor"), None),
        P("dp", None),
        P("dp", None, "tensor"),
        P("dp", "tensor"),
        P("dp", None, "tensor"),
        P("dp", "tensor"),
        P(),
        P(),
        P(),
        P(),
        P(("dp", "tensor"), None),
    )
    return jax.shard_map(
        local,
        mesh=mesh,
        in_specs=placed,
        out_specs=(
            P(("dp", "tensor"), None),
            P(("dp", "tensor"), None),
            P("dp", None, "tensor"),
            P("dp", "tensor"),
            P("dp", None, "tensor"),
            P("dp", "tensor"),
            P(),
            P(),
            P(),
            P(),
        ),
        check_vma=False,
    )
```

```python
import functools
import math

import jax
import jax.numpy as jnp
from jax import lax
from jax.experimental import pallas as pl
from jax.experimental.pallas import tpu as pltpu
from jax.sharding import PartitionSpec as P

HEAD_DIM = 64
EPS = 1e-06
BIG = 1e30
BLK = 256
SUB = 128
MESH = pl.DeviceIdType.MESH


def dot(a, b):
    return jnp.dot(a, b, preferred_element_type=jnp.float32)


def dot_nt(a, b):
    return lax.dot_general(a, b, (((1,), (1,)), ((), ())), preferred_element_type=jnp.float32)


def dot_tn(a, b):
    return lax.dot_general(a, b, (((0,), (0,)), ((), ())), preferred_element_type=jnp.float32)


def turned(a):
    return a.astype(jnp.float32).T


def seg_vector(len_ref, pos):
    begin = jnp.zeros_like(pos)
    edge = jnp.int32(0)
    for k in range(len_ref.shape[1] - 1):
        edge = edge + len_ref[0, k]
        begin = jnp.where(pos >= edge, edge, begin)
    return begin


def seg_scalar(len_ref, row):
    begin = jnp.int32(0)
    end = jnp.int32(0)
    edge = jnp.int32(0)
    for k in range(len_ref.shape[1]):
        after = edge + len_ref[0, k]
        inside = (row >= edge) & (row < after)
        begin = jnp.where(inside, edge, begin)
        end = jnp.where(inside, after, end)
        edge = after
    return begin, end


def place(me, chunk, per):
    return (chunk // per) ^ me, pl.multiple_of((chunk % per) * SUB, SUB)


def fwd_kernel(heads, parts, len_ref, me_ref, *refs):
    proj = refs[:parts]
    o_ref, ot_ref, lse_ref, qt, kh, vt, acc, mx, tot = refs[parts:]
    i = pl.program_id(0)
    part_rows = proj[0].shape[0]
    per = part_rows // SUB
    blk, hd = BLK, HEAD_DIM
    feats = heads * hd
    me = me_ref[0]

    @pl.when(i == 0)
    def _():
        for c in range(parts):
            base = (me ^ c) * part_rows
            def turn(s, carry, c=c, base=base):
                src = pl.ds(pl.multiple_of(s * SUB, SUB), SUB)
                at = pl.ds(pl.multiple_of(base + s * SUB, SUB), SUB)
                rows = proj[c][src, :]
                qt[:, at] = (turned(rows[:, :feats]) * 0.125).astype(jnp.bfloat16)
                vt[:, at] = turned(rows[:, 2 * feats :]).astype(jnp.bfloat16)
                for h in range(heads):
                    kh[h, at, :] = rows[:, feats + h * hd : feats + (h + 1) * hd]
                return carry
            lax.fori_loop(0, per, turn, 0)

    first = pl.multiple_of(i * blk, blk)
    cols = pl.ds(first, blk)
    pos = first + lax.broadcasted_iota(jnp.int32, (1, blk), 1)
    begin = seg_vector(len_ref, pos)
    b_first, _ = seg_scalar(len_ref, first)
    b_last, _ = seg_scalar(len_ref, first + blk - 1)
    j_lo = b_first // blk
    j_full = jnp.minimum((b_last + blk - 1) // blk, i)
    mx[...] = jnp.full_like(mx, -BIG)
    tot[...] = jnp.zeros_like(tot)
    acc[...] = jnp.zeros_like(acc)

    def step(j, masked, first_pass):
        at = pl.ds(pl.multiple_of(j * blk, blk), blk)
        if masked:
            key = j * blk + lax.broadcasted_iota(jnp.int32, (blk, blk), 0)
            ok = (key >= begin) & (key <= pos)
        scores = []
        for h in range(heads):
            s = dot(kh[h, at, :], qt[h * hd : (h + 1) * hd, cols])
            scores.append(jnp.where(ok, s, -BIG) if masked else s)
        if first_pass:
            for h in range(heads):
                old = mx[h : h + 1]
                new = jnp.maximum(old, jnp.max(scores[h], axis=0, keepdims=True))
                total = jnp.sum(jnp.exp(scores[h] - new), axis=0, keepdims=True)
                mx[h : h + 1] = new
                tot[h : h + 1] = jnp.exp(old - new) * tot[h : h + 1] + total
        else:
            for h in range(heads):
                hs = slice(h * hd, (h + 1) * hd)
                p = jnp.exp(scores[h] - mx[h : h + 1])
                acc[hs] += dot(vt[hs, at], p.astype(jnp.bfloat16))

    def loop(lo, hi, masked, first_pass):
        def body(j, carry):
            step(j, masked, first_pass)
            return carry
        lax.fori_loop(lo, hi, body, 0)

    for first_pass in (True, False):
        loop(j_lo, j_full, True, first_pass)
        loop(jnp.maximum(j_full, j_lo), i, False, first_pass)
        step(i, True, first_pass)
        if first_pass:
            mx[...] = mx[...] + jnp.log(tot[...])
            lse_ref[...] = mx[...]
    ot_ref[...] = acc[...]
    out = acc[...].T.astype(jnp.bfloat16)
    for s in range(blk // SUB):
        c, row = place(me, i * (blk // SUB) + s, per)
        o_ref[c, pl.ds(row, SUB), :] = out[s * SUB : (s + 1) * SUB]


def attn_fwd(lengths, me, proj):
    parts = len(proj)
    part_rows, width = proj[0].shape
    feats = width // 3
    rows = parts * part_rows
    heads = feats // HEAD_DIM
    return pl.pallas_call(
        functools.partial(fwd_kernel, heads, parts),
        out_shape=(
            jax.ShapeDtypeStruct((parts, part_rows, feats), jnp.bfloat16),
            jax.ShapeDtypeStruct((feats, rows), jnp.float32),
            jax.ShapeDtypeStruct((8, rows), jnp.float32),
        ),
        grid_spec=pltpu.PrefetchScalarGridSpec(
            num_scalar_prefetch=2,
            grid=(rows // BLK,),
            in_specs=[pl.BlockSpec((part_rows, width), lambda i, s, m: (0, 0))] * parts,
            out_specs=(
                pl.BlockSpec((parts, part_rows, feats), lambda i, s, m: (0, 0, 0)),
                pl.BlockSpec((feats, BLK), lambda i, s, m: (0, i)),
                pl.BlockSpec((8, BLK), lambda i, s, m: (0, i)),
            ),
            scratch_shapes=[
                pltpu.VMEM((feats, rows), jnp.bfloat16),
                pltpu.VMEM((heads, rows, HEAD_DIM), jnp.bfloat16),
                pltpu.VMEM((feats, rows), jnp.bfloat16),
                pltpu.VMEM((feats, BLK), jnp.float32),
                pltpu.VMEM((8, BLK), jnp.float32),
                pltpu.VMEM((8, BLK), jnp.float32),
            ],
        ),
        cost_estimate=pl.CostEstimate(
            flops=rows * feats * 4096, bytes_accessed=12 * rows * feats, transcendentals=rows * 512 * heads
        ),
        name="attn_fwd",
    )(lengths, me, *proj)


def bwd_kernel(heads, parts, len_ref, me_ref, *refs):
    proj = refs[:parts]
    grads = refs[parts : 2 * parts]
    ot_ref, lse_ref, d_ref, qt, qp, gt, gp, kh, vh, kt, dqt, delta, dkv = refs[2 * parts :]
    j = pl.program_id(0)
    n = pl.num_programs(0)
    part_rows = proj[0].shape[0]
    per = part_rows // SUB
    blk, hd = BLK, HEAD_DIM
    feats = heads * hd
    me = me_ref[0]

    @pl.when(j == 0)
    def _():
        zero = jnp.zeros((SUB, hd), jnp.bfloat16)
        for c in range(parts):
            base = (me ^ c) * part_rows
            def turn(s, carry, c=c, base=base):
                src = pl.ds(pl.multiple_of(s * SUB, SUB), SUB)
                at = pl.ds(pl.multiple_of(base + s * SUB, SUB), SUB)
                rows = proj[c][src, :]
                g = grads[c][src, :]
                g_turned = turned(g)
                qt[:, at] = (turned(rows[:, :feats]) * 0.125).astype(jnp.bfloat16)
                kt[:, at] = turned(rows[:, feats : 2 * feats]).astype(jnp.bfloat16)
                gt[:, at] = g_turned.astype(jnp.bfloat16)
                prod = g_turned * ot_ref[:, at]
                dqt[:, at] = jnp.zeros((feats, SUB), jnp.float32)
                for h in range(heads):
                    hs = slice(h * hd, (h + 1) * hd)
                    delta[h : h + 1, at] = jnp.sum(prod[hs], axis=0, keepdims=True)
                    qp[h, at, :] = jnp.concatenate([rows[:, hs], zero], axis=1)
                    gp[h, at, :] = jnp.concatenate([zero, g[:, hs]], axis=1)
                    kh[h, at, :] = rows[:, feats + h * hd : feats + (h + 1) * hd]
                    vh[h, at, :] = rows[:, 2 * feats + h * hd : 2 * feats + (h + 1) * hd]
                return carry
            lax.fori_loop(0, per, turn, 0)

    first = pl.multiple_of(j * blk, blk)
    keys = pl.ds(first, blk)
    _, e_first = seg_scalar(len_ref, first)
    _, e_last = seg_scalar(len_ref, first + blk - 1)
    i_hi = (e_last - 1) // blk + 1
    i_full = jnp.clip(e_first // blk, j + 1, i_hi)
    key = first + lax.broadcasted_iota(jnp.int32, (blk, blk), 0)

    def step(i, masked, start):
        at = pl.ds(pl.multiple_of(i * blk, blk), blk)
        if masked:
            pos = i * blk + lax.broadcasted_iota(jnp.int32, (1, blk), 1)
            begin = seg_vector(len_ref, pos)
            ok = (key >= begin) & (key <= pos)
        scores, dprobs = [], []
        for h in range(heads):
            hs = slice(h * hd, (h + 1) * hd)
            scores.append(dot(kh[h, keys, :], qt[hs, at]))
            dprobs.append(dot(vh[h, keys, :], gt[hs, at]))
        both = []
        for h in range(heads):
            e = scores[h] - lse_ref[h : h + 1, at]
            if masked:
                e = jnp.where(ok, e, -BIG)
            p = jnp.exp(e)
            ds = p * (dprobs[h] - delta[h : h + 1, at])
            both.append((p.astype(jnp.bfloat16), ds.astype(jnp.bfloat16)))
        for h in range(heads):
            hs = slice(h * hd, (h + 1) * hd)
            p, ds = both[h]
            add = dot(
                jnp.concatenate([ds, p], axis=1),
                jnp.concatenate([qp[h, at, :], gp[h, at, :]], axis=0),
            )
            if start:
                dkv[h] = add
            else:
                dkv[h] += add
            dqt[hs, at] += dot(kt[hs, keys], ds)

    def loop(lo, hi, masked):
        def body(i, carry):
            step(i, masked, False)
            return carry
        lax.fori_loop(lo, hi, body, 0)

    step(j, True, True)
    loop(j + 1, i_full, False)
    loop(i_full, i_hi, True)
    pair = jnp.concatenate(
        [dkv[h][:, :hd] * 0.125 for h in range(heads)] + [dkv[h][:, hd:] for h in range(heads)], axis=1
    ).astype(jnp.bfloat16)
    for s in range(blk // SUB):
        c, row = place(me, j * (blk // SUB) + s, per)
        d_ref[c, pl.ds(row, SUB), feats:] = pair[s * SUB : (s + 1) * SUB]

    @pl.when(j == n - 1)
    def _():
        for c in range(parts):
            base = (me ^ c) * part_rows
            def turn(s, carry, c=c, base=base):
                at = pl.ds(pl.multiple_of(base + s * SUB, SUB), SUB)
                dst = pl.ds(pl.multiple_of(s * SUB, SUB), SUB)
                d_ref[c, dst, :feats] = (dqt[:, at] * 0.125).T.astype(jnp.bfloat16)
                return carry
            lax.fori_loop(0, per, turn, 0)


def attn_bwd(lengths, me, proj, grads, heads_turned, log_total):
    parts = len(proj)
    part_rows, width = proj[0].shape
    feats = width // 3
    rows = parts * part_rows
    heads = feats // HEAD_DIM
    return pl.pallas_call(
        functools.partial(bwd_kernel, heads, parts),
        out_shape=jax.ShapeDtypeStruct((parts, part_rows, width), jnp.bfloat16),
        grid_spec=pltpu.PrefetchScalarGridSpec(
            num_scalar_prefetch=2,
            grid=(rows // BLK,),
            in_specs=[pl.BlockSpec((part_rows, width), lambda i, s, m: (0, 0))] * parts
            + [pl.BlockSpec((part_rows, feats), lambda i, s, m: (0, 0))] * parts
            + [
                pl.BlockSpec((feats, rows), lambda i, s, m: (0, 0)),
                pl.BlockSpec((8, rows), lambda i, s, m: (0, 0)),
            ],
            out_specs=pl.BlockSpec((parts, part_rows, width), lambda i, s, m: (0, 0, 0)),
            scratch_shapes=[
                pltpu.VMEM((feats, rows), jnp.bfloat16),
                pltpu.VMEM((heads, rows, 2 * HEAD_DIM), jnp.bfloat16),
                pltpu.VMEM((feats, rows), jnp.bfloat16),
                pltpu.VMEM((heads, rows, 2 * HEAD_DIM), jnp.bfloat16),
                pltpu.VMEM((heads, rows, HEAD_DIM), jnp.bfloat16),
                pltpu.VMEM((heads, rows, HEAD_DIM), jnp.bfloat16),
                pltpu.VMEM((feats, rows), jnp.bfloat16),
                pltpu.VMEM((feats, rows), jnp.float32),
                pltpu.VMEM((8, rows), jnp.float32),
                pltpu.VMEM((heads, BLK, 2 * HEAD_DIM), jnp.float32),
            ],
        ),
        cost_estimate=pl.CostEstimate(
            flops=rows * feats * 10240, bytes_accessed=20 * rows * feats, transcendentals=rows * 512 * heads
        ),
        name="attn_bwd",
    )(lengths, me, *proj, *grads, heads_turned, log_total)


def gelu_parts(v):
    c = math.sqrt(2 / math.pi)
    square = v * v
    t = jnp.tanh(c * v * (1.0 + 0.044715 * square))
    half = 0.5 * (1.0 + t)
    slope = half + (0.5 * v) * (1.0 - t * t) * (c * (1.0 + 3 * 0.044715 * square))
    return v * half, slope


def ffn_kernel(tile, x_ref, g_ref, wg_ref, wu_ref, wd_ref, h_ref, dg_ref, du_ref, branch_ref, dx_ref, branch, dx):
    u = pl.program_id(0)
    x = x_ref[...]
    gate = dot(x, wg_ref[...])
    up = dot(x, wu_ref[...])
    grad_hidden = dot(g_ref[...], wd_ref[...])
    act, slope = gelu_parts(gate)
    hidden = (act * up).astype(jnp.bfloat16)
    dgate = (slope * (grad_hidden * up)).astype(jnp.bfloat16)
    dup = (grad_hidden * act).astype(jnp.bfloat16)
    h_ref[...] = hidden
    dg_ref[...] = dgate
    du_ref[...] = dup
    b_add = dot_nt(hidden, wd_ref[...])
    d_add = dot_nt(dgate, wg_ref[...]) + dot_nt(dup, wu_ref[...])

    @pl.when(u == 0)
    def _():
        branch[...] = b_add
        dx[...] = d_add

    @pl.when(u > 0)
    def _():
        branch[...] += b_add
        dx[...] += d_add

    @pl.when(u == pl.num_programs(0) - 1)
    def _():
        branch_ref[...] = branch[...]
        dx_ref[...] = dx[...].astype(jnp.bfloat16)


def ffn_rows(x, g, weights, tile=256):
    rows, d = x.shape
    units = weights.shape[1] // 3
    n = units // tile
    full = pl.BlockSpec((rows, d), lambda u: (0, 0))
    cols = pl.BlockSpec((rows, tile), lambda u: (0, u))
    wide = jax.ShapeDtypeStruct((rows, units), jnp.bfloat16)
    narrow = jax.ShapeDtypeStruct((rows, d), jnp.bfloat16)
    return pl.pallas_call(
        functools.partial(ffn_kernel, tile),
        out_shape=(wide, wide, wide, jax.ShapeDtypeStruct((rows, d), jnp.float32), narrow),
        grid=(n,),
        in_specs=[
            full,
            full,
            pl.BlockSpec((d, tile), lambda u: (0, u)),
            pl.BlockSpec((d, tile), lambda u: (0, u + n)),
            pl.BlockSpec((d, tile), lambda u: (0, u + 2 * n)),
        ],
        out_specs=(cols, cols, cols, full, full),
        scratch_shapes=[pltpu.VMEM((rows, d), jnp.float32), pltpu.VMEM((rows, d), jnp.float32)],
        cost_estimate=pl.CostEstimate(
            flops=12 * rows * d * units,
            bytes_accessed=2 * (4 * rows * d + 3 * rows * units + 3 * d * units),
            transcendentals=rows * units,
        ),
        name="ffn_rows",
    )(x, g, weights, weights, weights)


def wgrad_kernel(parts, n, *refs):
    xs, gs, gates, ups, hiddens = [refs[parts * m : parts * (m + 1)] for m in range(5)]
    out, left_t = refs[-2:]
    i = pl.program_id(0)
    rows = xs[0].shape[0]

    def turn_all(lefts):
        for c in range(parts):
            def turn(s, carry, c=c):
                src = pl.ds(pl.multiple_of(s * SUB, SUB), SUB)
                at = pl.ds(pl.multiple_of(c * rows + s * SUB, SUB), SUB)
                left_t[:, at] = turned(lefts[c][src, :]).astype(jnp.bfloat16)
                return carry
            lax.fori_loop(0, rows // SUB, turn, 0)

    def product(rights):
        total = dot(left_t[:, :rows], rights[0][...])
        for c in range(1, parts):
            total += dot(left_t[:, c * rows : (c + 1) * rows], rights[c][...])
        out[...] = total.astype(jnp.bfloat16)

    @pl.when(i == 0)
    def _():
        turn_all(xs)

    @pl.when(i == 2 * n)
    def _():
        turn_all(gs)

    @pl.when(i < n)
    def _():
        product(gates)

    @pl.when((i >= n) & (i < 2 * n))
    def _():
        product(ups)

    @pl.when(i >= 2 * n)
    def _():
        product(hiddens)


def wgrad(xs, gs, gates, ups, hiddens, tile=256):
    parts = len(xs)
    rows, d = xs[0].shape
    units = gates[0].shape[1]
    n = units // tile

    def tiles(m):
        return [pl.BlockSpec((rows, tile), lambda i: (0, jnp.clip(i - m * n, 0, n - 1)))] * parts

    return pl.pallas_call(
        functools.partial(wgrad_kernel, parts, n),
        out_shape=jax.ShapeDtypeStruct((d, 3 * units), jnp.bfloat16),
        grid=(3 * n,),
        in_specs=[pl.BlockSpec((rows, d), lambda i: (0, 0))] * (2 * parts) + tiles(0) + tiles(1) + tiles(2),
        out_specs=pl.BlockSpec((d, tile), lambda i: (0, i)),
        scratch_shapes=[pltpu.VMEM((d, parts * rows), jnp.bfloat16)],
        cost_estimate=pl.CostEstimate(
            flops=6 * parts * rows * d * units,
            bytes_accessed=2 * parts * rows * (2 * d + 3 * units) + 6 * d * units,
            transcendentals=0,
        ),
        name="wgrad",
    )(*xs, *gs, *gates, *ups, *hiddens)


def rms_norm(features, norm_gain):
    return features * lax.rsqrt(jnp.mean(features * features, axis=-1, keepdims=True) + EPS) * norm_gain


def norm_back(v, gain, e):
    rate = lax.rsqrt(jnp.mean(v * v, axis=-1, keepdims=True) + EPS)
    scaled = gain * e
    dot_mean = jnp.mean(scaled * v, axis=-1, keepdims=True)
    return rate * scaled - v * (rate * rate * rate * dot_mean), jnp.sum(e * v * rate, axis=0, keepdims=True)


def middle_kernel(parts, share, came, got, middle, top, gain, *refs):
    weights = refs[:parts]
    grad_ref, low_ref = refs[parts : parts + 2]
    heads = refs[parts + 2 : 2 * parts + 2]
    gain_ref = refs[-1]
    f32 = jnp.float32
    e = share[...].astype(f32) + came[...].astype(f32) + got[...].astype(f32)
    grad, part = norm_back(middle[...], gain[...], e)
    grad = top[...] + grad
    grad_ref[...] = grad
    low = grad.astype(jnp.bfloat16)
    low_ref[...] = low
    for c in range(parts):
        heads[c][...] = dot(low, weights[c][...]).astype(jnp.bfloat16)

    @pl.when(pl.program_id(0) == 0)
    def _():
        gain_ref[...] = part

    @pl.when(pl.program_id(0) > 0)
    def _():
        gain_ref[...] += part


def middle_back(share, came, got, middle, top, gain, weights, block=160):
    rows, d = middle.shape
    feats = weights[0].shape[1]
    parts = len(weights)
    row = pl.BlockSpec((block, d), lambda i: (i, 0))
    one = pl.BlockSpec((1, d), lambda i: (0, 0))
    outs = pl.pallas_call(
        functools.partial(middle_kernel, parts),
        out_shape=(
            jax.ShapeDtypeStruct((rows, d), jnp.float32),
            jax.ShapeDtypeStruct((rows, d), jnp.bfloat16),
            *[jax.ShapeDtypeStruct((rows, feats), jnp.bfloat16)] * parts,
            jax.ShapeDtypeStruct((1, d), jnp.float32),
        ),
        grid=(rows // block,),
        in_specs=[row] * 5 + [one] + [pl.BlockSpec((d, feats), lambda i: (0, 0))] * parts,
        out_specs=(row, row, *[pl.BlockSpec((block, feats), lambda i: (i, 0))] * parts, one),
        cost_estimate=pl.CostEstimate(
            flops=2 * rows * d * feats * parts, bytes_accessed=22 * rows * d, transcendentals=rows
        ),
        name="middle_back",
    )(share, came, got, middle, top, gain[None], *weights)
    return outs[0], outs[1], list(outs[2 : 2 + parts]), outs[-1]


def input_kernel(share, came, got_a, got_b, inputs, cot, grad_middle, early, gain, mix, correct, out, sums):
    i = pl.program_id(0)
    f32 = jnp.float32
    d = gain.shape[1]
    got = jnp.where(i < pl.num_programs(0) // 2, got_a[...].astype(f32), got_b[...].astype(f32))
    e = share[...].astype(f32) + came[...].astype(f32) + got
    one, two = inputs[:, :d].astype(f32), inputs[:, d:].astype(f32)
    cot_one, cot_two = cot[:, :d].astype(f32), cot[:, d:].astype(f32)
    grad, part = norm_back(mix[0, 0] * one + mix[0, 1] * two, gain[...], e)
    main = cot_one + grad_middle[...] + grad - (correct[0] * cot_one + correct[1] * cot_two)
    out[:, :d] = mix[0, 0] * main + mix[1, 0] * cot_two
    out[:, d:] = mix[0, 1] * main + mix[1, 1] * cot_two

    @pl.when(i == 0)
    def _():
        sums[...] = early[...]

    sums[0:1] += part
    for r, value in enumerate((main * one, main * two, cot_two * one, cot_two * two)):
        sums[r + 1 : r + 2] += jnp.sum(value, axis=0, keepdims=True)


def input_back(share, came, got, inputs, cot, grad_middle, early, gain, mix, correct, block=160):
    rows, d = grad_middle.shape
    half = rows // block // 2
    row = pl.BlockSpec((block, d), lambda i: (i, 0))
    wide = pl.BlockSpec((block, 2 * d), lambda i: (i, 0))
    sums = pl.BlockSpec((8, d), lambda i: (0, 0))
    small = pl.BlockSpec(memory_space=pltpu.SMEM)
    return pl.pallas_call(
        input_kernel,
        out_shape=(jax.ShapeDtypeStruct((rows, 2 * d), jnp.float32), jax.ShapeDtypeStruct((8, d), jnp.float32)),
        grid=(2 * half,),
        in_specs=[
            row,
            row,
            pl.BlockSpec((block, d), lambda i: (jnp.minimum(i, half - 1), 0)),
            pl.BlockSpec((block, d), lambda i: (jnp.maximum(i - half, 0), 0)),
            wide,
            wide,
            row,
            sums,
            pl.BlockSpec((1, d), lambda i: (0, 0)),
            small,
            small,
        ],
        out_specs=(wide, sums),
        cost_estimate=pl.CostEstimate(flops=60 * rows * d, bytes_accessed=30 * rows * d, transcendentals=rows),
        name="input_back",
    )(share, came, *got, inputs, cot, grad_middle, early, gain[None], mix, correct)


def swap(array, bit):
    count = lax.axis_size("tensor")
    return lax.ppermute(array, "tensor", [(i, i ^ bit) for i in range(count)])


def after(value, *others):
    return lax.optimization_barrier((value, *others))[0]


def flipped(index, bits):
    bit = 1
    while bit <= bits:
        if bits & bit:
            index = index + bit - 2 * bit * lax.rem(lax.div(index, bit), 2)
        bit *= 2
    return index


def start_kernel(
    count, chunks, x, qkv, wo, sib, far, diag, qkv_all, wo_all,
    local_sem, sib_sem, far_send, far_recv, diag_send, diag_recv, qkv_dp, wo_dp,
):
    t = lax.axis_index("tensor")
    g = lax.axis_index("dp")
    order = []
    bit = 2
    while bit < count:
        order.append(bit)
        bit *= 2
    order.append(1)

    def last(e):
        return max(k for k, b in enumerate(order) if e & b)

    barrier = pltpu.get_barrier_semaphore()
    for c in (1, 2):
        pl.semaphore_signal(barrier, inc=1, device_id={"tensor": flipped(t, c)}, device_id_type=MESH)
    for b in order:
        pl.semaphore_signal(barrier, inc=1, device_id={"dp": flipped(g, b)}, device_id_type=MESH)
    pl.semaphore_wait(barrier, 2 + len(order))

    size = x.shape[0] // chunks

    def far_copy(k):
        rows = pl.ds(k * size, size)
        return pltpu.make_async_remote_copy(
            x.at[rows], far.at[rows], far_send.at[k], far_recv.at[k], {"tensor": flipped(t, 2)}, MESH
        )

    def diag_copy(k):
        rows = pl.ds(k * size, size)
        return pltpu.make_async_remote_copy(
            far.at[rows], diag.at[rows], diag_send.at[k], diag_recv.at[k], {"tensor": flipped(t, 1)}, MESH
        )

    def dp_copy(which, e):
        own, whole, sems = ((qkv, qkv_all, qkv_dp), (wo, wo_all, wo_dp))[which]
        b = order[last(e)]
        block = flipped(g, e ^ b)
        return pltpu.make_async_remote_copy(
            own if e == b else whole.at[block],
            whole.at[block],
            sems.at[0, e - 1],
            sems.at[1, e - 1],
            {"dp": flipped(g, b)},
            MESH,
        )

    def dp_arrival(which, e):
        whole, sems = ((qkv_all, qkv_dp), (wo_all, wo_dp))[which]
        dst = whole.at[flipped(g, e)]
        return pltpu.make_async_remote_copy(
            dst, dst, sems.at[0, e - 1], sems.at[1, e - 1], {"dp": flipped(g, order[last(e)])}, MESH
        )

    sends = []

    def go(copy):
        copy.start()
        sends.append(copy)

    for b in order:
        go(dp_copy(0, b))
    fars = [far_copy(k) for k in range(chunks)]
    for copy in fars:
        go(copy)
    near = pltpu.make_async_remote_copy(
        x, sib, sib_sem.at[0], sib_sem.at[1], {"tensor": flipped(t, 1)}, MESH
    )
    go(near)
    kept = [
        pltpu.make_async_copy(qkv, qkv_all.at[g], local_sem.at[0]),
        pltpu.make_async_copy(wo, wo_all.at[g], local_sem.at[1]),
    ]
    for copy in kept:
        copy.start()
    for b in order:
        go(dp_copy(1, b))
    diags = []

    def pass_on(k):
        fars[k].wait_recv()
        diags.append(diag_copy(k))
        go(diags[-1])

    done = 0
    for e in sorted(range(1, count), key=lambda e: (last(e), e)):
        for which in (0, 1):
            dp_arrival(which, e).wait_recv()
            for b in order[last(e) + 1 :]:
                go(dp_copy(which, e ^ b))
        if done < chunks and e & 1 == 0:
            pass_on(done)
            done += 1
    while done < chunks:
        pass_on(done)
        done += 1
    for copy in diags:
        copy.wait_recv()
    near.wait_recv()
    for copy in sends:
        copy.wait_send()
    for copy in kept:
        copy.wait()


def start(x, qkv, wo, chunks=4):
    count = lax.axis_size("dp")
    rows = jax.ShapeDtypeStruct(x.shape, x.dtype)
    dma = pltpu.SemaphoreType.DMA
    sib, far, diag, qkv_all, wo_all = pl.pallas_call(
        functools.partial(start_kernel, count, chunks),
        out_shape=(
            rows,
            rows,
            rows,
            jax.ShapeDtypeStruct((count, *qkv.shape), qkv.dtype),
            jax.ShapeDtypeStruct((count, *wo.shape), wo.dtype),
        ),
        in_specs=[pl.BlockSpec(memory_space=pl.ANY)] * 3,
        out_specs=(pl.BlockSpec(memory_space=pl.ANY),) * 5,
        scratch_shapes=[
            dma((2,)),
            dma((2,)),
            dma((chunks,)),
            dma((chunks,)),
            dma((chunks,)),
            dma((chunks,)),
            dma((2, count - 1)),
            dma((2, count - 1)),
        ],
        compiler_params=pltpu.CompilerParams(collective_id=0, has_side_effects=True),
        cost_estimate=pl.CostEstimate(flops=0, bytes_accessed=100_000_000, transcendentals=0),
        name="start",
    )(x, qkv, wo)
    whole = count * qkv.shape[0]
    return [x, sib, far, diag], qkv_all.reshape(whole, -1), wo_all.reshape(whole, -1)


def spread(rows):
    far = swap(rows, 2)
    return [rows, swap(rows, 1), far, swap(far, 1)]


def exchange(blocks):
    return [blocks[0]] + [swap(blocks[c], c) for c in range(1, len(blocks))]


def summed(shares, before=None, beside=None):
    f32 = jnp.float32
    far = (shares[2].astype(f32) + swap(shares[3], 1).astype(f32)).astype(jnp.bfloat16)
    if before is not None:
        far = after(far, before)
    got = swap(far, 2)
    near = shares[0].astype(f32) + swap(shares[1], 1).astype(f32)
    if beside is not None:
        got, beside = lax.optimization_barrier((got, beside(far)))
    return near + got.astype(f32), beside


def end_kernel(count, mine, total, near, mid, far, near_sem, far_sem):
    t = lax.axis_index("tensor")
    g = lax.axis_index("dp")
    barrier = pltpu.get_barrier_semaphore()
    for c in (1, 2, 3):
        pl.semaphore_signal(barrier, inc=1, device_id={"tensor": flipped(t, c)}, device_id_type=MESH)
    for e in range(1, count):
        pl.semaphore_signal(barrier, inc=1, device_id={"dp": flipped(g, e)}, device_id_type=MESH)
    pl.semaphore_wait(barrier, 2 + count)

    nears = [
        pltpu.make_async_remote_copy(
            mine, near.at[c - 1], near_sem.at[0, c - 1], near_sem.at[1, c - 1], {"tensor": flipped(t, c)}, MESH
        )
        for c in (1, 2, 3)
    ]
    fars = [
        pltpu.make_async_remote_copy(
            mid, far.at[e - 1], far_sem.at[0, e - 1], far_sem.at[1, e - 1], {"dp": flipped(g, e)}, MESH
        )
        for e in range(1, count)
    ]
    for copy in nears:
        copy.start()
    for copy in nears:
        copy.wait_recv()
    mid[...] = (mine[...] + near[0]) + (near[1] + near[2])
    for copy in fars:
        copy.start()
    for copy in fars:
        copy.wait_recv()
    level = [mid[...]] + [far[e] for e in range(count - 1)]
    while len(level) > 1:
        level = [level[k] + level[k + 1] for k in range(0, len(level), 2)]
    total[...] = level[0]
    for copy in nears + fars:
        copy.wait_send()


def end(mine):
    count = lax.axis_size("dp")
    dma = pltpu.SemaphoreType.DMA
    vmem = pl.BlockSpec(memory_space=pltpu.VMEM)
    return pl.pallas_call(
        functools.partial(end_kernel, count),
        out_shape=jax.ShapeDtypeStruct(mine.shape, jnp.float32),
        in_specs=[vmem],
        out_specs=vmem,
        scratch_shapes=[
            pltpu.VMEM((3, *mine.shape), jnp.float32),
            pltpu.VMEM(mine.shape, jnp.float32),
            pltpu.VMEM((count - 1, *mine.shape), jnp.float32),
            dma((2, 3)),
            dma((2, count - 1)),
        ],
        compiler_params=pltpu.CompilerParams(collective_id=1, has_side_effects=True),
        cost_estimate=pl.CostEstimate(flops=0, bytes_accessed=30_000_000, transcendentals=0),
        name="end",
    )(mine)


def local(
    block_input, seq_lengths, w_qkv, w_out, w_gate_up, w_down, gain_attn, gain_ffn, mix_matrix, correct_gain, cotangent
):
    f32, bf16 = jnp.float32, jnp.bfloat16
    width = gain_attn.shape[0]
    me = lax.axis_index("tensor").astype(jnp.int32)[None]
    shard = w_qkv.shape[0]
    feats = w_out.shape[1]
    inputs = block_input.astype(f32)
    stream_one = inputs[:, :width]
    stream_two = inputs[:, width:]
    predicted_main = mix_matrix[0, 0] * stream_one + mix_matrix[0, 1] * stream_two
    predicted_side = mix_matrix[1, 0] * stream_one + mix_matrix[1, 1] * stream_two
    units = w_down.shape[1]

    normed_attn, qkv_all, out_mine = start(
        rms_norm(predicted_main, gain_attn).astype(bf16),
        w_qkv.reshape(shard, 3 * feats).astype(bf16),
        w_out.astype(bf16),
    )
    ffn_mine = jnp.concatenate([w_gate_up.reshape(shard, -1), w_down], axis=1).astype(bf16)
    ffn_all = lax.all_gather(after(ffn_mine, normed_attn[1]), "dp", axis=0, tiled=True)
    proj = [dot(x, qkv_all).astype(bf16) for x in normed_attn]
    attended, heads_turned, log_total = attn_fwd(seq_lengths, me, proj)

    incoming = cotangent.astype(f32)
    cot_one = incoming[:, :width]
    cot_two = incoming[:, width:]
    grad_top = correct_gain[0] * cot_one + correct_gain[1] * cot_two
    grad_ffn = spread(after(grad_top.astype(bf16), normed_attn[1]))

    out_parts = [out_mine] + [swap(out_mine, c) for c in (1, 2, 3)]
    attended = after(attended, grad_ffn[2], out_parts[2], out_parts[3])
    head_parts = exchange([attended[c] for c in range(len(proj))])
    attn_branch = sum(dot_nt(a, w) for a, w in zip(head_parts, out_parts))
    middle = predicted_main + attn_branch

    normed_mine = rms_norm(middle, gain_ffn).astype(bf16)
    normed_ffn = [normed_mine, swap(normed_mine, 1), swap(normed_mine, 2)]
    pieces = [ffn_rows(x, g, ffn_all) for x, g in zip(normed_ffn, grad_ffn[:2])]
    normed_ffn[2] = after(normed_ffn[2], pieces[0][0], pieces[1][0])
    normed_ffn.append(swap(normed_ffn[2], 1))
    pieces += [ffn_rows(x, g, ffn_all) for x, g in zip(normed_ffn[2:], grad_ffn[2:])]
    hidden, dgate, dup, branch, dnormed = zip(*pieces)
    far = (dnormed[2].astype(f32) + swap(dnormed[3], 1).astype(f32)).astype(bf16)
    got = swap(far, 2)
    came = swap(dnormed[1], 1)
    weight_ffn = wgrad([after(normed_ffn[0], far)] + normed_ffn[1:], grad_ffn, dgate, dup, hidden)
    got, came, weight_ffn = lax.optimization_barrier((got, came, weight_ffn))
    weight_ffn = lax.psum_scatter(weight_ffn, "dp", scatter_dimension=0, tiled=True)
    grad_middle, grad_attn, grad_heads, grad_gain_ffn = middle_back(
        dnormed[0], came, got, middle, grad_top, gain_ffn, out_parts
    )
    grad_heads = exchange(grad_heads)
    grad_proj = attn_bwd(seq_lengths, me, proj, grad_heads, heads_turned, log_total)
    *late, later_attn = lax.optimization_barrier((*head_parts, grad_heads[2], grad_heads[3], grad_attn))
    out_shares = exchange([dot_tn(later_attn, a).astype(bf16) for a in late[:4]])
    weight_out = sum(s.astype(f32) for s in out_shares)
    ffn_branch, (grad_proj, weight_out) = summed(branch, before=late[4], beside=lambda far: (grad_proj, weight_out))
    grad_proj = [grad_proj[c] for c in range(len(proj))]

    correction = (middle + ffn_branch) - predicted_main
    block_output = jnp.concatenate(
        [predicted_main + correct_gain[0] * correction, predicted_side + correct_gain[1] * correction], axis=1
    ).astype(bf16)
    early = jnp.concatenate(
        [
            jnp.zeros((5, width), f32),
            grad_gain_ffn,
            jnp.sum(cot_one * correction, axis=0, keepdims=True),
            jnp.sum(cot_two * correction, axis=0, keepdims=True),
        ],
        axis=0,
    )

    far = [dot_nt(g, qkv_all).astype(bf16) for g in grad_proj[2:]]
    far = (far[0].astype(f32) + swap(far[1], 1).astype(f32)).astype(bf16)
    half = far.shape[0] // 2
    got = [swap(far[:half], 2), swap(far[half:], 2)]
    *late, far = lax.optimization_barrier((*grad_proj, *normed_attn, weight_out, far))
    weight_qkv = sum(dot_tn(x, g) for x, g in zip(late[4:8], late[:4]))
    last = jnp.concatenate([weight_qkv, late[8]], axis=1).astype(bf16)
    last, weight_ffn = lax.optimization_barrier((last, weight_ffn))
    summed_last = lax.psum_scatter(last, "dp", scatter_dimension=0, tiled=True)
    got[0], *late = lax.optimization_barrier((got[0], *late[:2]))
    near = [dot_nt(g, qkv_all).astype(bf16) for g in late]
    came = swap(near[1], 1)
    got[1], last, came, early, block_output = lax.optimization_barrier((got[1], last, came, early, block_output))
    grad_input, small = input_back(
        near[0], came, got, block_input, cotangent, grad_middle, early, gain_attn, mix_matrix, correct_gain
    )
    weight_ffn = weight_ffn.astype(f32)
    sum_gate_up = weight_ffn[:, : 2 * units].reshape(shard, 2, units)
    sum_down = weight_ffn[:, 2 * units :]
    small = end(small)
    last = summed_last.astype(f32)
    sum_qkv = last[:, : 3 * feats].reshape(shard, 3, feats)
    sum_out = last[:, 3 * feats :]
    return (
        block_output,
        grad_input,
        sum_qkv,
        sum_out,
        sum_gate_up,
        sum_down,
        small[0],
        small[5],
        small[1:5].sum(axis=1).reshape(2, 2),
        small[6:].sum(axis=1),
    )


def solution(mesh):
    placed = (
        P(("dp", "tensor"), None),
        P("dp", None),
        P("dp", None, "tensor"),
        P("dp", "tensor"),
        P("dp", None, "tensor"),
        P("dp", "tensor"),
        P(),
        P(),
        P(),
        P(),
        P(("dp", "tensor"), None),
    )
    return jax.shard_map(
        local,
        mesh=mesh,
        in_specs=placed,
        out_specs=(
            P(("dp", "tensor"), None),
            P(("dp", "tensor"), None),
            P("dp", None, "tensor"),
            P("dp", "tensor"),
            P("dp", None, "tensor"),
            P("dp", "tensor"),
            P(),
            P(),
            P(),
            P(),
        ),
        check_vma=False,
    )
```

```python
import functools
import math

import jax
import jax.numpy as jnp
from jax import lax
from jax.experimental import pallas as pl
from jax.experimental.pallas import tpu as pltpu
from jax.sharding import PartitionSpec as P

HEAD_DIM = 64
EPS = 1e-06
BIG = 1e30
BLK = 256
SUB = 128
MESH = pl.DeviceIdType.MESH


def dot(a, b):
    return jnp.dot(a, b, preferred_element_type=jnp.float32)


def dot_nt(a, b):
    return lax.dot_general(a, b, (((1,), (1,)), ((), ())), preferred_element_type=jnp.float32)


def dot_tn(a, b):
    return lax.dot_general(a, b, (((0,), (0,)), ((), ())), preferred_element_type=jnp.float32)


def turned(a):
    return a.astype(jnp.float32).T


def seg_vector(len_ref, pos):
    begin = jnp.zeros_like(pos)
    edge = jnp.int32(0)
    for k in range(len_ref.shape[1] - 1):
        edge = edge + len_ref[0, k]
        begin = jnp.where(pos >= edge, edge, begin)
    return begin


def seg_scalar(len_ref, row):
    begin = jnp.int32(0)
    end = jnp.int32(0)
    edge = jnp.int32(0)
    for k in range(len_ref.shape[1]):
        after = edge + len_ref[0, k]
        inside = (row >= edge) & (row < after)
        begin = jnp.where(inside, edge, begin)
        end = jnp.where(inside, after, end)
        edge = after
    return begin, end


def place(me, chunk, per):
    return (chunk // per) ^ me, pl.multiple_of((chunk % per) * SUB, SUB)


def fwd_kernel(heads, parts, len_ref, me_ref, *refs):
    proj = refs[:parts]
    o_ref, ot_ref, lse_ref, qt, kh, vt, acc, mx, tot = refs[parts:]
    i = pl.program_id(0)
    part_rows = proj[0].shape[0]
    per = part_rows // SUB
    blk, hd = BLK, HEAD_DIM
    feats = heads * hd
    me = me_ref[0]

    @pl.when(i == 0)
    def _():
        for c in range(parts):
            base = (me ^ c) * part_rows
            def turn(s, carry, c=c, base=base):
                src = pl.ds(pl.multiple_of(s * SUB, SUB), SUB)
                at = pl.ds(pl.multiple_of(base + s * SUB, SUB), SUB)
                rows = proj[c][src, :]
                qt[:, at] = (turned(rows[:, :feats]) * 0.125).astype(jnp.bfloat16)
                vt[:, at] = turned(rows[:, 2 * feats :]).astype(jnp.bfloat16)
                for h in range(heads):
                    kh[h, at, :] = rows[:, feats + h * hd : feats + (h + 1) * hd]
                return carry
            lax.fori_loop(0, per, turn, 0)

    first = pl.multiple_of(i * blk, blk)
    cols = pl.ds(first, blk)
    pos = first + lax.broadcasted_iota(jnp.int32, (1, blk), 1)
    begin = seg_vector(len_ref, pos)
    b_first, _ = seg_scalar(len_ref, first)
    b_last, _ = seg_scalar(len_ref, first + blk - 1)
    j_lo = b_first // blk
    j_full = jnp.minimum((b_last + blk - 1) // blk, i)
    mx[...] = jnp.full_like(mx, -BIG)
    tot[...] = jnp.zeros_like(tot)
    acc[...] = jnp.zeros_like(acc)

    def step(j, masked, first_pass):
        at = pl.ds(pl.multiple_of(j * blk, blk), blk)
        if masked:
            key = j * blk + lax.broadcasted_iota(jnp.int32, (blk, blk), 0)
            ok = (key >= begin) & (key <= pos)
        scores = []
        for h in range(heads):
            s = dot(kh[h, at, :], qt[h * hd : (h + 1) * hd, cols])
            scores.append(jnp.where(ok, s, -BIG) if masked else s)
        if first_pass:
            for h in range(heads):
                old = mx[h : h + 1]
                new = jnp.maximum(old, jnp.max(scores[h], axis=0, keepdims=True))
                total = jnp.sum(jnp.exp(scores[h] - new), axis=0, keepdims=True)
                mx[h : h + 1] = new
                tot[h : h + 1] = jnp.exp(old - new) * tot[h : h + 1] + total
        else:
            for h in range(heads):
                hs = slice(h * hd, (h + 1) * hd)
                p = jnp.exp(scores[h] - mx[h : h + 1])
                acc[hs] += dot(vt[hs, at], p.astype(jnp.bfloat16))

    def loop(lo, hi, masked, first_pass):
        def body(j, carry):
            step(j, masked, first_pass)
            return carry
        lax.fori_loop(lo, hi, body, 0)

    for first_pass in (True, False):
        loop(j_lo, j_full, True, first_pass)
        loop(jnp.maximum(j_full, j_lo), i, False, first_pass)
        step(i, True, first_pass)
        if first_pass:
            mx[...] = mx[...] + jnp.log(tot[...])
            lse_ref[...] = mx[...]
    ot_ref[...] = acc[...]
    out = acc[...].T.astype(jnp.bfloat16)
    for s in range(blk // SUB):
        c, row = place(me, i * (blk // SUB) + s, per)
        o_ref[c, pl.ds(row, SUB), :] = out[s * SUB : (s + 1) * SUB]


def attn_fwd(lengths, me, proj):
    parts = len(proj)
    part_rows, width = proj[0].shape
    feats = width // 3
    rows = parts * part_rows
    heads = feats // HEAD_DIM
    return pl.pallas_call(
        functools.partial(fwd_kernel, heads, parts),
        out_shape=(
            jax.ShapeDtypeStruct((parts, part_rows, feats), jnp.bfloat16),
            jax.ShapeDtypeStruct((feats, rows), jnp.float32),
            jax.ShapeDtypeStruct((8, rows), jnp.float32),
        ),
        grid_spec=pltpu.PrefetchScalarGridSpec(
            num_scalar_prefetch=2,
            grid=(rows // BLK,),
            in_specs=[pl.BlockSpec((part_rows, width), lambda i, s, m: (0, 0))] * parts,
            out_specs=(
                pl.BlockSpec((parts, part_rows, feats), lambda i, s, m: (0, 0, 0)),
                pl.BlockSpec((feats, BLK), lambda i, s, m: (0, i)),
                pl.BlockSpec((8, BLK), lambda i, s, m: (0, i)),
            ),
            scratch_shapes=[
                pltpu.VMEM((feats, rows), jnp.bfloat16),
                pltpu.VMEM((heads, rows, HEAD_DIM), jnp.bfloat16),
                pltpu.VMEM((feats, rows), jnp.bfloat16),
                pltpu.VMEM((feats, BLK), jnp.float32),
                pltpu.VMEM((8, BLK), jnp.float32),
                pltpu.VMEM((8, BLK), jnp.float32),
            ],
        ),
        cost_estimate=pl.CostEstimate(
            flops=rows * feats * 4096, bytes_accessed=12 * rows * feats, transcendentals=rows * 512 * heads
        ),
        name="attn_fwd",
    )(lengths, me, *proj)


def bwd_kernel(heads, parts, len_ref, me_ref, *refs):
    proj = refs[:parts]
    grads = refs[parts : 2 * parts]
    ot_ref, lse_ref, d_ref, qt, qp, gt, gp, kh, vh, kt, dqt, delta, dkv = refs[2 * parts :]
    j = pl.program_id(0)
    n = pl.num_programs(0)
    part_rows = proj[0].shape[0]
    per = part_rows // SUB
    blk, hd = BLK, HEAD_DIM
    feats = heads * hd
    me = me_ref[0]

    @pl.when(j == 0)
    def _():
        zero = jnp.zeros((SUB, hd), jnp.bfloat16)
        for c in range(parts):
            base = (me ^ c) * part_rows
            def turn(s, carry, c=c, base=base):
                src = pl.ds(pl.multiple_of(s * SUB, SUB), SUB)
                at = pl.ds(pl.multiple_of(base + s * SUB, SUB), SUB)
                rows = proj[c][src, :]
                g = grads[c][src, :]
                g_turned = turned(g)
                qt[:, at] = (turned(rows[:, :feats]) * 0.125).astype(jnp.bfloat16)
                kt[:, at] = turned(rows[:, feats : 2 * feats]).astype(jnp.bfloat16)
                gt[:, at] = g_turned.astype(jnp.bfloat16)
                prod = g_turned * ot_ref[:, at]
                dqt[:, at] = jnp.zeros((feats, SUB), jnp.float32)
                for h in range(heads):
                    hs = slice(h * hd, (h + 1) * hd)
                    delta[h : h + 1, at] = jnp.sum(prod[hs], axis=0, keepdims=True)
                    qp[h, at, :] = jnp.concatenate([rows[:, hs], zero], axis=1)
                    gp[h, at, :] = jnp.concatenate([zero, g[:, hs]], axis=1)
                    kh[h, at, :] = rows[:, feats + h * hd : feats + (h + 1) * hd]
                    vh[h, at, :] = rows[:, 2 * feats + h * hd : 2 * feats + (h + 1) * hd]
                return carry
            lax.fori_loop(0, per, turn, 0)

    first = pl.multiple_of(j * blk, blk)
    keys = pl.ds(first, blk)
    _, e_first = seg_scalar(len_ref, first)
    _, e_last = seg_scalar(len_ref, first + blk - 1)
    i_hi = (e_last - 1) // blk + 1
    i_full = jnp.clip(e_first // blk, j + 1, i_hi)
    key = first + lax.broadcasted_iota(jnp.int32, (blk, blk), 0)

    def step(i, masked, start):
        at = pl.ds(pl.multiple_of(i * blk, blk), blk)
        if masked:
            pos = i * blk + lax.broadcasted_iota(jnp.int32, (1, blk), 1)
            begin = seg_vector(len_ref, pos)
            ok = (key >= begin) & (key <= pos)
        scores, dprobs = [], []
        for h in range(heads):
            hs = slice(h * hd, (h + 1) * hd)
            scores.append(dot(kh[h, keys, :], qt[hs, at]))
            dprobs.append(dot(vh[h, keys, :], gt[hs, at]))
        both = []
        for h in range(heads):
            e = scores[h] - lse_ref[h : h + 1, at]
            if masked:
                e = jnp.where(ok, e, -BIG)
            p = jnp.exp(e)
            ds = p * (dprobs[h] - delta[h : h + 1, at])
            both.append((p.astype(jnp.bfloat16), ds.astype(jnp.bfloat16)))
        for h in range(heads):
            hs = slice(h * hd, (h + 1) * hd)
            p, ds = both[h]
            add = dot(
                jnp.concatenate([ds, p], axis=1),
                jnp.concatenate([qp[h, at, :], gp[h, at, :]], axis=0),
            )
            if start:
                dkv[h] = add
            else:
                dkv[h] += add
            dqt[hs, at] += dot(kt[hs, keys], ds)

    def loop(lo, hi, masked):
        def body(i, carry):
            step(i, masked, False)
            return carry
        lax.fori_loop(lo, hi, body, 0)

    step(j, True, True)
    loop(j + 1, i_full, False)
    loop(i_full, i_hi, True)
    pair = jnp.concatenate(
        [dkv[h][:, :hd] * 0.125 for h in range(heads)] + [dkv[h][:, hd:] for h in range(heads)], axis=1
    ).astype(jnp.bfloat16)
    for s in range(blk // SUB):
        c, row = place(me, j * (blk // SUB) + s, per)
        d_ref[c, pl.ds(row, SUB), feats:] = pair[s * SUB : (s + 1) * SUB]

    @pl.when(j == n - 1)
    def _():
        for c in range(parts):
            base = (me ^ c) * part_rows
            def turn(s, carry, c=c, base=base):
                at = pl.ds(pl.multiple_of(base + s * SUB, SUB), SUB)
                dst = pl.ds(pl.multiple_of(s * SUB, SUB), SUB)
                d_ref[c, dst, :feats] = (dqt[:, at] * 0.125).T.astype(jnp.bfloat16)
                return carry
            lax.fori_loop(0, per, turn, 0)


def attn_bwd(lengths, me, proj, grads, heads_turned, log_total):
    parts = len(proj)
    part_rows, width = proj[0].shape
    feats = width // 3
    rows = parts * part_rows
    heads = feats // HEAD_DIM
    return pl.pallas_call(
        functools.partial(bwd_kernel, heads, parts),
        out_shape=jax.ShapeDtypeStruct((parts, part_rows, width), jnp.bfloat16),
        grid_spec=pltpu.PrefetchScalarGridSpec(
            num_scalar_prefetch=2,
            grid=(rows // BLK,),
            in_specs=[pl.BlockSpec((part_rows, width), lambda i, s, m: (0, 0))] * parts
            + [pl.BlockSpec((part_rows, feats), lambda i, s, m: (0, 0))] * parts
            + [
                pl.BlockSpec((feats, rows), lambda i, s, m: (0, 0)),
                pl.BlockSpec((8, rows), lambda i, s, m: (0, 0)),
            ],
            out_specs=pl.BlockSpec((parts, part_rows, width), lambda i, s, m: (0, 0, 0)),
            scratch_shapes=[
                pltpu.VMEM((feats, rows), jnp.bfloat16),
                pltpu.VMEM((heads, rows, 2 * HEAD_DIM), jnp.bfloat16),
                pltpu.VMEM((feats, rows), jnp.bfloat16),
                pltpu.VMEM((heads, rows, 2 * HEAD_DIM), jnp.bfloat16),
                pltpu.VMEM((heads, rows, HEAD_DIM), jnp.bfloat16),
                pltpu.VMEM((heads, rows, HEAD_DIM), jnp.bfloat16),
                pltpu.VMEM((feats, rows), jnp.bfloat16),
                pltpu.VMEM((feats, rows), jnp.float32),
                pltpu.VMEM((8, rows), jnp.float32),
                pltpu.VMEM((heads, BLK, 2 * HEAD_DIM), jnp.float32),
            ],
        ),
        cost_estimate=pl.CostEstimate(
            flops=rows * feats * 10240, bytes_accessed=20 * rows * feats, transcendentals=rows * 512 * heads
        ),
        name="attn_bwd",
    )(lengths, me, *proj, *grads, heads_turned, log_total)


def gelu_parts(v):
    c = math.sqrt(2 / math.pi)
    square = v * v
    t = jnp.tanh(c * v * (1.0 + 0.044715 * square))
    half = 0.5 * (1.0 + t)
    slope = half + (0.5 * v) * (1.0 - t * t) * (c * (1.0 + 3 * 0.044715 * square))
    return v * half, slope


def ffn_kernel(tile, x_ref, g_ref, wg_ref, wu_ref, wd_ref, h_ref, dg_ref, du_ref, branch_ref, dx_ref, branch, dx):
    u = pl.program_id(0)
    x = x_ref[...]
    gate = dot(x, wg_ref[...])
    up = dot(x, wu_ref[...])
    grad_hidden = dot(g_ref[...], wd_ref[...])
    act, slope = gelu_parts(gate)
    hidden = (act * up).astype(jnp.bfloat16)
    dgate = (slope * (grad_hidden * up)).astype(jnp.bfloat16)
    dup = (grad_hidden * act).astype(jnp.bfloat16)
    h_ref[...] = hidden
    dg_ref[...] = dgate
    du_ref[...] = dup
    b_add = dot_nt(hidden, wd_ref[...])
    d_add = dot_nt(dgate, wg_ref[...]) + dot_nt(dup, wu_ref[...])

    @pl.when(u == 0)
    def _():
        branch[...] = b_add
        dx[...] = d_add

    @pl.when(u > 0)
    def _():
        branch[...] += b_add
        dx[...] += d_add

    @pl.when(u == pl.num_programs(0) - 1)
    def _():
        branch_ref[...] = branch[...]
        dx_ref[...] = dx[...].astype(jnp.bfloat16)


def ffn_rows(x, g, weights, tile=256):
    rows, d = x.shape
    units = weights.shape[1] // 3
    n = units // tile
    full = pl.BlockSpec((rows, d), lambda u: (0, 0))
    cols = pl.BlockSpec((rows, tile), lambda u: (0, u))
    wide = jax.ShapeDtypeStruct((rows, units), jnp.bfloat16)
    narrow = jax.ShapeDtypeStruct((rows, d), jnp.bfloat16)
    return pl.pallas_call(
        functools.partial(ffn_kernel, tile),
        out_shape=(wide, wide, wide, jax.ShapeDtypeStruct((rows, d), jnp.float32), narrow),
        grid=(n,),
        in_specs=[
            full,
            full,
            pl.BlockSpec((d, tile), lambda u: (0, u)),
            pl.BlockSpec((d, tile), lambda u: (0, u + n)),
            pl.BlockSpec((d, tile), lambda u: (0, u + 2 * n)),
        ],
        out_specs=(cols, cols, cols, full, full),
        scratch_shapes=[pltpu.VMEM((rows, d), jnp.float32), pltpu.VMEM((rows, d), jnp.float32)],
        cost_estimate=pl.CostEstimate(
            flops=12 * rows * d * units,
            bytes_accessed=2 * (4 * rows * d + 3 * rows * units + 3 * d * units),
            transcendentals=rows * units,
        ),
        name="ffn_rows",
    )(x, g, weights, weights, weights)


def wgrad_kernel(parts, n, *refs):
    xs, gs, gates, ups, hiddens = [refs[parts * m : parts * (m + 1)] for m in range(5)]
    out, left_t = refs[-2:]
    i = pl.program_id(0)
    rows = xs[0].shape[0]

    def turn_all(lefts):
        for c in range(parts):
            def turn(s, carry, c=c):
                src = pl.ds(pl.multiple_of(s * SUB, SUB), SUB)
                at = pl.ds(pl.multiple_of(c * rows + s * SUB, SUB), SUB)
                left_t[:, at] = turned(lefts[c][src, :]).astype(jnp.bfloat16)
                return carry
            lax.fori_loop(0, rows // SUB, turn, 0)

    def product(rights):
        total = dot(left_t[:, :rows], rights[0][...])
        for c in range(1, parts):
            total += dot(left_t[:, c * rows : (c + 1) * rows], rights[c][...])
        out[...] = total.astype(jnp.bfloat16)

    @pl.when(i == 0)
    def _():
        turn_all(xs)

    @pl.when(i == 2 * n)
    def _():
        turn_all(gs)

    @pl.when(i < n)
    def _():
        product(gates)

    @pl.when((i >= n) & (i < 2 * n))
    def _():
        product(ups)

    @pl.when(i >= 2 * n)
    def _():
        product(hiddens)


def wgrad(xs, gs, gates, ups, hiddens, tile=256):
    parts = len(xs)
    rows, d = xs[0].shape
    units = gates[0].shape[1]
    n = units // tile

    def tiles(m):
        return [pl.BlockSpec((rows, tile), lambda i: (0, jnp.clip(i - m * n, 0, n - 1)))] * parts

    return pl.pallas_call(
        functools.partial(wgrad_kernel, parts, n),
        out_shape=jax.ShapeDtypeStruct((d, 3 * units), jnp.bfloat16),
        grid=(3 * n,),
        in_specs=[pl.BlockSpec((rows, d), lambda i: (0, 0))] * (2 * parts) + tiles(0) + tiles(1) + tiles(2),
        out_specs=pl.BlockSpec((d, tile), lambda i: (0, i)),
        scratch_shapes=[pltpu.VMEM((d, parts * rows), jnp.bfloat16)],
        cost_estimate=pl.CostEstimate(
            flops=6 * parts * rows * d * units,
            bytes_accessed=2 * parts * rows * (2 * d + 3 * units) + 6 * d * units,
            transcendentals=0,
        ),
        name="wgrad",
    )(*xs, *gs, *gates, *ups, *hiddens)


def rms_norm(features, norm_gain):
    return features * lax.rsqrt(jnp.mean(features * features, axis=-1, keepdims=True) + EPS) * norm_gain


def norm_back(v, gain, e):
    rate = lax.rsqrt(jnp.mean(v * v, axis=-1, keepdims=True) + EPS)
    scaled = gain * e
    dot_mean = jnp.mean(scaled * v, axis=-1, keepdims=True)
    return rate * scaled - v * (rate * rate * rate * dot_mean), jnp.sum(e * v * rate, axis=0, keepdims=True)


def middle_kernel(parts, share, came, got, middle, top, gain, *refs):
    weights = refs[:parts]
    grad_ref, low_ref = refs[parts : parts + 2]
    heads = refs[parts + 2 : 2 * parts + 2]
    gain_ref = refs[-1]
    f32 = jnp.float32
    e = share[...].astype(f32) + came[...].astype(f32) + got[...].astype(f32)
    grad, part = norm_back(middle[...], gain[...], e)
    grad = top[...] + grad
    grad_ref[...] = grad
    low = grad.astype(jnp.bfloat16)
    low_ref[...] = low
    for c in range(parts):
        heads[c][...] = dot(low, weights[c][...]).astype(jnp.bfloat16)

    @pl.when(pl.program_id(0) == 0)
    def _():
        gain_ref[...] = part

    @pl.when(pl.program_id(0) > 0)
    def _():
        gain_ref[...] += part


def middle_back(share, came, got, middle, top, gain, weights, block=160):
    rows, d = middle.shape
    feats = weights[0].shape[1]
    parts = len(weights)
    row = pl.BlockSpec((block, d), lambda i: (i, 0))
    one = pl.BlockSpec((1, d), lambda i: (0, 0))
    outs = pl.pallas_call(
        functools.partial(middle_kernel, parts),
        out_shape=(
            jax.ShapeDtypeStruct((rows, d), jnp.float32),
            jax.ShapeDtypeStruct((rows, d), jnp.bfloat16),
            *[jax.ShapeDtypeStruct((rows, feats), jnp.bfloat16)] * parts,
            jax.ShapeDtypeStruct((1, d), jnp.float32),
        ),
        grid=(rows // block,),
        in_specs=[row] * 5 + [one] + [pl.BlockSpec((d, feats), lambda i: (0, 0))] * parts,
        out_specs=(row, row, *[pl.BlockSpec((block, feats), lambda i: (i, 0))] * parts, one),
        cost_estimate=pl.CostEstimate(
            flops=2 * rows * d * feats * parts, bytes_accessed=22 * rows * d, transcendentals=rows
        ),
        name="middle_back",
    )(share, came, got, middle, top, gain[None], *weights)
    return outs[0], outs[1], list(outs[2 : 2 + parts]), outs[-1]


def input_kernel(share, came, got_a, got_b, inputs, cot, grad_middle, early, gain, mix, correct, out, sums):
    i = pl.program_id(0)
    f32 = jnp.float32
    d = gain.shape[1]
    got = jnp.where(i < pl.num_programs(0) // 2, got_a[...].astype(f32), got_b[...].astype(f32))
    e = share[...].astype(f32) + came[...].astype(f32) + got
    one, two = inputs[:, :d].astype(f32), inputs[:, d:].astype(f32)
    cot_one, cot_two = cot[:, :d].astype(f32), cot[:, d:].astype(f32)
    grad, part = norm_back(mix[0, 0] * one + mix[0, 1] * two, gain[...], e)
    main = cot_one + grad_middle[...] + grad - (correct[0] * cot_one + correct[1] * cot_two)
    out[:, :d] = mix[0, 0] * main + mix[1, 0] * cot_two
    out[:, d:] = mix[0, 1] * main + mix[1, 1] * cot_two

    @pl.when(i == 0)
    def _():
        sums[...] = early[...]

    sums[0:1] += part
    for r, value in enumerate((main * one, main * two, cot_two * one, cot_two * two)):
        sums[r + 1 : r + 2] += jnp.sum(value, axis=0, keepdims=True)


def input_back(share, came, got, inputs, cot, grad_middle, early, gain, mix, correct, block=160):
    rows, d = grad_middle.shape
    half = rows // block // 2
    row = pl.BlockSpec((block, d), lambda i: (i, 0))
    wide = pl.BlockSpec((block, 2 * d), lambda i: (i, 0))
    sums = pl.BlockSpec((8, d), lambda i: (0, 0))
    small = pl.BlockSpec(memory_space=pltpu.SMEM)
    return pl.pallas_call(
        input_kernel,
        out_shape=(jax.ShapeDtypeStruct((rows, 2 * d), jnp.float32), jax.ShapeDtypeStruct((8, d), jnp.float32)),
        grid=(2 * half,),
        in_specs=[
            row,
            row,
            pl.BlockSpec((block, d), lambda i: (jnp.minimum(i, half - 1), 0)),
            pl.BlockSpec((block, d), lambda i: (jnp.maximum(i - half, 0), 0)),
            wide,
            wide,
            row,
            sums,
            pl.BlockSpec((1, d), lambda i: (0, 0)),
            small,
            small,
        ],
        out_specs=(wide, sums),
        cost_estimate=pl.CostEstimate(flops=60 * rows * d, bytes_accessed=30 * rows * d, transcendentals=rows),
        name="input_back",
    )(share, came, *got, inputs, cot, grad_middle, early, gain[None], mix, correct)


def swap(array, bit):
    count = lax.axis_size("tensor")
    return lax.ppermute(array, "tensor", [(i, i ^ bit) for i in range(count)])


def after(value, *others):
    return lax.optimization_barrier((value, *others))[0]


def flipped(index, bits):
    bit = 1
    while bit <= bits:
        if bits & bit:
            index = index + bit - 2 * bit * lax.rem(lax.div(index, bit), 2)
        bit *= 2
    return index


def start_kernel(
    count, chunks, x, qkv, wo, sib, far, diag, qkv_all, wo_all,
    local_sem, sib_sem, far_send, far_recv, diag_send, diag_recv, qkv_dp, wo_dp,
):
    t = lax.axis_index("tensor")
    g = lax.axis_index("dp")
    order = []
    bit = 2
    while bit < count:
        order.append(bit)
        bit *= 2
    order.append(1)

    def last(e):
        return max(k for k, b in enumerate(order) if e & b)

    barrier = pltpu.get_barrier_semaphore()
    for c in (1, 2):
        pl.semaphore_signal(barrier, inc=1, device_id={"tensor": flipped(t, c)}, device_id_type=MESH)
    for b in order:
        pl.semaphore_signal(barrier, inc=1, device_id={"dp": flipped(g, b)}, device_id_type=MESH)
    pl.semaphore_wait(barrier, 2 + len(order))

    size = x.shape[0] // chunks

    def far_copy(k):
        rows = pl.ds(k * size, size)
        return pltpu.make_async_remote_copy(
            x.at[rows], far.at[rows], far_send.at[k], far_recv.at[k], {"tensor": flipped(t, 2)}, MESH
        )

    def diag_copy(k):
        rows = pl.ds(k * size, size)
        return pltpu.make_async_remote_copy(
            far.at[rows], diag.at[rows], diag_send.at[k], diag_recv.at[k], {"tensor": flipped(t, 1)}, MESH
        )

    def dp_copy(which, e):
        own, whole, sems = ((qkv, qkv_all, qkv_dp), (wo, wo_all, wo_dp))[which]
        b = order[last(e)]
        block = flipped(g, e ^ b)
        return pltpu.make_async_remote_copy(
            own if e == b else whole.at[block],
            whole.at[block],
            sems.at[0, e - 1],
            sems.at[1, e - 1],
            {"dp": flipped(g, b)},
            MESH,
        )

    def dp_arrival(which, e):
        whole, sems = ((qkv_all, qkv_dp), (wo_all, wo_dp))[which]
        dst = whole.at[flipped(g, e)]
        return pltpu.make_async_remote_copy(
            dst, dst, sems.at[0, e - 1], sems.at[1, e - 1], {"dp": flipped(g, order[last(e)])}, MESH
        )

    sends = []

    def go(copy):
        copy.start()
        sends.append(copy)

    for b in order:
        go(dp_copy(0, b))
    fars = [far_copy(k) for k in range(chunks)]
    for copy in fars:
        go(copy)
    near = pltpu.make_async_remote_copy(
        x, sib, sib_sem.at[0], sib_sem.at[1], {"tensor": flipped(t, 1)}, MESH
    )
    go(near)
    kept = [
        pltpu.make_async_copy(qkv, qkv_all.at[g], local_sem.at[0]),
        pltpu.make_async_copy(wo, wo_all.at[g], local_sem.at[1]),
    ]
    for copy in kept:
        copy.start()
    for b in order:
        go(dp_copy(1, b))
    diags = []

    def pass_on(k):
        fars[k].wait_recv()
        diags.append(diag_copy(k))
        go(diags[-1])

    done = 0
    for e in sorted(range(1, count), key=lambda e: (last(e), e)):
        for which in (0, 1):
            dp_arrival(which, e).wait_recv()
            for b in order[last(e) + 1 :]:
                go(dp_copy(which, e ^ b))
        if done < chunks and e & 1 == 0:
            pass_on(done)
            done += 1
    while done < chunks:
        pass_on(done)
        done += 1
    for copy in diags:
        copy.wait_recv()
    near.wait_recv()
    for copy in sends:
        copy.wait_send()
    for copy in kept:
        copy.wait()


def start(x, qkv, wo, chunks=4):
    count = lax.axis_size("dp")
    rows = jax.ShapeDtypeStruct(x.shape, x.dtype)
    dma = pltpu.SemaphoreType.DMA
    sib, far, diag, qkv_all, wo_all = pl.pallas_call(
        functools.partial(start_kernel, count, chunks),
        out_shape=(
            rows,
            rows,
            rows,
            jax.ShapeDtypeStruct((count, *qkv.shape), qkv.dtype),
            jax.ShapeDtypeStruct((count, *wo.shape), wo.dtype),
        ),
        in_specs=[pl.BlockSpec(memory_space=pl.ANY)] * 3,
        out_specs=(pl.BlockSpec(memory_space=pl.ANY),) * 5,
        scratch_shapes=[
            dma((2,)),
            dma((2,)),
            dma((chunks,)),
            dma((chunks,)),
            dma((chunks,)),
            dma((chunks,)),
            dma((2, count - 1)),
            dma((2, count - 1)),
        ],
        compiler_params=pltpu.CompilerParams(collective_id=0, has_side_effects=True),
        cost_estimate=pl.CostEstimate(flops=0, bytes_accessed=100_000_000, transcendentals=0),
        name="start",
    )(x, qkv, wo)
    whole = count * qkv.shape[0]
    return [x, sib, far, diag], qkv_all.reshape(whole, -1), wo_all.reshape(whole, -1)


def spread(rows):
    far = swap(rows, 2)
    return [rows, swap(rows, 1), far, swap(far, 1)]


def exchange(blocks):
    return [blocks[0]] + [swap(blocks[c], c) for c in range(1, len(blocks))]


def summed(shares, before=None, beside=None):
    f32 = jnp.float32
    far = (shares[2].astype(f32) + swap(shares[3], 1).astype(f32)).astype(jnp.bfloat16)
    if before is not None:
        far = after(far, before)
    got = swap(far, 2)
    near = shares[0].astype(f32) + swap(shares[1], 1).astype(f32)
    if beside is not None:
        got, beside = lax.optimization_barrier((got, beside(far)))
    return near + got.astype(f32), beside


def end_kernel(count, mine, total, near, mid, far, near_sem, far_sem):
    t = lax.axis_index("tensor")
    g = lax.axis_index("dp")
    barrier = pltpu.get_barrier_semaphore()
    for c in (1, 2, 3):
        pl.semaphore_signal(barrier, inc=1, device_id={"tensor": flipped(t, c)}, device_id_type=MESH)
    for e in range(1, count):
        pl.semaphore_signal(barrier, inc=1, device_id={"dp": flipped(g, e)}, device_id_type=MESH)
    pl.semaphore_wait(barrier, 2 + count)

    nears = [
        pltpu.make_async_remote_copy(
            mine, near.at[c - 1], near_sem.at[0, c - 1], near_sem.at[1, c - 1], {"tensor": flipped(t, c)}, MESH
        )
        for c in (1, 2, 3)
    ]
    fars = [
        pltpu.make_async_remote_copy(
            mid, far.at[e - 1], far_sem.at[0, e - 1], far_sem.at[1, e - 1], {"dp": flipped(g, e)}, MESH
        )
        for e in range(1, count)
    ]
    for copy in nears:
        copy.start()
    for copy in nears:
        copy.wait_recv()
    mid[...] = (mine[...] + near[0]) + (near[1] + near[2])
    for copy in fars:
        copy.start()
    for copy in fars:
        copy.wait_recv()
    level = [mid[...]] + [far[e] for e in range(count - 1)]
    while len(level) > 1:
        level = [level[k] + level[k + 1] for k in range(0, len(level), 2)]
    total[...] = level[0]
    for copy in nears + fars:
        copy.wait_send()


def end(mine):
    count = lax.axis_size("dp")
    dma = pltpu.SemaphoreType.DMA
    vmem = pl.BlockSpec(memory_space=pltpu.VMEM)
    return pl.pallas_call(
        functools.partial(end_kernel, count),
        out_shape=jax.ShapeDtypeStruct(mine.shape, jnp.float32),
        in_specs=[vmem],
        out_specs=vmem,
        scratch_shapes=[
            pltpu.VMEM((3, *mine.shape), jnp.float32),
            pltpu.VMEM(mine.shape, jnp.float32),
            pltpu.VMEM((count - 1, *mine.shape), jnp.float32),
            dma((2, 3)),
            dma((2, count - 1)),
        ],
        compiler_params=pltpu.CompilerParams(collective_id=1, has_side_effects=True),
        cost_estimate=pl.CostEstimate(flops=0, bytes_accessed=30_000_000, transcendentals=0),
        name="end",
    )(mine)


def local(
    block_input, seq_lengths, w_qkv, w_out, w_gate_up, w_down, gain_attn, gain_ffn, mix_matrix, correct_gain, cotangent
):
    f32, bf16 = jnp.float32, jnp.bfloat16
    width = gain_attn.shape[0]
    me = lax.axis_index("tensor").astype(jnp.int32)[None]
    shard = w_qkv.shape[0]
    feats = w_out.shape[1]
    inputs = block_input.astype(f32)
    stream_one = inputs[:, :width]
    stream_two = inputs[:, width:]
    predicted_main = mix_matrix[0, 0] * stream_one + mix_matrix[0, 1] * stream_two
    predicted_side = mix_matrix[1, 0] * stream_one + mix_matrix[1, 1] * stream_two
    units = w_down.shape[1]

    normed_attn, qkv_all, out_mine = start(
        rms_norm(predicted_main, gain_attn).astype(bf16),
        w_qkv.reshape(shard, 3 * feats).astype(bf16),
        w_out.astype(bf16),
    )
    ffn_mine = jnp.concatenate([w_gate_up.reshape(shard, -1), w_down], axis=1).astype(bf16)
    ffn_all = lax.all_gather(after(ffn_mine, normed_attn[1]), "dp", axis=0, tiled=True)
    proj = [dot(x, qkv_all).astype(bf16) for x in normed_attn]
    attended, heads_turned, log_total = attn_fwd(seq_lengths, me, proj)

    incoming = cotangent.astype(f32)
    cot_one = incoming[:, :width]
    cot_two = incoming[:, width:]
    grad_top = correct_gain[0] * cot_one + correct_gain[1] * cot_two
    grad_ffn = spread(after(grad_top.astype(bf16), normed_attn[1]))

    out_parts = [out_mine] + [swap(out_mine, c) for c in (1, 2, 3)]
    attended = after(attended, grad_ffn[2], out_parts[2], out_parts[3])
    head_parts = exchange([attended[c] for c in range(len(proj))])
    attn_branch = sum(dot_nt(a, w) for a, w in zip(head_parts, out_parts))
    middle = predicted_main + attn_branch

    normed_mine = rms_norm(middle, gain_ffn).astype(bf16)
    normed_ffn = [normed_mine, swap(normed_mine, 1), swap(normed_mine, 2)]
    pieces = [ffn_rows(x, g, ffn_all) for x, g in zip(normed_ffn, grad_ffn[:2])]
    normed_ffn[2] = after(normed_ffn[2], pieces[0][0], pieces[1][0])
    normed_ffn.append(swap(normed_ffn[2], 1))
    pieces += [ffn_rows(x, g, ffn_all) for x, g in zip(normed_ffn[2:], grad_ffn[2:])]
    hidden, dgate, dup, branch, dnormed = zip(*pieces)
    far = (dnormed[2].astype(f32) + swap(dnormed[3], 1).astype(f32)).astype(bf16)
    got = swap(far, 2)
    came = swap(dnormed[1], 1)
    weight_ffn = wgrad([after(normed_ffn[0], far)] + normed_ffn[1:], grad_ffn, dgate, dup, hidden)
    got, came, weight_ffn = lax.optimization_barrier((got, came, weight_ffn))
    weight_ffn = lax.psum_scatter(weight_ffn, "dp", scatter_dimension=0, tiled=True)
    grad_middle, grad_attn, grad_heads, grad_gain_ffn = middle_back(
        dnormed[0], came, got, middle, grad_top, gain_ffn, out_parts
    )
    grad_heads = exchange(grad_heads)
    grad_proj = attn_bwd(seq_lengths, me, proj, grad_heads, heads_turned, log_total)
    *late, later_attn = lax.optimization_barrier((*head_parts, grad_heads[2], grad_heads[3], grad_attn))
    out_shares = exchange([dot_tn(later_attn, a).astype(bf16) for a in late[:4]])
    weight_out = sum(s.astype(f32) for s in out_shares)
    ffn_branch, (grad_proj, weight_out) = summed(branch, before=late[4], beside=lambda far: (grad_proj, weight_out))
    grad_proj = [grad_proj[c] for c in range(len(proj))]

    correction = (middle + ffn_branch) - predicted_main
    block_output = jnp.concatenate(
        [predicted_main + correct_gain[0] * correction, predicted_side + correct_gain[1] * correction], axis=1
    ).astype(bf16)
    early = jnp.concatenate(
        [
            jnp.zeros((5, width), f32),
            grad_gain_ffn,
            jnp.sum(cot_one * correction, axis=0, keepdims=True),
            jnp.sum(cot_two * correction, axis=0, keepdims=True),
        ],
        axis=0,
    )

    far = [dot_nt(g, qkv_all).astype(bf16) for g in grad_proj[2:]]
    far = (far[0].astype(f32) + swap(far[1], 1).astype(f32)).astype(bf16)
    half = far.shape[0] // 2
    got = [swap(far[:half], 2), swap(far[half:], 2)]
    *late, far = lax.optimization_barrier((*grad_proj, *normed_attn, weight_out, far))
    weight_qkv = sum(dot_tn(x, g) for x, g in zip(late[4:8], late[:4]))
    last = jnp.concatenate([weight_qkv, late[8]], axis=1).astype(bf16)
    last, got[0] = lax.optimization_barrier((last.reshape(lax.axis_size("dp"), shard, -1), got[0]))
    last = lax.all_to_all(last, "dp", split_axis=0, concat_axis=0, tiled=True)
    got[0], weight_ffn, *late = lax.optimization_barrier((got[0], weight_ffn, *late[:2]))
    near = [dot_nt(g, qkv_all).astype(bf16) for g in late]
    came = swap(near[1], 1)
    got[1], came, early, block_output = lax.optimization_barrier((got[1], came, early, block_output))
    grad_input, small = input_back(
        near[0], came, got, block_input, cotangent, grad_middle, early, gain_attn, mix_matrix, correct_gain
    )
    weight_ffn = weight_ffn.astype(f32)
    sum_gate_up = weight_ffn[:, : 2 * units].reshape(shard, 2, units)
    sum_down = weight_ffn[:, 2 * units :]
    small, last = lax.optimization_barrier((end(small), last))
    last = last.astype(f32).sum(axis=0)
    sum_qkv = last[:, : 3 * feats].reshape(shard, 3, feats)
    sum_out = last[:, 3 * feats :]
    return (
        block_output,
        grad_input,
        sum_qkv,
        sum_out,
        sum_gate_up,
        sum_down,
        small[0],
        small[5],
        small[1:5].sum(axis=1).reshape(2, 2),
        small[6:].sum(axis=1),
    )


def solution(mesh):
    placed = (
        P(("dp", "tensor"), None),
        P("dp", None),
        P("dp", None, "tensor"),
        P("dp", "tensor"),
        P("dp", None, "tensor"),
        P("dp", "tensor"),
        P(),
        P(),
        P(),
        P(),
        P(("dp", "tensor"), None),
    )
    return jax.shard_map(
        local,
        mesh=mesh,
        in_specs=placed,
        out_specs=(
            P(("dp", "tensor"), None),
            P(("dp", "tensor"), None),
            P("dp", None, "tensor"),
            P("dp", "tensor"),
            P("dp", None, "tensor"),
            P("dp", "tensor"),
            P(),
            P(),
            P(),
            P(),
        ),
        check_vma=False,
    )
```
